32 devices in a mesh: groups: 2 (over y), tiles: 4 (over z), views: 2 (over x), gz: 2 (over core).
Axes of the slice: x: 2, y: 2, z: 4, core: 2. Of those that a mesh axis runs over, the one named last changes fastest.
Arguments:
- view_data: bfloat16 [4, 4, 16, 128, 128], P(('groups', 'views'), 'tiles', 'gz'), parts along dimension 0, may hold values from 0.19921875 to 2
- estimate: float32 [32, 512, 128], P(('groups', 'gz'), 'tiles'), parts along dimension 0, may hold values from 0.5 to 1.5
- psf_taps: float32 [2, 2, 2, 9], P('views'), may hold values from 0.02 to 0.3
- offsets: int32 [2, 8], P('views'), may hold values from 0 to 3, as said below
Outputs:
- updated_estimate: float32 [32, 512, 128], P(('groups', 'gz'), 'tiles'), parts along dimension 0
The draws below stay inside these ranges and needn't reach their ends.
There are 2 independent parts, one for each index of `groups`. The reference program is written for one: setup_inputs(seed, part) draws one part's arguments, and reference() takes and returns one part's arrays. A program takes and returns all parts, laid end to end along the dimension named above; an argument that names none is the same for every part. Nothing has to cross between parts.
Inputs may be any that keep to these rules, and one draw needn't show every extreme that they name: `offsets`: in each view's row no value appears more than 4 times, and one value appears exactly 4 times.
All inputs are finite; a program needn't handle non-finite values.
Results may differ from the reference program's by a relative error of at most 0.0022.
The reference program's roundings to bfloat16 on the way count: a program that leaves them out, or rounds other values in their place, can miss the bound.
Values may be sent and summed in bfloat16 or wider, within the bound.
No kernel may reach another device: no remote copies, remote signals or barrier semaphores. Data moves between devices by JAX's collectives and lax.ppermute only.
A program may use at most 64 MiB of HBM per device.

```python
import math
import jax
import jax.numpy as jnp
from jax import lax

TX = 128
TY = 128
KW = 9
ITERS = 2
OWNERS = 4
VIEWS = 2
TZ = 16
SUBS = 8
RB = 16
FY = 512


def draw_offsets(key, part):
    cycle_values = jnp.arange(SUBS, dtype=jnp.int32) % OWNERS

    def one_row(row_key):
        key_first, key_second, key_third = jax.random.split(row_key, 3)
        emptied = 1 + jax.random.randint(key_first, (), 0, OWNERS - 2, dtype=jnp.int32)
        doubled = (emptied + 1 + jax.random.randint(key_second, (), 0, OWNERS - 1, dtype=jnp.int32)) % OWNERS
        merged = jnp.where(cycle_values == emptied, doubled, cycle_values)
        return jax.random.permutation(key_third, merged)
    return jax.vmap(one_row)(jax.random.split(key, VIEWS)).astype(jnp.int32)


def steps_of(rng, extent, cuts, least, top_value):
    level, own = 1.0, jax.random.fold_in(rng, 6)
    for dim, blocks in cuts:
        heights = jnp.exp(jax.random.uniform(jax.random.fold_in(own, dim), (blocks,), jnp.float32, least / len(cuts), top_value / len(cuts)))
        level = level * jnp.repeat(heights, extent[dim] // blocks).reshape([-1 if axis == dim else 1 for axis in range(len(extent))])
    return level


def setup_inputs(seed: int = 0, part: int = 0) -> dict:
    arg_keys = jax.random.split(jax.random.key(seed), 5)
    part_keys = jax.random.split(jax.random.fold_in(arg_keys[4], part), 5)
    view_data = jnp.clip(0.19921875 + 1.8007812 * jax.random.uniform(part_keys[0], (VIEWS, OWNERS, TZ, TY, TX), jnp.float32) ** steps_of(part_keys[0], (VIEWS, OWNERS, TZ, TY, TX), ((0, 2), (1, 4), (2, 2)), -0.2, 0.2), 0.19921875, 2.0).astype(jnp.bfloat16)
    estimate = jnp.clip(0.5 + 1.0 * jax.random.uniform(part_keys[1], (TZ, FY, TX), jnp.float32) ** steps_of(part_keys[1], (TZ, FY, TX), ((0, 2), (1, 4)), -0.2, 0.2), 0.5, 1.5)
    psf_taps = jnp.clip(jnp.exp(math.log(0.3) - 2.7080503 * jax.random.uniform(arg_keys[2], (VIEWS, 2, 2, KW), jnp.float32) ** steps_of(arg_keys[2], (VIEWS, 2, 2, KW), ((0, 2),), -0.2, 0.2)), 0.02, 0.3)
    offsets = draw_offsets(jax.random.fold_in(arg_keys[4], 71), part)
    return dict(view_data=view_data, estimate=estimate, psf_taps=psf_taps, offsets=offsets)


TV_WEIGHT = 0.1
SMOOTH_SQUARE = 0.0025

def toeplitz_matrix(profile, length):
    half_width = (profile.shape[0] - 1) // 2
    position = jnp.arange(length, dtype=jnp.int32)
    offset = position[None, :] - position[:, None] + half_width
    tap_index = jnp.arange(profile.shape[0], dtype=jnp.int32)
    picked = (offset[:, :, None] == tap_index[None, None, :]).astype(jnp.float32)
    return lax.optimization_barrier(jnp.sum(picked * profile[None, None, :], axis=2)).astype(jnp.bfloat16)

def curvature(padded):
    anchor = padded[:-1, :-1, :-1]
    grad_z = padded[1:, :-1, :-1] - anchor
    grad_y = padded[:-1, 1:, :-1] - anchor
    grad_x = padded[:-1, :-1, 1:] - anchor
    magnitude = jnp.sqrt(grad_z * grad_z + grad_y * grad_y + grad_x * grad_x + SMOOTH_SQUARE)
    unit_z = grad_z / magnitude
    unit_y = grad_y / magnitude
    unit_x = grad_x / magnitude
    return unit_z[1:, 1:, 1:] - unit_z[:-1, 1:, 1:] + (unit_y[1:, 1:, 1:] - unit_y[1:, :-1, 1:]) + (unit_x[1:, 1:, 1:] - unit_x[1:, 1:, :-1])

def reference_correction(view_tile, observed, kernel_y, kernel_x):
    blurred = jnp.zeros(view_tile.shape, jnp.float32)
    for term_index in range(2):
        half_blur = jnp.einsum('yk,...kx->...yx', kernel_y[term_index].astype(jnp.float32), view_tile.astype(jnp.float32)).astype(jnp.bfloat16)
        blurred = blurred + jnp.einsum('...yk,xk->...yx', half_blur.astype(jnp.float32), kernel_x[term_index].astype(jnp.float32))
    quotient = (observed.astype(jnp.float32) / blurred).astype(jnp.bfloat16)
    log_sum = jnp.zeros(view_tile.shape, jnp.float32)
    for term_index in range(2):
        half_back = jnp.einsum('ky,...kx->...yx', kernel_y[term_index].astype(jnp.float32), quotient.astype(jnp.float32)).astype(jnp.bfloat16)
        log_sum = log_sum + jnp.einsum('...yk,kx->...yx', half_back.astype(jnp.float32), kernel_x[term_index].astype(jnp.float32))
    return log_sum.astype(jnp.bfloat16)

def reference(view_data, estimate, psf_taps, offsets):
    current = estimate
    position = jnp.arange(SUBS, dtype=jnp.int32)
    tile_index = jnp.arange(OWNERS, dtype=jnp.int32)
    for iteration in range(ITERS):
        joined_blocks = current.astype(jnp.bfloat16).reshape(TZ, OWNERS, SUBS, RB, TX)

        def one_view(carried, inputs):
            observed, profiles, view_shift = inputs
            kernel_y = jnp.stack([toeplitz_matrix(profiles[term_index, 0], TY) for term_index in range(2)])
            kernel_x = jnp.stack([toeplitz_matrix(profiles[term_index, 1], TX) for term_index in range(2)])
            owner_tile = (tile_index[:, None] + view_shift[None, :]) % OWNERS
            picked = joined_blocks[:, owner_tile, position[None, :]]
            view_tile = jnp.transpose(picked, (1, 0, 2, 3, 4)).reshape(OWNERS, TZ, TY, TX)
            correction = reference_correction(view_tile, observed, kernel_y, kernel_x)
            correction = correction.reshape(OWNERS, TZ, SUBS, RB, TX)
            source_tile = (tile_index[:, None] - view_shift[None, :]) % OWNERS
            placed = correction[source_tile, :, position[None, :]]
            placed = jnp.transpose(placed, (2, 0, 1, 3, 4)).reshape(TZ, FY, TX)
            return (carried + jnp.log(placed.astype(jnp.float32)), None)
        log_sum, unused = lax.scan(one_view, jnp.zeros((TZ, FY, TX), jnp.float32), (view_data, psf_taps, offsets))
        padded = jnp.pad(current, 1)
        damping = 1.0 - TV_WEIGHT * curvature(padded)
        current = current * jnp.exp(log_sum / VIEWS) / damping
    return current
```

```python
import functools

import jax
import jax.numpy as jnp
from jax import lax
from jax.experimental import pallas as pl
from jax.experimental.pallas import tpu as pltpu
from jax.sharding import PartitionSpec as P

ITERS = 2
CAP = 4


TV_WEIGHT = 0.1
SMOOTH_SQUARE = 0.0025


def with_halo(cells, sides, width):
    for axis, dim in sides:
        count = lax.axis_size(axis)
        ends = count - 1
        head = lax.slice_in_dim(cells, 0, width, axis=dim)
        tail = lax.slice_in_dim(cells, cells.shape[dim] - width, cells.shape[dim], axis=dim)
        cells = jnp.concatenate(
            [
                lax.ppermute(tail, axis, [(i, (i + 1) % count) for i in range(ends)]),
                cells,
                lax.ppermute(head, axis, [((i + 1) % count, i) for i in range(ends)]),
            ],
            axis=dim,
        )
    return cells


def toeplitz_matrix(profile, length):
    half_width = (profile.shape[0] - 1) // 2
    position = jnp.arange(length, dtype=jnp.int32)
    offset = position[None, :] - position[:, None] + half_width
    tap_index = jnp.arange(profile.shape[0], dtype=jnp.int32)
    picked = (offset[:, :, None] == tap_index[None, None, :]).astype(jnp.float32)
    return jnp.sum(picked * profile[None, None, :], axis=2).astype(jnp.bfloat16)


def curvature(padded):
    anchor = padded[:-1, :-1, :-1]
    grad_z = padded[1:, :-1, :-1] - anchor
    grad_y = padded[:-1, 1:, :-1] - anchor
    grad_x = padded[:-1, :-1, 1:] - anchor
    magnitude = jnp.sqrt(grad_z * grad_z + grad_y * grad_y + grad_x * grad_x + SMOOTH_SQUARE)
    unit_z = grad_z / magnitude
    unit_y = grad_y / magnitude
    unit_x = grad_x / magnitude
    return (
        unit_z[1:, 1:, 1:]
        - unit_z[:-1, 1:, 1:]
        + (unit_y[1:, 1:, 1:] - unit_y[1:, :-1, 1:])
        + (unit_x[1:, 1:, 1:] - unit_x[1:, 1:, :-1])
    )


def view_correction(view_tile, observed, kernel_y, kernel_x):
    blurred = jnp.zeros(view_tile.shape, jnp.float32)
    for term_index in range(2):
        half_blur = jnp.einsum(
            "yk,zkx->zyx", kernel_y[term_index], view_tile, preferred_element_type=jnp.float32
        ).astype(jnp.bfloat16)
        blurred = blurred + jnp.einsum(
            "zyk,xk->zyx", half_blur, kernel_x[term_index], preferred_element_type=jnp.float32
        )
    quotient = (observed.astype(jnp.float32) / blurred).astype(jnp.bfloat16)
    log_sum = jnp.zeros(view_tile.shape, jnp.float32)
    for term_index in range(2):
        half_back = jnp.einsum(
            "ky,zkx->zyx", kernel_y[term_index], quotient, preferred_element_type=jnp.float32
        ).astype(jnp.bfloat16)
        log_sum = log_sum + jnp.einsum(
            "zyk,kx->zyx", half_back, kernel_x[term_index], preferred_element_type=jnp.float32
        )
    return log_sum.astype(jnp.bfloat16)


def shards(view_data, estimate, psf_taps, offsets):
    owners = lax.axis_size("tiles")
    view_count = lax.axis_size("views")
    observed = view_data[0, 0]
    planes, height, columns = estimate.shape
    view_shift = offsets[0]
    blocks = view_shift.shape[0]
    block_rows = height // blocks
    slot_count = owners * CAP
    kernel_y = jnp.stack(
        [toeplitz_matrix(psf_taps[0, term_index, 0], height) for term_index in range(2)]
    )
    kernel_x = jnp.stack(
        [toeplitz_matrix(psf_taps[0, term_index, 1], columns) for term_index in range(2)]
    )
    position = jnp.arange(blocks, dtype=jnp.int32)
    same_owner = view_shift[:, None] == view_shift[None, :]
    before = position[None, :] < position[:, None]
    slot_rank = jnp.sum((same_owner & before).astype(jnp.int32), axis=1)
    member = lax.axis_index("tiles")
    target = (member + view_shift) % owners
    source_tile = (member - view_shift) % owners
    slot_index = jnp.arange(slot_count, dtype=jnp.int32)
    to_owner = ((target * CAP + slot_rank)[:, None] == slot_index[None, :]).astype(jnp.bfloat16)
    from_tile = ((source_tile * CAP + slot_rank)[:, None] == slot_index[None, :]).astype(
        jnp.bfloat16
    )
    current = estimate
    for iteration in range(ITERS):
        padded = with_halo(current, (("tiles", 1), ("gz", 0)), 1)
        padded = jnp.pad(padded, ((0, 0), (0, 0), (1, 1)))
        owned_blocks = current.astype(jnp.bfloat16).reshape(planes, blocks, block_rows, columns)
        outgoing = jnp.einsum(
            "sk,zsrx->kzrx", from_tile, owned_blocks, preferred_element_type=jnp.float32
        ).astype(jnp.bfloat16)
        incoming = lax.all_to_all(
            outgoing.reshape(owners, CAP, planes, block_rows, columns),
            "tiles",
            split_axis=0,
            concat_axis=0,
            tiled=True,
        )
        view_tile = jnp.einsum(
            "sk,kzrx->zsrx",
            to_owner,
            incoming.reshape(slot_count, planes, block_rows, columns),
            preferred_element_type=jnp.float32,
        ).astype(jnp.bfloat16)
        view_tile = view_tile.reshape(planes, height, columns)
        correction = view_correction(view_tile, observed, kernel_y, kernel_x)
        correction = correction.reshape(planes, blocks, block_rows, columns)
        returned = jnp.einsum(
            "sk,zsrx->kzrx", to_owner, correction, preferred_element_type=jnp.float32
        ).astype(jnp.bfloat16)
        gathered = lax.all_to_all(
            returned.reshape(owners, CAP, planes, block_rows, columns),
            "tiles",
            split_axis=0,
            concat_axis=0,
            tiled=True,
        )
        owned_rows = jnp.einsum(
            "sk,kzrx->zsrx",
            from_tile,
            gathered.reshape(slot_count, planes, block_rows, columns),
            preferred_element_type=jnp.float32,
        ).reshape(planes, height, columns)
        log_values = jnp.log(owned_rows)
        share_rows = height // view_count
        log_part = lax.psum_scatter(log_values, "views", scatter_dimension=1, tiled=True)
        first_row = lax.axis_index("views") * share_rows
        window = lax.dynamic_slice_in_dim(padded, first_row, share_rows + 2, 1)
        damping = 1.0 - TV_WEIGHT * curvature(window)
        rows_now = lax.dynamic_slice_in_dim(current, first_row, share_rows, 1)
        updated = rows_now * jnp.exp(log_part / view_count) / damping
        current = lax.all_gather(updated, "views", axis=1, tiled=True)
    return current


PAD_ROWS = 16


def chip_order(tiles, views):
    return [v * tiles + (t if v % 2 == 0 else tiles - 1 - t) for t in range(tiles) for v in range(views)]


def correction_kernel(offsets_ref, current_ref, data_ref, matrices_ref, log_ref, tiles_ref, halves_ref, back_ref):
    views, blocks = offsets_ref.shape
    tiles = data_ref.shape[0]
    height, columns = matrices_ref.shape[-2] // 2, matrices_ref.shape[-1]
    rows = height // blocks
    for v in range(views):
        for t in range(tiles):
            for s in range(blocks):
                owner = lax.rem(t + offsets_ref[v, s], tiles)
                start = pl.multiple_of(owner * height + s * rows, rows)
                tiles_ref[s * rows : (s + 1) * rows, t * columns : (t + 1) * columns] = current_ref[
                    pl.ds(start, rows), :
                ]
        half = jnp.dot(matrices_ref[v, 0], tiles_ref[...], preferred_element_type=jnp.float32)
        half = half.astype(jnp.bfloat16)
        for t in range(tiles):
            for r in range(2):
                halves_ref[t * height : (t + 1) * height, r * columns : (r + 1) * columns] = half[
                    r * height : (r + 1) * height, t * columns : (t + 1) * columns
                ]
        blurred = jnp.dot(halves_ref[...], matrices_ref[v, 1], preferred_element_type=jnp.float32)
        for t in range(tiles):
            observed = data_ref[t, v, 0:height, :].astype(jnp.float32)
            quotient = observed / blurred[t * height : (t + 1) * height]
            tiles_ref[:, t * columns : (t + 1) * columns] = quotient.astype(jnp.bfloat16)
        half = jnp.dot(matrices_ref[v, 2], tiles_ref[...], preferred_element_type=jnp.float32)
        half = half.astype(jnp.bfloat16)
        for t in range(tiles):
            for r in range(2):
                halves_ref[t * height : (t + 1) * height, r * columns : (r + 1) * columns] = half[
                    r * height : (r + 1) * height, t * columns : (t + 1) * columns
                ]
        back = jnp.dot(halves_ref[...], matrices_ref[v, 3], preferred_element_type=jnp.float32)
        back_ref[v] = jnp.log(back.astype(jnp.bfloat16).astype(jnp.float32))
    for o in range(tiles):
        for s in range(blocks):
            total = None
            for v in range(views):
                tile = lax.rem(o - offsets_ref[v, s] + tiles, tiles)
                start = pl.multiple_of(tile * height + s * rows, rows)
                part = back_ref[v, pl.ds(start, rows), :]
                total = part if total is None else total + part
            log_ref[o * height + s * rows : o * height + (s + 1) * rows, :] = total


def correction_logs(offsets, current, received, matrices):
    tiles, views = received.shape[:2]
    height = matrices.shape[-2] // 2
    columns = current.shape[-1]
    return pl.pallas_call(
        correction_kernel,
        out_shape=jax.ShapeDtypeStruct(current.shape, jnp.float32),
        in_specs=[pl.BlockSpec(memory_space=pltpu.SMEM)] + [pl.BlockSpec(memory_space=pltpu.VMEM)] * 3,
        out_specs=pl.BlockSpec(memory_space=pltpu.VMEM),
        scratch_shapes=[
            pltpu.VMEM((height, tiles * columns), jnp.bfloat16),
            pltpu.VMEM((tiles * height, 2 * columns), jnp.bfloat16),
            pltpu.VMEM((views, tiles * height, columns), jnp.float32),
        ],
        cost_estimate=pl.CostEstimate(flops=300_000_000, bytes_accessed=1_500_000, transcendentals=0),
        name="correction",
    )(offsets, current, received, matrices)


def update_kernel(views, core_ref, current_ref, twin_ref, other_ref, log_ref, new_ref, narrow_ref):
    rows, columns = current_ref.shape
    first = core_ref[0] == 0
    current = current_ref[...]
    twin, other = twin_ref[...], other_ref[...]
    above = jnp.where(first, twin, other)
    below = jnp.where(first, other, twin)
    row = lax.broadcasted_iota(jnp.int32, (rows, columns), 0)
    column = lax.broadcasted_iota(jnp.int32, (rows, columns), 1)

    def next_row(x):
        return jnp.where(row == rows - 1, 0.0, pltpu.roll(x, rows - 1, 0))

    def next_column(x):
        return jnp.where(column == columns - 1, 0.0, pltpu.roll(x, columns - 1, 1))

    def scale(z, y, x):
        return lax.rsqrt(z * z + y * y + x * x + SMOOTH_SQUARE)

    grad_z = above - current
    grad_y = next_row(current) - current
    grad_x = next_column(current) - current
    inverse = scale(grad_z, grad_y, grad_x)
    unit_y, unit_x = grad_y * inverse, grad_x * inverse
    edge = current * lax.rsqrt(current * current + SMOOTH_SQUARE)
    before_y = jnp.where(row == 0, edge, pltpu.roll(unit_y, 1, 0))
    before_x = jnp.where(column == 0, edge, pltpu.roll(unit_x, 1, 1))
    lower_z = current - below
    lower = lower_z * scale(lower_z, next_row(below) - below, next_column(below) - below)
    divergence = grad_z * inverse - lower + (unit_y - before_y) + (unit_x - before_x)
    damping = 1.0 - TV_WEIGHT * divergence
    new = current * jnp.exp(log_ref[...] / views) / damping
    new_ref[...] = new
    narrow_ref[...] = new.astype(narrow_ref.dtype)


def update(views, core, current, twin, other, logs):
    return pl.pallas_call(
        functools.partial(update_kernel, views),
        out_shape=(
            jax.ShapeDtypeStruct(current.shape, jnp.float32),
            jax.ShapeDtypeStruct(current.shape, jnp.bfloat16),
        ),
        in_specs=[pl.BlockSpec(memory_space=pltpu.SMEM)] + [pl.BlockSpec(memory_space=pltpu.VMEM)] * 4,
        out_specs=[pl.BlockSpec(memory_space=pltpu.VMEM)] * 2,
        name="update",
    )(core, current, twin, other, logs)


def plane_shards(view_data, estimate, psf_taps, offsets):
    tiles, views = lax.axis_size("tiles"), lax.axis_size("views")
    grid = ("tiles", "views")
    places = chip_order(tiles, views)
    planes, height, columns = estimate.shape
    half_planes = planes // 2
    blocks = offsets.shape[1]
    taps = psf_taps.shape[-1]
    share = height // views
    core = lax.axis_index("gz")
    view = lax.axis_index("views")

    rows = lax.dynamic_slice_in_dim(estimate, view * share, share, 1)
    high = lax.reduce_precision(rows, 8, 7)
    low = rows - high
    info = jnp.concatenate([psf_taps.reshape(-1), offsets.reshape(-1).astype(jnp.float32)])
    info = jnp.pad(info, (0, columns - info.shape[0])).astype(jnp.bfloat16)
    payload = jnp.concatenate(
        [
            view_data[0, 0],
            high.astype(jnp.bfloat16),
            low.astype(jnp.bfloat16),
            jnp.broadcast_to(info, (planes, PAD_ROWS, columns)),
        ],
        axis=1,
    )
    paired = payload.reshape(half_planes, 2, payload.shape[1], columns)
    keep = lax.dynamic_index_in_dim(paired, core, 1, keepdims=False)
    give = lax.dynamic_index_in_dim(paired, 1 - core, 1, keepdims=False)
    swap = [(0, 1), (1, 0)]
    got = lax.ppermute(give, "gz", swap)
    lead = jnp.where(core == 0, keep, got)
    rear = jnp.where(core == 0, got, keep)
    outgoing = jnp.stack([lead[p] if p < half_planes else rear[p - half_planes] for p in places])
    received = lax.all_to_all(outgoing, grid, 0, 0, tiled=True)
    received = received.reshape(tiles, views, payload.shape[1], columns)

    narrow = received[:, :, height : height + share].reshape(tiles * height, columns)
    rest = received[:, :, height + share : height + 2 * share].reshape(tiles * height, columns)
    current = narrow.astype(jnp.float32) + rest.astype(jnp.float32)
    info = received[0, :, height + 2 * share, :].astype(jnp.float32)
    profiles = info[:, : 4 * taps].reshape(views, 2, 2, taps)
    shifts = info[:, 4 * taps : 4 * taps + blocks].astype(jnp.int32)
    profile_y, profile_x = profiles[:, :, 0], profiles[:, :, 1]
    chosen = jnp.stack([profile_y, profile_x[..., ::-1], profile_y[..., ::-1], profile_x], axis=1)
    matrices = jax.vmap(jax.vmap(jax.vmap(lambda p: toeplitz_matrix(p, columns))))(chosen)
    matrices = matrices.reshape(views, 4, 2 * columns, columns)

    def place(t, v):
        return places[t * views + v]

    at = {place(t, v): t * views + v for t in range(tiles) for v in range(views)}
    hops = []
    for p in range(planes - 1):
        one, two = at[p] * 2 + 1, at[p + 1] * 2
        hops += [(one, two), (two, one)]

    flag = core.reshape(1).astype(jnp.int32)
    for iteration in range(ITERS):
        other = lax.ppermute(current, ("tiles", "views", "gz"), hops)
        twin = lax.ppermute(current, "gz", swap)
        logs = correction_logs(shifts, narrow, received, matrices)
        current, narrow = update(views, flag, current, twin, other, logs)

    result = current.astype(jnp.float16).reshape(tiles, 1, height, columns)
    result = jnp.broadcast_to(result, (tiles, views, height, columns)).reshape(planes, height, columns)
    result = lax.all_to_all(result, grid, 0, 0, tiled=True)
    result = jnp.stack([result[at[p]] for p in range(planes)])
    result = result.reshape(2, half_planes, height, columns)
    keep = lax.dynamic_index_in_dim(result, core, 0, keepdims=False)
    give = lax.dynamic_index_in_dim(result, 1 - core, 0, keepdims=False)
    got = lax.ppermute(give, "gz", swap)
    even = jnp.where(core == 0, keep, got)
    odd = jnp.where(core == 0, got, keep)
    return jnp.stack([even, odd], axis=1).reshape(planes, height, columns).astype(jnp.float32)


def one_plane_each(mesh, view_data, estimate, psf_taps, offsets):
    tiles, views, depth = mesh.shape["tiles"], mesh.shape["views"], mesh.shape["gz"]
    planes = estimate.shape[0] // (mesh.shape["groups"] * depth)
    height, columns = estimate.shape[1] // tiles, estimate.shape[2]
    return (
        depth == 2
        and tiles * views == planes
        and planes % 2 == 0
        and height == columns
        and height % (16 * offsets.shape[1]) == 0
        and height % (16 * views) == 0
        and 4 * psf_taps.shape[-1] + offsets.shape[1] <= columns
    )


def solution(mesh):
    in_specs = (
        P(("groups", "views"), "tiles", "gz", None, None),
        P(("groups", "gz"), "tiles", None),
        P("views", None, None, None),
        P("views", None),
    )
    out_specs = P(("groups", "gz"), "tiles", None)

    def step(*arrays):
        body = plane_shards if one_plane_each(mesh, *arrays) else shards
        return jax.shard_map(body, mesh=mesh, in_specs=in_specs, out_specs=out_specs, check_vma=False)(*arrays)

    return step
```

```python
import functools

import jax
import jax.numpy as jnp
from jax import lax
from jax.experimental import pallas as pl
from jax.experimental.pallas import tpu as pltpu
from jax.sharding import PartitionSpec as P

ITERS = 2
CAP = 4


TV_WEIGHT = 0.1
SMOOTH_SQUARE = 0.0025


def with_halo(cells, sides, width):
    for axis, dim in sides:
        count = lax.axis_size(axis)
        ends = count - 1
        head = lax.slice_in_dim(cells, 0, width, axis=dim)
        tail = lax.slice_in_dim(cells, cells.shape[dim] - width, cells.shape[dim], axis=dim)
        cells = jnp.concatenate(
            [
                lax.ppermute(tail, axis, [(i, (i + 1) % count) for i in range(ends)]),
                cells,
                lax.ppermute(head, axis, [((i + 1) % count, i) for i in range(ends)]),
            ],
            axis=dim,
        )
    return cells


def toeplitz_matrix(profile, length):
    half_width = (profile.shape[0] - 1) // 2
    position = jnp.arange(length, dtype=jnp.int32)
    offset = position[None, :] - position[:, None] + half_width
    tap_index = jnp.arange(profile.shape[0], dtype=jnp.int32)
    picked = (offset[:, :, None] == tap_index[None, None, :]).astype(jnp.float32)
    return jnp.sum(picked * profile[None, None, :], axis=2).astype(jnp.bfloat16)


def curvature(padded):
    anchor = padded[:-1, :-1, :-1]
    grad_z = padded[1:, :-1, :-1] - anchor
    grad_y = padded[:-1, 1:, :-1] - anchor
    grad_x = padded[:-1, :-1, 1:] - anchor
    magnitude = jnp.sqrt(grad_z * grad_z + grad_y * grad_y + grad_x * grad_x + SMOOTH_SQUARE)
    unit_z = grad_z / magnitude
    unit_y = grad_y / magnitude
    unit_x = grad_x / magnitude
    return (
        unit_z[1:, 1:, 1:]
        - unit_z[:-1, 1:, 1:]
        + (unit_y[1:, 1:, 1:] - unit_y[1:, :-1, 1:])
        + (unit_x[1:, 1:, 1:] - unit_x[1:, 1:, :-1])
    )


def view_correction(view_tile, observed, kernel_y, kernel_x):
    blurred = jnp.zeros(view_tile.shape, jnp.float32)
    for term_index in range(2):
        half_blur = jnp.einsum(
            "yk,zkx->zyx", kernel_y[term_index], view_tile, preferred_element_type=jnp.float32
        ).astype(jnp.bfloat16)
        blurred = blurred + jnp.einsum(
            "zyk,xk->zyx", half_blur, kernel_x[term_index], preferred_element_type=jnp.float32
        )
    quotient = (observed.astype(jnp.float32) / blurred).astype(jnp.bfloat16)
    log_sum = jnp.zeros(view_tile.shape, jnp.float32)
    for term_index in range(2):
        half_back = jnp.einsum(
            "ky,zkx->zyx", kernel_y[term_index], quotient, preferred_element_type=jnp.float32
        ).astype(jnp.bfloat16)
        log_sum = log_sum + jnp.einsum(
            "zyk,kx->zyx", half_back, kernel_x[term_index], preferred_element_type=jnp.float32
        )
    return log_sum.astype(jnp.bfloat16)


def shards(view_data, estimate, psf_taps, offsets):
    owners = lax.axis_size("tiles")
    view_count = lax.axis_size("views")
    observed = view_data[0, 0]
    planes, height, columns = estimate.shape
    view_shift = offsets[0]
    blocks = view_shift.shape[0]
    block_rows = height // blocks
    slot_count = owners * CAP
    kernel_y = jnp.stack(
        [toeplitz_matrix(psf_taps[0, term_index, 0], height) for term_index in range(2)]
    )
    kernel_x = jnp.stack(
        [toeplitz_matrix(psf_taps[0, term_index, 1], columns) for term_index in range(2)]
    )
    position = jnp.arange(blocks, dtype=jnp.int32)
    same_owner = view_shift[:, None] == view_shift[None, :]
    before = position[None, :] < position[:, None]
    slot_rank = jnp.sum((same_owner & before).astype(jnp.int32), axis=1)
    member = lax.axis_index("tiles")
    target = (member + view_shift) % owners
    source_tile = (member - view_shift) % owners
    slot_index = jnp.arange(slot_count, dtype=jnp.int32)
    to_owner = ((target * CAP + slot_rank)[:, None] == slot_index[None, :]).astype(jnp.bfloat16)
    from_tile = ((source_tile * CAP + slot_rank)[:, None] == slot_index[None, :]).astype(
        jnp.bfloat16
    )
    current = estimate
    for iteration in range(ITERS):
        padded = with_halo(current, (("tiles", 1), ("gz", 0)), 1)
        padded = jnp.pad(padded, ((0, 0), (0, 0), (1, 1)))
        owned_blocks = current.astype(jnp.bfloat16).reshape(planes, blocks, block_rows, columns)
        outgoing = jnp.einsum(
            "sk,zsrx->kzrx", from_tile, owned_blocks, preferred_element_type=jnp.float32
        ).astype(jnp.bfloat16)
        incoming = lax.all_to_all(
            outgoing.reshape(owners, CAP, planes, block_rows, columns),
            "tiles",
            split_axis=0,
            concat_axis=0,
            tiled=True,
        )
        view_tile = jnp.einsum(
            "sk,kzrx->zsrx",
            to_owner,
            incoming.reshape(slot_count, planes, block_rows, columns),
            preferred_element_type=jnp.float32,
        ).astype(jnp.bfloat16)
        view_tile = view_tile.reshape(planes, height, columns)
        correction = view_correction(view_tile, observed, kernel_y, kernel_x)
        correction = correction.reshape(planes, blocks, block_rows, columns)
        returned = jnp.einsum(
            "sk,zsrx->kzrx", to_owner, correction, preferred_element_type=jnp.float32
        ).astype(jnp.bfloat16)
        gathered = lax.all_to_all(
            returned.reshape(owners, CAP, planes, block_rows, columns),
            "tiles",
            split_axis=0,
            concat_axis=0,
            tiled=True,
        )
        owned_rows = jnp.einsum(
            "sk,kzrx->zsrx",
            from_tile,
            gathered.reshape(slot_count, planes, block_rows, columns),
            preferred_element_type=jnp.float32,
        ).reshape(planes, height, columns)
        log_values = jnp.log(owned_rows)
        share_rows = height // view_count
        log_part = lax.psum_scatter(log_values, "views", scatter_dimension=1, tiled=True)
        first_row = lax.axis_index("views") * share_rows
        window = lax.dynamic_slice_in_dim(padded, first_row, share_rows + 2, 1)
        damping = 1.0 - TV_WEIGHT * curvature(window)
        rows_now = lax.dynamic_slice_in_dim(current, first_row, share_rows, 1)
        updated = rows_now * jnp.exp(log_part / view_count) / damping
        current = lax.all_gather(updated, "views", axis=1, tiled=True)
    return current


INFO_ROWS = 16
CHUNK = 32
VMEM = pl.BlockSpec(memory_space=pltpu.VMEM)
SMEM = pl.BlockSpec(memory_space=pltpu.SMEM)
LIMIT = pltpu.CompilerParams(vmem_limit_bytes=16 * 2**20)


def gather_kernel(tiles, tile_ref, *refs):
    pieces, (wide_ref, narrow_ref) = refs[:tiles], refs[tiles:]
    for k in range(tiles):
        owner = lax.bitwise_xor(tile_ref[0], k)
        wide_ref[owner] = pieces[k][...]
        narrow_ref[owner] = pieces[k][...].astype(narrow_ref.dtype)


def gather_plane(tile, pieces):
    shape = (len(pieces), *pieces[0].shape)
    return pl.pallas_call(
        functools.partial(gather_kernel, len(pieces)),
        out_shape=(jax.ShapeDtypeStruct(shape, jnp.float32), jax.ShapeDtypeStruct(shape, jnp.bfloat16)),
        in_specs=[SMEM] + [VMEM] * len(pieces),
        out_specs=[VMEM] * 2,
        compiler_params=LIMIT,
        name="gather_plane",
    )(tile, *pieces)


def correction_kernel(tiles, tile_ref, offsets_ref, current_ref, matrices_ref, *refs):
    data, log_ref = refs[:tiles], refs[tiles]
    work = refs[tiles + 1 :]
    views, blocks = offsets_ref.shape
    height, columns = data[0].shape[-2:]
    rows = height // blocks
    me = tile_ref[0]
    shift = [[offsets_ref[w, s] for s in range(blocks)] for w in range(views)]
    planes = [work[3 * w] for w in range(views)]
    halves = [work[3 * w + 1] for w in range(views)]
    logs = [work[3 * w + 2] for w in range(views)]

    def first(w, kind):
        half = jnp.dot(matrices_ref[w, kind], planes[w][...], preferred_element_type=jnp.float32)
        half = half.astype(jnp.bfloat16)
        for k in range(tiles):
            for r in range(2):
                halves[w][k * height : (k + 1) * height, r * columns : (r + 1) * columns] = half[
                    r * height : (r + 1) * height, k * columns : (k + 1) * columns
                ]

    for w in range(views):
        for k in range(tiles):
            tile = lax.bitwise_xor(me, k)
            for s in range(blocks):
                owner = lax.rem(tile + shift[w][s], tiles)
                planes[w][s * rows : (s + 1) * rows, k * columns : (k + 1) * columns] = current_ref[
                    owner, s * rows : (s + 1) * rows, :
                ]
    for w in range(views):
        first(w, 0)
    for w in range(views):
        blurred = jnp.dot(halves[w][...], matrices_ref[w, 1], preferred_element_type=jnp.float32)
        for k in range(tiles):
            quotient = data[k][w].astype(jnp.float32) / blurred[k * height : (k + 1) * height]
            planes[w][:, k * columns : (k + 1) * columns] = quotient.astype(jnp.bfloat16)
    for w in range(views):
        first(w, 2)
    for w in range(views):
        back = jnp.dot(halves[w][...], matrices_ref[w, 3], preferred_element_type=jnp.float32)
        logs[w][...] = jnp.log(back.astype(jnp.bfloat16).astype(jnp.float32))
    for o in range(tiles):
        for s in range(blocks):
            total = None
            for w in range(views):
                tile = lax.rem(o - shift[w][s] + tiles, tiles)
                start = pl.multiple_of(lax.bitwise_xor(tile, me) * height + s * rows, rows)
                part = logs[w][pl.ds(start, rows), :]
                total = part if total is None else total + part
            log_ref[o * height + s * rows : o * height + (s + 1) * rows, :] = total


def correction_logs(tile, offsets, current, matrices, data):
    tiles, height, columns = current.shape
    scratch = [
        pltpu.VMEM((height, tiles * columns), jnp.bfloat16),
        pltpu.VMEM((tiles * height, 2 * columns), jnp.bfloat16),
        pltpu.VMEM((tiles * height, columns), jnp.float32),
    ]
    return pl.pallas_call(
        functools.partial(correction_kernel, tiles),
        out_shape=jax.ShapeDtypeStruct((tiles * height, columns), jnp.float32),
        in_specs=[SMEM, SMEM] + [VMEM] * (2 + tiles),
        out_specs=VMEM,
        scratch_shapes=scratch * offsets.shape[0],
        cost_estimate=pl.CostEstimate(flops=300_000_000, bytes_accessed=1_500_000, transcendentals=0),
        compiler_params=LIMIT,
        name="correction",
    )(tile, offsets, current, matrices, *data)


def update_kernel(views, core_ref, current_ref, twin_ref, other_ref, log_ref, new_ref, narrow_ref):
    total, columns = current_ref.shape
    first = core_ref[0] == 0
    row = lax.broadcasted_iota(jnp.int32, (CHUNK, columns), 0)
    column = lax.broadcasted_iota(jnp.int32, (CHUNK, columns), 1)

    def scale(z, y, x):
        return lax.rsqrt(z * z + y * y + x * x + SMOOTH_SQUARE)

    def pick(low, high, start, size):
        return jnp.where(first, low[start : start + size, :], high[start : start + size, :])

    def next_row(x, following):
        return jnp.where(row == CHUNK - 1, following, pltpu.roll(x, CHUNK - 1, 0))

    def next_column(x):
        return jnp.where(column == columns - 1, 0.0, pltpu.roll(x, columns - 1, 1))

    def edge(x):
        return x * lax.rsqrt(x * x + SMOOTH_SQUARE)

    carry = edge(current_ref[0:1, :])
    for start in range(0, total, CHUNK):
        stop = start + CHUNK
        current = current_ref[start:stop, :]
        above = pick(twin_ref, other_ref, start, CHUNK)
        below = pick(other_ref, twin_ref, start, CHUNK)
        if stop < total:
            current_next, below_next = current_ref[stop : stop + 1, :], pick(other_ref, twin_ref, stop, 1)
        else:
            current_next = below_next = jnp.zeros((1, columns), jnp.float32)
        grad_z = above - current
        grad_y = next_row(current, current_next) - current
        grad_x = next_column(current) - current
        inverse = scale(grad_z, grad_y, grad_x)
        unit_y, unit_x = grad_y * inverse, grad_x * inverse
        before_y = jnp.where(row == 0, carry, pltpu.roll(unit_y, 1, 0))
        before_x = jnp.where(column == 0, edge(current), pltpu.roll(unit_x, 1, 1))
        carry = unit_y[CHUNK - 1 : CHUNK, :]
        lower_z = current - below
        lower = lower_z * scale(lower_z, next_row(below, below_next) - below, next_column(below) - below)
        divergence = grad_z * inverse - lower + (unit_y - before_y) + (unit_x - before_x)
        damping = 1.0 - TV_WEIGHT * divergence
        new = current * jnp.exp(log_ref[start:stop, :] * (1.0 / views)) / damping
        new_ref[start:stop, :] = new
        narrow_ref[start:stop, :] = new.astype(narrow_ref.dtype)


def update(views, core, current, twin, other, logs):
    return pl.pallas_call(
        functools.partial(update_kernel, views),
        out_shape=(
            jax.ShapeDtypeStruct(current.shape, jnp.float32),
            jax.ShapeDtypeStruct(current.shape, jnp.bfloat16),
        ),
        in_specs=[SMEM] + [VMEM] * 4,
        out_specs=[VMEM] * 2,
        compiler_params=LIMIT,
        name="update",
    )(core, current, twin, other, logs)


def plane_shards(view_data, estimate, psf_taps, offsets):
    tiles, views = lax.axis_size("tiles"), lax.axis_size("views")
    square = ("tiles", "views", "gz")
    planes, height, columns = estimate.shape
    blocks = offsets.shape[1]
    taps = psf_taps.shape[-1]
    tile, view, core = lax.axis_index("tiles"), lax.axis_index("views"), lax.axis_index("gz")
    straight = view == core
    swap = [(0, 1), (1, 0)]

    def device(t, v, g):
        return (t * views + v) * 2 + g

    def place(chain, t):
        return jnp.where(chain == 0, t, tiles - 1 - t)

    def by_core(x):
        pairs = x.reshape(tiles, 2, *x.shape[1:])
        keep = lax.dynamic_index_in_dim(pairs, core, 1, keepdims=False)
        return keep, lax.ppermute(lax.dynamic_index_in_dim(pairs, 1 - core, 1, keepdims=False), "gz", swap)

    def over_tiles(pick):
        return [pick(tile)] + [
            lax.ppermute(pick(lax.bitwise_xor(tile, k)), "tiles", [(t, t ^ k) for t in range(tiles)])
            for k in range(1, tiles)
        ]

    keep, got = by_core(estimate)
    chain = jnp.where(straight, keep, got)
    pieces = over_tiles(lambda t: lax.dynamic_index_in_dim(chain, place(view, t), 0, keepdims=False))

    keep, got = by_core(view_data[0, 0])
    mine = jnp.where(straight, keep, got)
    info = jnp.concatenate([psf_taps.reshape(-1), offsets.reshape(-1).astype(jnp.float32)])
    info = jnp.pad(info, (0, columns - info.shape[0])).astype(jnp.bfloat16)
    sent = jnp.concatenate(
        [
            jnp.where(straight, got, keep).reshape(tiles * height, columns),
            jnp.broadcast_to(info, (INFO_ROWS, columns)),
        ]
    )
    came = lax.ppermute(sent, "views", swap)
    both = jnp.stack([mine, came[: tiles * height].reshape(tiles, height, columns)], axis=1)
    data = over_tiles(lambda t: lax.dynamic_index_in_dim(both, place(view, t), 0, keepdims=False))

    info = jnp.stack([info, came[tiles * height]]).astype(jnp.float32)
    profiles = info[:, : 4 * taps].reshape(views, 2, 2, taps)
    shifts = info[:, 4 * taps : 4 * taps + blocks].astype(jnp.int32)
    profile_y, profile_x = profiles[:, :, 0], profiles[:, :, 1]
    chosen = jnp.stack([profile_y, profile_x[..., ::-1], profile_y[..., ::-1], profile_x], axis=1)
    matrices = jax.vmap(jax.vmap(jax.vmap(lambda p: toeplitz_matrix(p, columns))))(chosen)
    matrices = matrices.reshape(views, 4, 2 * columns, columns)

    path = [(t, 0) for t in range(tiles)] + [(t, 1) for t in reversed(range(tiles))]
    hops = []
    for here, there in zip(path[:-1], path[1:]):
        one, two = device(*here, 1), device(*there, 0)
        hops += [(one, two), (two, one)]

    me = tile.reshape(1).astype(jnp.int32)
    flag = core.reshape(1).astype(jnp.int32)
    current, narrow = gather_plane(me, pieces)
    current = current.reshape(tiles * height, columns)
    for iteration in range(ITERS):
        other = lax.ppermute(current, square, hops)
        twin = lax.ppermute(current, "gz", swap)
        logs = correction_logs(me, shifts, narrow, matrices, data)
        current, narrow = update(views, flag, current, twin, other, logs)
        narrow = narrow.reshape(tiles, height, columns)

    result = current.astype(jnp.float16).reshape(tiles, height, columns)
    result = jnp.stack(over_tiles(lambda t: lax.dynamic_index_in_dim(result, t, 0, keepdims=False)))
    turn, across = [], []
    for t in range(tiles):
        for v in range(2):
            turn += [(device(t, v, 1 - v), device(t, v, v)), (device(t, v, v), device(t, 1 - v, v))]
            across += [(device(t, v, 1 - v), device(t, 1 - v, v))]
    turned = lax.ppermute(result, square, turn)
    crossed = lax.ppermute(result, square, across)
    same = jnp.where(straight, result, turned)
    twin = jnp.where(straight, turned, crossed)
    ordered = []
    for i in range(tiles):
        k = lax.bitwise_xor(place(core, i), tile)
        same_i = lax.dynamic_index_in_dim(same, k, 0, keepdims=False)
        twin_i = lax.dynamic_index_in_dim(twin, k, 0, keepdims=False)
        ordered += [jnp.where(core == 0, same_i, twin_i), jnp.where(core == 0, twin_i, same_i)]
    return jnp.stack(ordered).astype(jnp.float32)


def one_plane_each(mesh, view_data, estimate, psf_taps, offsets):
    tiles, views, depth = mesh.shape["tiles"], mesh.shape["views"], mesh.shape["gz"]
    planes = estimate.shape[0] // (mesh.shape["groups"] * depth)
    height, columns = estimate.shape[1] // tiles, estimate.shape[2]
    return (
        depth == 2
        and views == 2
        and planes == 2 * tiles
        and tiles & (tiles - 1) == 0
        and height == columns
        and height % (16 * offsets.shape[1]) == 0
        and 4 * psf_taps.shape[-1] + offsets.shape[1] <= columns
    )


def solution(mesh):
    in_specs = (
        P(("groups", "views"), "tiles", "gz", None, None),
        P(("groups", "gz"), "tiles", None),
        P("views", None, None, None),
        P("views", None),
    )
    out_specs = P(("groups", "gz"), "tiles", None)

    def step(*arrays):
        body = plane_shards if one_plane_each(mesh, *arrays) else shards
        return jax.shard_map(body, mesh=mesh, in_specs=in_specs, out_specs=out_specs, check_vma=False)(*arrays)

    return step
```

```python
import functools

import jax
import jax.numpy as jnp
from jax import lax
from jax.experimental import pallas as pl
from jax.experimental.pallas import tpu as pltpu
from jax.sharding import PartitionSpec as P


ITERS = 2
CAP = 4


TV_WEIGHT = 0.1
SMOOTH_SQUARE = 0.0025


def with_halo(cells, sides, width):
    for axis, dim in sides:
        count = lax.axis_size(axis)
        ends = count - 1
        head = lax.slice_in_dim(cells, 0, width, axis=dim)
        tail = lax.slice_in_dim(cells, cells.shape[dim] - width, cells.shape[dim], axis=dim)
        cells = jnp.concatenate(
            [
                lax.ppermute(tail, axis, [(i, (i + 1) % count) for i in range(ends)]),
                cells,
                lax.ppermute(head, axis, [((i + 1) % count, i) for i in range(ends)]),
            ],
            axis=dim,
        )
    return cells


def toeplitz_matrix(profile, length):
    half_width = (profile.shape[0] - 1) // 2
    position = jnp.arange(length, dtype=jnp.int32)
    offset = position[None, :] - position[:, None] + half_width
    tap_index = jnp.arange(profile.shape[0], dtype=jnp.int32)
    picked = (offset[:, :, None] == tap_index[None, None, :]).astype(jnp.float32)
    return jnp.sum(picked * profile[None, None, :], axis=2).astype(jnp.bfloat16)


def curvature(padded):
    anchor = padded[:-1, :-1, :-1]
    grad_z = padded[1:, :-1, :-1] - anchor
    grad_y = padded[:-1, 1:, :-1] - anchor
    grad_x = padded[:-1, :-1, 1:] - anchor
    magnitude = jnp.sqrt(grad_z * grad_z + grad_y * grad_y + grad_x * grad_x + SMOOTH_SQUARE)
    unit_z = grad_z / magnitude
    unit_y = grad_y / magnitude
    unit_x = grad_x / magnitude
    return (
        unit_z[1:, 1:, 1:]
        - unit_z[:-1, 1:, 1:]
        + (unit_y[1:, 1:, 1:] - unit_y[1:, :-1, 1:])
        + (unit_x[1:, 1:, 1:] - unit_x[1:, 1:, :-1])
    )


def view_correction(view_tile, observed, kernel_y, kernel_x):
    blurred = jnp.zeros(view_tile.shape, jnp.float32)
    for term_index in range(2):
        half_blur = jnp.einsum(
            "yk,zkx->zyx", kernel_y[term_index], view_tile, preferred_element_type=jnp.float32
        ).astype(jnp.bfloat16)
        blurred = blurred + jnp.einsum(
            "zyk,xk->zyx", half_blur, kernel_x[term_index], preferred_element_type=jnp.float32
        )
    quotient = (observed.astype(jnp.float32) / blurred).astype(jnp.bfloat16)
    log_sum = jnp.zeros(view_tile.shape, jnp.float32)
    for term_index in range(2):
        half_back = jnp.einsum(
            "ky,zkx->zyx", kernel_y[term_index], quotient, preferred_element_type=jnp.float32
        ).astype(jnp.bfloat16)
        log_sum = log_sum + jnp.einsum(
            "zyk,kx->zyx", half_back, kernel_x[term_index], preferred_element_type=jnp.float32
        )
    return log_sum.astype(jnp.bfloat16)


def shards(view_data, estimate, psf_taps, offsets):
    owners = lax.axis_size("tiles")
    view_count = lax.axis_size("views")
    observed = view_data[0, 0]
    planes, height, columns = estimate.shape
    view_shift = offsets[0]
    blocks = view_shift.shape[0]
    block_rows = height // blocks
    slot_count = owners * CAP
    kernel_y = jnp.stack(
        [toeplitz_matrix(psf_taps[0, term_index, 0], height) for term_index in range(2)]
    )
    kernel_x = jnp.stack(
        [toeplitz_matrix(psf_taps[0, term_index, 1], columns) for term_index in range(2)]
    )
    position = jnp.arange(blocks, dtype=jnp.int32)
    same_owner = view_shift[:, None] == view_shift[None, :]
    before = position[None, :] < position[:, None]
    slot_rank = jnp.sum((same_owner & before).astype(jnp.int32), axis=1)
    member = lax.axis_index("tiles")
    target = (member + view_shift) % owners
    source_tile = (member - view_shift) % owners
    slot_index = jnp.arange(slot_count, dtype=jnp.int32)
    to_owner = ((target * CAP + slot_rank)[:, None] == slot_index[None, :]).astype(jnp.bfloat16)
    from_tile = ((source_tile * CAP + slot_rank)[:, None] == slot_index[None, :]).astype(
        jnp.bfloat16
    )
    current = estimate
    for _ in range(ITERS):
        padded = with_halo(current, (("tiles", 1), ("gz", 0)), 1)
        padded = jnp.pad(padded, ((0, 0), (0, 0), (1, 1)))
        owned_blocks = current.astype(jnp.bfloat16).reshape(planes, blocks, block_rows, columns)
        outgoing = jnp.einsum(
            "sk,zsrx->kzrx", from_tile, owned_blocks, preferred_element_type=jnp.float32
        ).astype(jnp.bfloat16)
        incoming = lax.all_to_all(
            outgoing.reshape(owners, CAP, planes, block_rows, columns),
            "tiles",
            split_axis=0,
            concat_axis=0,
            tiled=True,
        )
        view_tile = jnp.einsum(
            "sk,kzrx->zsrx",
            to_owner,
            incoming.reshape(slot_count, planes, block_rows, columns),
            preferred_element_type=jnp.float32,
        ).astype(jnp.bfloat16)
        view_tile = view_tile.reshape(planes, height, columns)
        correction = view_correction(view_tile, observed, kernel_y, kernel_x)
        correction = correction.reshape(planes, blocks, block_rows, columns)
        returned = jnp.einsum(
            "sk,zsrx->kzrx", to_owner, correction, preferred_element_type=jnp.float32
        ).astype(jnp.bfloat16)
        gathered = lax.all_to_all(
            returned.reshape(owners, CAP, planes, block_rows, columns),
            "tiles",
            split_axis=0,
            concat_axis=0,
            tiled=True,
        )
        owned_rows = jnp.einsum(
            "sk,kzrx->zsrx",
            from_tile,
            gathered.reshape(slot_count, planes, block_rows, columns),
            preferred_element_type=jnp.float32,
        ).reshape(planes, height, columns)
        log_values = jnp.log(owned_rows)
        share_rows = height // view_count
        log_part = lax.psum_scatter(log_values, "views", scatter_dimension=1, tiled=True)
        first_row = lax.axis_index("views") * share_rows
        window = lax.dynamic_slice_in_dim(padded, first_row, share_rows + 2, 1)
        damping = 1.0 - TV_WEIGHT * curvature(window)
        rows_now = lax.dynamic_slice_in_dim(current, first_row, share_rows, 1)
        updated = rows_now * jnp.exp(log_part / view_count) / damping
        current = lax.all_gather(updated, "views", axis=1, tiled=True)
    return current


INFO_ROWS = 16
CHUNK = 32
ANY = pl.BlockSpec(memory_space=pl.ANY)
VMEM = pl.BlockSpec(memory_space=pltpu.VMEM)
SMEM = pl.BlockSpec(memory_space=pltpu.SMEM)
LIMIT = pltpu.CompilerParams(vmem_limit_bytes=16 * 2**20)


def split_kernel(core_ref, wide_ref, narrow_ref, *refs):
    outs, sems = refs[:-1], refs[-1]
    core = core_ref[0]
    copies = []
    for n, (source, pick) in enumerate(
        [(wide_ref, 1 - core), (narrow_ref, 1 - core), (wide_ref, core), (narrow_ref, core)]
    ):
        copies.append(pltpu.make_async_copy(source.at[:, pick], outs[n], sems.at[n]))
    for copy in copies:
        copy.start()
    for copy in copies:
        copy.wait()


def split_by_core(core, wide, narrow):
    pairs = [x.reshape(x.shape[0] // 2, 2, *x.shape[1:]) for x in (wide, narrow)]
    shapes = [jax.ShapeDtypeStruct((x.shape[0], *x.shape[2:]), x.dtype) for x in pairs]
    return pl.pallas_call(
        split_kernel,
        out_shape=shapes * 2,
        in_specs=[SMEM, ANY, ANY],
        out_specs=[VMEM] * 4,
        scratch_shapes=[pltpu.SemaphoreType.DMA((4,))],
        compiler_params=LIMIT,
        name="split_by_core",
    )(core, *pairs)


def matrices_kernel(taps, info_ref, out_ref):
    views, columns = info_ref.shape
    length = out_ref.shape[-2] // 2
    half_width = (taps - 1) // 2
    row = lax.broadcasted_iota(jnp.int32, (length, columns), 0)
    column = lax.broadcasted_iota(jnp.int32, (length, columns), 1)
    band = jnp.abs(row - column) <= half_width
    for v in range(views):
        profile = jnp.broadcast_to(info_ref[v : v + 1, :], (8, columns))
        for kind, (flipped, axis) in enumerate([(0, 0), (1, 1), (1, 0), (0, 1)]):
            for r in range(2):
                lane = (4 * flipped + 2 * r + axis) * taps + half_width
                spread = jnp.broadcast_to(pltpu.roll(profile, columns - lane, 1)[0:1], (length, columns))
                rolled = pltpu.roll(spread, 0, 1, stride=1, stride_axis=0)
                rolled = jnp.where(band, rolled, 0.0).astype(out_ref.dtype)
                out_ref[v, kind, r * length : (r + 1) * length, :] = rolled


def blur_matrices(taps, length, info):
    views, columns = info.shape
    return pl.pallas_call(
        functools.partial(matrices_kernel, taps),
        out_shape=jax.ShapeDtypeStruct((views, 4, 2 * length, columns), jnp.bfloat16),
        in_specs=[VMEM],
        out_specs=VMEM,
        compiler_params=LIMIT,
        name="blur_matrices",
    )(info)


def gather_kernel(tiles, tile_ref, *refs):
    pieces, (wide_ref, narrow_ref) = refs[:tiles], refs[tiles:]
    for k in range(tiles):
        owner = lax.bitwise_xor(tile_ref[0], k)
        wide_ref[owner] = pieces[k][...]
        narrow_ref[owner] = pieces[k][...].astype(narrow_ref.dtype)


def gather_plane(tile, pieces):
    shape = (len(pieces), *pieces[0].shape)
    return pl.pallas_call(
        functools.partial(gather_kernel, len(pieces)),
        out_shape=(jax.ShapeDtypeStruct(shape, jnp.float32), jax.ShapeDtypeStruct(shape, jnp.bfloat16)),
        in_specs=[SMEM] + [VMEM] * len(pieces),
        out_specs=[VMEM] * 2,
        compiler_params=LIMIT,
        name="gather_plane",
    )(tile, *pieces)


def correction_kernel(tiles, tile_ref, offsets_ref, current_ref, matrices_ref, *refs):
    data, log_ref = refs[:tiles], refs[tiles]
    work = refs[tiles + 1 :]
    views, blocks = offsets_ref.shape
    height, columns = data[0].shape[-2:]
    rows = height // blocks
    me = tile_ref[0]
    shift = [[offsets_ref[w, s] for s in range(blocks)] for w in range(views)]
    planes = [work[3 * w] for w in range(views)]
    halves = [work[3 * w + 1] for w in range(views)]
    logs = [work[3 * w + 2] for w in range(views)]

    def first(w, kind):
        half = jnp.dot(matrices_ref[w, kind], planes[w][...], preferred_element_type=jnp.float32)
        half = half.astype(jnp.bfloat16)
        for k in range(tiles):
            for r in range(2):
                halves[w][k * height : (k + 1) * height, r * columns : (r + 1) * columns] = half[
                    r * height : (r + 1) * height, k * columns : (k + 1) * columns
                ]

    for w in range(views):
        for k in range(tiles):
            tile = lax.bitwise_xor(me, k)
            for s in range(blocks):
                owner = lax.rem(tile + shift[w][s], tiles)
                planes[w][s * rows : (s + 1) * rows, k * columns : (k + 1) * columns] = current_ref[
                    owner, s * rows : (s + 1) * rows, :
                ]
    for w in range(views):
        first(w, 0)
    for w in range(views):
        blurred = jnp.dot(halves[w][...], matrices_ref[w, 1], preferred_element_type=jnp.float32)
        for k in range(tiles):
            quotient = data[k][w].astype(jnp.float32) / blurred[k * height : (k + 1) * height]
            planes[w][:, k * columns : (k + 1) * columns] = quotient.astype(jnp.bfloat16)
    for w in range(views):
        first(w, 2)
    for w in range(views):
        back = jnp.dot(halves[w][...], matrices_ref[w, 3], preferred_element_type=jnp.float32)
        logs[w][...] = jnp.log(back.astype(jnp.bfloat16).astype(jnp.float32))
    for o in range(tiles):
        for s in range(blocks):
            total = None
            for w in range(views):
                tile = lax.rem(o - shift[w][s] + tiles, tiles)
                start = pl.multiple_of(lax.bitwise_xor(tile, me) * height + s * rows, rows)
                part = logs[w][pl.ds(start, rows), :]
                total = part if total is None else total + part
            log_ref[o * height + s * rows : o * height + (s + 1) * rows, :] = total


def correction_logs(tile, offsets, current, matrices, data):
    tiles, height, columns = current.shape
    scratch = [
        pltpu.VMEM((height, tiles * columns), jnp.bfloat16),
        pltpu.VMEM((tiles * height, 2 * columns), jnp.bfloat16),
        pltpu.VMEM((tiles * height, columns), jnp.float32),
    ]
    return pl.pallas_call(
        functools.partial(correction_kernel, tiles),
        out_shape=jax.ShapeDtypeStruct((tiles * height, columns), jnp.float32),
        in_specs=[SMEM, SMEM] + [VMEM] * (2 + tiles),
        out_specs=VMEM,
        scratch_shapes=scratch * offsets.shape[0],
        cost_estimate=pl.CostEstimate(flops=300_000_000, bytes_accessed=1_500_000, transcendentals=0),
        compiler_params=LIMIT,
        name="correction",
    )(tile, offsets, current, matrices, *data)


def update_kernel(views, core_ref, current_ref, twin_ref, other_ref, log_ref, new_ref, narrow_ref):
    total, columns = current_ref.shape
    first = core_ref[0] == 0
    row = lax.broadcasted_iota(jnp.int32, (CHUNK, columns), 0)
    column = lax.broadcasted_iota(jnp.int32, (CHUNK, columns), 1)

    def scale(z, y, x):
        return lax.rsqrt(z * z + y * y + x * x + SMOOTH_SQUARE)

    def pick(low, high, start, size):
        return jnp.where(first, low[start : start + size, :], high[start : start + size, :])

    def next_row(x, following):
        return jnp.where(row == CHUNK - 1, following, pltpu.roll(x, CHUNK - 1, 0))

    def next_column(x):
        return jnp.where(column == columns - 1, 0.0, pltpu.roll(x, columns - 1, 1))

    def edge(x):
        return x * lax.rsqrt(x * x + SMOOTH_SQUARE)

    carry = edge(current_ref[0:1, :])
    for start in range(0, total, CHUNK):
        stop = start + CHUNK
        current = current_ref[start:stop, :]
        above = pick(twin_ref, other_ref, start, CHUNK)
        below = pick(other_ref, twin_ref, start, CHUNK)
        if stop < total:
            current_next, below_next = current_ref[stop : stop + 1, :], pick(other_ref, twin_ref, stop, 1)
        else:
            current_next = below_next = jnp.zeros((1, columns), jnp.float32)
        grad_z = above - current
        grad_y = next_row(current, current_next) - current
        grad_x = next_column(current) - current
        inverse = scale(grad_z, grad_y, grad_x)
        unit_y, unit_x = grad_y * inverse, grad_x * inverse
        before_y = jnp.where(row == 0, carry, pltpu.roll(unit_y, 1, 0))
        before_x = jnp.where(column == 0, edge(current), pltpu.roll(unit_x, 1, 1))
        carry = unit_y[CHUNK - 1 : CHUNK, :]
        lower_z = current - below
        lower = lower_z * scale(lower_z, next_row(below, below_next) - below, next_column(below) - below)
        divergence = grad_z * inverse - lower + (unit_y - before_y) + (unit_x - before_x)
        damping = 1.0 - TV_WEIGHT * divergence
        new = current * jnp.exp(log_ref[start:stop, :] * (1.0 / views)) / damping
        new_ref[start:stop, :] = new
        narrow_ref[start:stop, :] = new.astype(narrow_ref.dtype)


def update(views, core, current, twin, other, logs):
    return pl.pallas_call(
        functools.partial(update_kernel, views),
        out_shape=(
            jax.ShapeDtypeStruct(current.shape, jnp.float32),
            jax.ShapeDtypeStruct(current.shape, jnp.bfloat16),
        ),
        in_specs=[SMEM] + [VMEM] * 4,
        out_specs=[VMEM] * 2,
        compiler_params=LIMIT,
        name="update",
    )(core, current, twin, other, logs)


def plane_shards(view_data, estimate, psf_taps, offsets):
    tiles, views = lax.axis_size("tiles"), lax.axis_size("views")
    square = ("tiles", "views", "gz")
    _, height, columns = estimate.shape
    blocks = offsets.shape[1]
    taps = psf_taps.shape[-1]
    tile, view, core = lax.axis_index("tiles"), lax.axis_index("views"), lax.axis_index("gz")
    straight = view == core
    swap = [(0, 1), (1, 0)]

    def device(t, v, g):
        return (t * views + v) * 2 + g

    def place(chain, t):
        return jnp.where(chain == 0, t, tiles - 1 - t)

    def over_tiles(pick):
        return [pick(tile)] + [
            lax.ppermute(pick(lax.bitwise_xor(tile, k)), "tiles", [(t, t ^ k) for t in range(tiles)])
            for k in range(1, tiles)
        ]

    me = tile.reshape(1).astype(jnp.int32)
    flag = core.reshape(1).astype(jnp.int32)
    give, give_data, keep, keep_data = split_by_core(flag, estimate, view_data[0, 0])

    chain = jnp.where(straight, keep, lax.ppermute(give, "gz", swap))
    pieces = over_tiles(lambda t: lax.dynamic_index_in_dim(chain, place(view, t), 0, keepdims=False))

    got_data = lax.ppermute(give_data, "gz", swap)
    mine = jnp.where(straight, keep_data, got_data)
    profiles = [psf_taps.reshape(-1), psf_taps[..., ::-1].reshape(-1)]
    info = jnp.concatenate([*profiles, offsets.reshape(-1).astype(jnp.float32)])
    info = jnp.pad(info, (0, columns - info.shape[0])).astype(jnp.bfloat16)
    sent = jnp.concatenate(
        [
            jnp.where(straight, got_data, keep_data).reshape(tiles * height, columns),
            jnp.broadcast_to(info, (INFO_ROWS, columns)),
        ]
    )
    came = lax.ppermute(sent, "views", swap)
    both = jnp.stack([mine, came[: tiles * height].reshape(tiles, height, columns)], axis=1)
    data = over_tiles(lambda t: lax.dynamic_index_in_dim(both, place(view, t), 0, keepdims=False))

    info = jnp.stack([info, came[tiles * height]]).astype(jnp.float32)
    shifts = info[:, 8 * taps : 8 * taps + blocks].astype(jnp.int32)
    matrices = blur_matrices(taps, height, info)

    path = [(t, 0) for t in range(tiles)] + [(t, 1) for t in reversed(range(tiles))]
    hops = []
    for here, there in zip(path[:-1], path[1:]):
        one, two = device(*here, 1), device(*there, 0)
        hops += [(one, two), (two, one)]

    current, narrow = gather_plane(me, pieces)
    current = current.reshape(tiles * height, columns)
    for _ in range(ITERS):
        other = lax.ppermute(current, square, hops)
        twin = lax.ppermute(current, "gz", swap)
        logs = correction_logs(me, shifts, narrow, matrices, data)
        current, narrow = update(views, flag, current, twin, other, logs)
        narrow = narrow.reshape(tiles, height, columns)

    result = current.astype(jnp.float16).reshape(tiles, height, columns)
    result = jnp.stack(over_tiles(lambda t: lax.dynamic_index_in_dim(result, t, 0, keepdims=False)))
    crossed = lax.ppermute(result, "views", swap)
    twin = lax.ppermute(jnp.where(straight, crossed, result), "gz", swap)
    same = jnp.where(straight, result, crossed)
    ordered = []
    for i in range(tiles):
        k = lax.bitwise_xor(place(core, i), tile)
        same_i = lax.dynamic_index_in_dim(same, k, 0, keepdims=False)
        twin_i = lax.dynamic_index_in_dim(twin, k, 0, keepdims=False)
        ordered += [jnp.where(core == 0, same_i, twin_i), jnp.where(core == 0, twin_i, same_i)]
    return jnp.stack(ordered).astype(jnp.float32)


def one_plane_each(mesh, view_data, estimate, psf_taps, offsets):
    tiles, views, depth = mesh.shape["tiles"], mesh.shape["views"], mesh.shape["gz"]
    planes = estimate.shape[0] // (mesh.shape["groups"] * depth)
    height, columns = estimate.shape[1] // tiles, estimate.shape[2]
    return (
        depth == 2
        and views == 2
        and planes == 2 * tiles
        and tiles & (tiles - 1) == 0
        and height == columns
        and height % (16 * offsets.shape[1]) == 0
        and columns == 128
        and 8 * psf_taps.shape[-1] + offsets.shape[1] <= columns
    )


def solution(mesh):
    in_specs = (
        P(("groups", "views"), "tiles", "gz", None, None),
        P(("groups", "gz"), "tiles", None),
        P("views", None, None, None),
        P("views", None),
    )
    out_specs = P(("groups", "gz"), "tiles", None)

    def step(*arrays):
        if not one_plane_each(mesh, *arrays):
            return jax.shard_map(shards, mesh=mesh, in_specs=in_specs, out_specs=out_specs, check_vma=False)(*arrays)
        body = jax.shard_map(plane_shards, mesh=mesh, in_specs=in_specs, out_specs=out_specs, check_vma=False)
        return body(*arrays)

    return step
```

```python
import functools

import jax
import jax.numpy as jnp
from jax import lax
from jax.experimental import pallas as pl
from jax.experimental.pallas import tpu as pltpu
from jax.sharding import PartitionSpec as P


ITERS = 2
CAP = 4


TV_WEIGHT = 0.1
SMOOTH_SQUARE = 0.0025


def with_halo(cells, sides, width):
    for axis, dim in sides:
        count = lax.axis_size(axis)
        ends = count - 1
        head = lax.slice_in_dim(cells, 0, width, axis=dim)
        tail = lax.slice_in_dim(cells, cells.shape[dim] - width, cells.shape[dim], axis=dim)
        cells = jnp.concatenate(
            [
                lax.ppermute(tail, axis, [(i, (i + 1) % count) for i in range(ends)]),
                cells,
                lax.ppermute(head, axis, [((i + 1) % count, i) for i in range(ends)]),
            ],
            axis=dim,
        )
    return cells


def toeplitz_matrix(profile, length):
    half_width = (profile.shape[0] - 1) // 2
    position = jnp.arange(length, dtype=jnp.int32)
    offset = position[None, :] - position[:, None] + half_width
    tap_index = jnp.arange(profile.shape[0], dtype=jnp.int32)
    picked = (offset[:, :, None] == tap_index[None, None, :]).astype(jnp.float32)
    return jnp.sum(picked * profile[None, None, :], axis=2).astype(jnp.bfloat16)


def curvature(padded):
    anchor = padded[:-1, :-1, :-1]
    grad_z = padded[1:, :-1, :-1] - anchor
    grad_y = padded[:-1, 1:, :-1] - anchor
    grad_x = padded[:-1, :-1, 1:] - anchor
    magnitude = jnp.sqrt(grad_z * grad_z + grad_y * grad_y + grad_x * grad_x + SMOOTH_SQUARE)
    unit_z = grad_z / magnitude
    unit_y = grad_y / magnitude
    unit_x = grad_x / magnitude
    return (
        unit_z[1:, 1:, 1:]
        - unit_z[:-1, 1:, 1:]
        + (unit_y[1:, 1:, 1:] - unit_y[1:, :-1, 1:])
        + (unit_x[1:, 1:, 1:] - unit_x[1:, 1:, :-1])
    )


def view_correction(view_tile, observed, kernel_y, kernel_x):
    blurred = jnp.zeros(view_tile.shape, jnp.float32)
    for term_index in range(2):
        half_blur = jnp.einsum(
            "yk,zkx->zyx", kernel_y[term_index], view_tile, preferred_element_type=jnp.float32
        ).astype(jnp.bfloat16)
        blurred = blurred + jnp.einsum(
            "zyk,xk->zyx", half_blur, kernel_x[term_index], preferred_element_type=jnp.float32
        )
    quotient = (observed.astype(jnp.float32) / blurred).astype(jnp.bfloat16)
    log_sum = jnp.zeros(view_tile.shape, jnp.float32)
    for term_index in range(2):
        half_back = jnp.einsum(
            "ky,zkx->zyx", kernel_y[term_index], quotient, preferred_element_type=jnp.float32
        ).astype(jnp.bfloat16)
        log_sum = log_sum + jnp.einsum(
            "zyk,kx->zyx", half_back, kernel_x[term_index], preferred_element_type=jnp.float32
        )
    return log_sum.astype(jnp.bfloat16)


def shards(view_data, estimate, psf_taps, offsets):
    owners = lax.axis_size("tiles")
    view_count = lax.axis_size("views")
    observed = view_data[0, 0]
    planes, height, columns = estimate.shape
    view_shift = offsets[0]
    blocks = view_shift.shape[0]
    block_rows = height // blocks
    slot_count = owners * CAP
    kernel_y = jnp.stack(
        [toeplitz_matrix(psf_taps[0, term_index, 0], height) for term_index in range(2)]
    )
    kernel_x = jnp.stack(
        [toeplitz_matrix(psf_taps[0, term_index, 1], columns) for term_index in range(2)]
    )
    position = jnp.arange(blocks, dtype=jnp.int32)
    same_owner = view_shift[:, None] == view_shift[None, :]
    before = position[None, :] < position[:, None]
    slot_rank = jnp.sum((same_owner & before).astype(jnp.int32), axis=1)
    member = lax.axis_index("tiles")
    target = (member + view_shift) % owners
    source_tile = (member - view_shift) % owners
    slot_index = jnp.arange(slot_count, dtype=jnp.int32)
    to_owner = ((target * CAP + slot_rank)[:, None] == slot_index[None, :]).astype(jnp.bfloat16)
    from_tile = ((source_tile * CAP + slot_rank)[:, None] == slot_index[None, :]).astype(
        jnp.bfloat16
    )
    current = estimate
    for _ in range(ITERS):
        padded = with_halo(current, (("tiles", 1), ("gz", 0)), 1)
        padded = jnp.pad(padded, ((0, 0), (0, 0), (1, 1)))
        owned_blocks = current.astype(jnp.bfloat16).reshape(planes, blocks, block_rows, columns)
        outgoing = jnp.einsum(
            "sk,zsrx->kzrx", from_tile, owned_blocks, preferred_element_type=jnp.float32
        ).astype(jnp.bfloat16)
        incoming = lax.all_to_all(
            outgoing.reshape(owners, CAP, planes, block_rows, columns),
            "tiles",
            split_axis=0,
            concat_axis=0,
            tiled=True,
        )
        view_tile = jnp.einsum(
            "sk,kzrx->zsrx",
            to_owner,
            incoming.reshape(slot_count, planes, block_rows, columns),
            preferred_element_type=jnp.float32,
        ).astype(jnp.bfloat16)
        view_tile = view_tile.reshape(planes, height, columns)
        correction = view_correction(view_tile, observed, kernel_y, kernel_x)
        correction = correction.reshape(planes, blocks, block_rows, columns)
        returned = jnp.einsum(
            "sk,zsrx->kzrx", to_owner, correction, preferred_element_type=jnp.float32
        ).astype(jnp.bfloat16)
        gathered = lax.all_to_all(
            returned.reshape(owners, CAP, planes, block_rows, columns),
            "tiles",
            split_axis=0,
            concat_axis=0,
            tiled=True,
        )
        owned_rows = jnp.einsum(
            "sk,kzrx->zsrx",
            from_tile,
            gathered.reshape(slot_count, planes, block_rows, columns),
            preferred_element_type=jnp.float32,
        ).reshape(planes, height, columns)
        log_values = jnp.log(owned_rows)
        share_rows = height // view_count
        log_part = lax.psum_scatter(log_values, "views", scatter_dimension=1, tiled=True)
        first_row = lax.axis_index("views") * share_rows
        window = lax.dynamic_slice_in_dim(padded, first_row, share_rows + 2, 1)
        damping = 1.0 - TV_WEIGHT * curvature(window)
        rows_now = lax.dynamic_slice_in_dim(current, first_row, share_rows, 1)
        updated = rows_now * jnp.exp(log_part / view_count) / damping
        current = lax.all_gather(updated, "views", axis=1, tiled=True)
    return current


INFO_ROWS = 16
CHUNK = 32
VMEM = pl.BlockSpec(memory_space=pltpu.VMEM)
SMEM = pl.BlockSpec(memory_space=pltpu.SMEM)
LIMIT = pltpu.CompilerParams(vmem_limit_bytes=16 * 2**20)


def matrices_kernel(taps, info_ref, out_ref):
    views, columns = info_ref.shape
    length = out_ref.shape[-2] // 2
    half_width = (taps - 1) // 2
    row = lax.broadcasted_iota(jnp.int32, (length, columns), 0)
    column = lax.broadcasted_iota(jnp.int32, (length, columns), 1)
    band = jnp.abs(row - column) <= half_width
    for v in range(views):
        profile = jnp.broadcast_to(info_ref[v : v + 1, :], (8, columns))
        for kind, (flipped, axis) in enumerate([(0, 0), (1, 1), (1, 0), (0, 1)]):
            for r in range(2):
                lane = (4 * flipped + 2 * r + axis) * taps + half_width
                spread = jnp.broadcast_to(pltpu.roll(profile, columns - lane, 1)[0:1], (length, columns))
                rolled = pltpu.roll(spread, 0, 1, stride=1, stride_axis=0)
                rolled = jnp.where(band, rolled, 0.0).astype(out_ref.dtype)
                out_ref[v, kind, r * length : (r + 1) * length, :] = rolled


def blur_matrices(taps, length, info):
    views, columns = info.shape
    return pl.pallas_call(
        functools.partial(matrices_kernel, taps),
        out_shape=jax.ShapeDtypeStruct((views, 4, 2 * length, columns), jnp.bfloat16),
        in_specs=[VMEM],
        out_specs=VMEM,
        compiler_params=LIMIT,
        name="blur_matrices",
    )(info)


def correction_kernel(tiles, tile_ref, offsets_ref, current_ref, matrices_ref, *refs):
    views, blocks = offsets_ref.shape
    data, log_ref, work = refs[: views * tiles], refs[views * tiles], refs[views * tiles + 1 :]
    height, columns = data[0].shape
    rows = height // blocks
    me = tile_ref[0]
    shift = [[offsets_ref[w, s] for s in range(blocks)] for w in range(views)]
    planes = [work[3 * w] for w in range(views)]
    halves = [work[3 * w + 1] for w in range(views)]
    logs = [work[3 * w + 2] for w in range(views)]

    def first(w, kind):
        half = jnp.dot(matrices_ref[w, kind], planes[w][...], preferred_element_type=jnp.float32)
        half = half.astype(jnp.bfloat16)
        for k in range(tiles):
            for r in range(2):
                halves[w][k * height : (k + 1) * height, r * columns : (r + 1) * columns] = half[
                    r * height : (r + 1) * height, k * columns : (k + 1) * columns
                ]

    for w in range(views):
        for k in range(tiles):
            tile = lax.bitwise_xor(me, k)
            for s in range(blocks):
                owner = lax.rem(tile + shift[w][s], tiles)
                planes[w][s * rows : (s + 1) * rows, k * columns : (k + 1) * columns] = current_ref[
                    owner, s * rows : (s + 1) * rows, :
                ]
    for w in range(views):
        first(w, 0)
    for w in range(views):
        blurred = jnp.dot(halves[w][...], matrices_ref[w, 1], preferred_element_type=jnp.float32)
        for k in range(tiles):
            quotient = data[w * tiles + k][...].astype(jnp.float32) / blurred[k * height : (k + 1) * height]
            planes[w][:, k * columns : (k + 1) * columns] = quotient.astype(jnp.bfloat16)
    for w in range(views):
        first(w, 2)
    for w in range(views):
        back = jnp.dot(halves[w][...], matrices_ref[w, 3], preferred_element_type=jnp.float32)
        logs[w][...] = jnp.log(back.astype(jnp.bfloat16).astype(jnp.float32))
    for o in range(tiles):
        for s in range(blocks):
            total = None
            for w in range(views):
                tile = lax.rem(o - shift[w][s] + tiles, tiles)
                start = pl.multiple_of(lax.bitwise_xor(tile, me) * height + s * rows, rows)
                part = logs[w][pl.ds(start, rows), :]
                total = part if total is None else total + part
            log_ref[o * height + s * rows : o * height + (s + 1) * rows, :] = total


def correction_logs(tile, offsets, current, matrices, data):
    tiles, height, columns = current.shape
    scratch = [
        pltpu.VMEM((height, tiles * columns), jnp.bfloat16),
        pltpu.VMEM((tiles * height, 2 * columns), jnp.bfloat16),
        pltpu.VMEM((tiles * height, columns), jnp.float32),
    ]
    return pl.pallas_call(
        functools.partial(correction_kernel, tiles),
        out_shape=jax.ShapeDtypeStruct((tiles * height, columns), jnp.float32),
        in_specs=[SMEM, SMEM] + [VMEM] * (2 + len(data)),
        out_specs=VMEM,
        scratch_shapes=scratch * offsets.shape[0],
        cost_estimate=pl.CostEstimate(flops=300_000_000, bytes_accessed=1_500_000, transcendentals=0),
        compiler_params=LIMIT,
        name="correction",
    )(tile, offsets, current, matrices, *data)


def update_kernel(views, core_ref, current_ref, twin_ref, other_ref, log_ref, *new_refs):
    total, columns = current_ref.shape
    first = core_ref[0] == 0
    row = lax.broadcasted_iota(jnp.int32, (CHUNK, columns), 0)
    column = lax.broadcasted_iota(jnp.int32, (CHUNK, columns), 1)

    def scale(z, y, x):
        return lax.rsqrt(z * z + y * y + x * x + SMOOTH_SQUARE)

    def pick(low, high, start, size):
        return jnp.where(first, low[start : start + size, :], high[start : start + size, :])

    def next_row(x, following):
        return jnp.where(row == CHUNK - 1, following, pltpu.roll(x, CHUNK - 1, 0))

    def next_column(x):
        return jnp.where(column == columns - 1, 0.0, pltpu.roll(x, columns - 1, 1))

    def edge(x):
        return x * lax.rsqrt(x * x + SMOOTH_SQUARE)

    carry = edge(current_ref[0:1, :])
    for start in range(0, total, CHUNK):
        stop = start + CHUNK
        current = current_ref[start:stop, :]
        above = pick(twin_ref, other_ref, start, CHUNK)
        below = pick(other_ref, twin_ref, start, CHUNK)
        if stop < total:
            current_next, below_next = current_ref[stop : stop + 1, :], pick(other_ref, twin_ref, stop, 1)
        else:
            current_next = below_next = jnp.zeros((1, columns), jnp.float32)
        grad_z = above - current
        grad_y = next_row(current, current_next) - current
        grad_x = next_column(current) - current
        inverse = scale(grad_z, grad_y, grad_x)
        unit_y, unit_x = grad_y * inverse, grad_x * inverse
        before_y = jnp.where(row == 0, carry, pltpu.roll(unit_y, 1, 0))
        before_x = jnp.where(column == 0, edge(current), pltpu.roll(unit_x, 1, 1))
        carry = unit_y[CHUNK - 1 : CHUNK, :]
        lower_z = current - below
        lower = lower_z * scale(lower_z, next_row(below, below_next) - below, next_column(below) - below)
        divergence = grad_z * inverse - lower + (unit_y - before_y) + (unit_x - before_x)
        damping = 1.0 - TV_WEIGHT * divergence
        new = current * jnp.exp(log_ref[start:stop, :] * (1.0 / views)) / damping
        for ref in new_refs:
            ref[start:stop, :] = new.astype(ref.dtype)


def update(views, core, current, twin, other, logs, dtypes):
    return pl.pallas_call(
        functools.partial(update_kernel, views),
        out_shape=[jax.ShapeDtypeStruct(current.shape, dtype) for dtype in dtypes],
        in_specs=[SMEM] + [VMEM] * 4,
        out_specs=[VMEM] * len(dtypes),
        compiler_params=LIMIT,
        name="update",
    )(core, current, twin, other, logs)


def plane_shards(view_data, estimate, psf_taps, offsets):
    tiles, views = lax.axis_size("tiles"), lax.axis_size("views")
    square = ("tiles", "views", "gz")
    _, height, columns = estimate.shape
    blocks = offsets.shape[1]
    taps = psf_taps.shape[-1]
    tile, view, core = lax.axis_index("tiles"), lax.axis_index("views"), lax.axis_index("gz")
    straight = view == core
    swap = [(0, 1), (1, 0)]

    def device(t, v, g):
        return (t * views + v) * 2 + g

    def place(chain, t):
        return jnp.where(chain == 0, t, tiles - 1 - t)

    def over_tiles(pick):
        pieces = [pick(tile)]
        for k in range(1, tiles):
            pieces.append(
                lax.ppermute(pick(lax.bitwise_xor(tile, k)), "tiles", [(t, t ^ k) for t in range(tiles)])
            )
        return pieces

    me = tile.reshape(1).astype(jnp.int32)
    flag = core.reshape(1).astype(jnp.int32)

    def coded(parity):
        planes, data = (
            lax.dynamic_index_in_dim(x.reshape(tiles, 2, height, columns), parity, 1, keepdims=False)
            for x in (estimate, view_data)
        )
        return jnp.stack([(planes - 1.0).astype(jnp.float16), data.astype(jnp.float16)])

    keep = coded(core)
    got = lax.ppermute(coded(1 - core), "gz", swap)
    mine = jnp.where(straight, keep, got)
    profiles = [psf_taps.reshape(-1), psf_taps[..., ::-1].reshape(-1)]
    info = jnp.concatenate([*profiles, offsets.reshape(-1).astype(jnp.float32)])
    info = jnp.pad(info, (0, columns - info.shape[0])).astype(jnp.bfloat16).astype(jnp.float16)
    sent = jnp.concatenate(
        [
            jnp.where(straight, got[1], keep[1]).reshape(tiles * height, columns),
            jnp.broadcast_to(info, (INFO_ROWS, columns)),
        ]
    )
    came = lax.ppermute(sent, "views", swap)
    theirs = came[: tiles * height].reshape(tiles, height, columns)
    pieces = over_tiles(lambda t: lax.dynamic_index_in_dim(mine, place(view, t), 1, keepdims=False))
    others = over_tiles(lambda t: lax.dynamic_index_in_dim(theirs, place(view, t), 0, keepdims=False))
    data = [piece[1].astype(jnp.bfloat16) for piece in pieces] + [x.astype(jnp.bfloat16) for x in others]

    info = jnp.stack([info, came[tiles * height]]).astype(jnp.float32)
    shifts = info[:, 8 * taps : 8 * taps + blocks].astype(jnp.int32)
    matrices = blur_matrices(taps, height, info)

    path = [(t, 0) for t in range(tiles)] + [(t, 1) for t in reversed(range(tiles))]
    hops = []
    for here, there in zip(path[:-1], path[1:]):
        one, two = device(*here, 1), device(*there, 0)
        hops += [(one, two), (two, one)]

    def owned_by(o):
        chosen = pieces[o][0]
        for t in range(1, tiles):
            chosen = jnp.where(tile == t, pieces[o ^ t][0], chosen)
        return chosen

    plane = jnp.concatenate([owned_by(o) for o in range(tiles)])
    current = plane.astype(jnp.float32) + 1.0
    narrow = current.astype(jnp.bfloat16)
    at_end = jnp.where(view == 0, (tile == 0) & (core == 0), (tile == 0) & (core == 1))
    for iteration in range(ITERS):
        last = iteration == ITERS - 1
        other = lax.ppermute(plane, square, hops)
        twin = lax.ppermute(plane, "gz", swap)
        other = jnp.where(at_end, 0.0, other.astype(jnp.float32) + 1.0)
        twin = twin.astype(jnp.float32) + 1.0
        logs = correction_logs(me, shifts, narrow.reshape(tiles, height, columns), matrices, data)
        current, *rest = update(
            views, flag, current, twin, other, logs, [jnp.float32] if last else [jnp.float32, jnp.bfloat16]
        )
        if not last:
            narrow = rest[0]
            plane = (current - 1.0).astype(jnp.float16)

    result = current.astype(jnp.float16).reshape(tiles, height, columns)
    result = jnp.stack(over_tiles(lambda t: lax.dynamic_index_in_dim(result, t, 0, keepdims=False)))
    turn, across = [], []
    for t in range(tiles):
        for v in range(2):
            turn += [(device(t, v, 1 - v), device(t, v, v)), (device(t, v, v), device(t, 1 - v, v))]
            across += [(device(t, v, 1 - v), device(t, 1 - v, v))]
    turned = lax.ppermute(result, square, turn)
    crossed = lax.ppermute(result, square, across)
    same = jnp.where(straight, result, turned)
    twin = jnp.where(straight, turned, crossed)
    ordered = []
    for i in range(tiles):
        k = lax.bitwise_xor(place(core, i), tile)
        same_i = lax.dynamic_index_in_dim(same, k, 0, keepdims=False)
        twin_i = lax.dynamic_index_in_dim(twin, k, 0, keepdims=False)
        ordered += [jnp.where(core == 0, same_i, twin_i), jnp.where(core == 0, twin_i, same_i)]
    return jnp.stack(ordered).astype(jnp.float32)


def one_plane_each(mesh, view_data, estimate, psf_taps, offsets):
    tiles, views, depth = mesh.shape["tiles"], mesh.shape["views"], mesh.shape["gz"]
    planes = estimate.shape[0] // (mesh.shape["groups"] * depth)
    height, columns = estimate.shape[1] // tiles, estimate.shape[2]
    return (
        depth == 2
        and views == 2
        and planes == 2 * tiles
        and tiles & (tiles - 1) == 0
        and height == columns
        and height % (16 * offsets.shape[1]) == 0
        and columns == 128
        and 8 * psf_taps.shape[-1] + offsets.shape[1] <= columns
    )


def solution(mesh):
    in_specs = (
        P(("groups", "views"), "tiles", "gz", None, None),
        P(("groups", "gz"), "tiles", None),
        P("views", None, None, None),
        P("views", None),
    )
    out_specs = P(("groups", "gz"), "tiles", None)

    def step(*arrays):
        if not one_plane_each(mesh, *arrays):
            return jax.shard_map(shards, mesh=mesh, in_specs=in_specs, out_specs=out_specs, check_vma=False)(*arrays)
        body = jax.shard_map(plane_shards, mesh=mesh, in_specs=in_specs, out_specs=out_specs, check_vma=False)
        return body(*arrays)

    return step
```

```python
import functools

import jax
import jax.numpy as jnp
from jax import lax
from jax.experimental import pallas as pl
from jax.experimental.pallas import tpu as pltpu
from jax.sharding import PartitionSpec as P


ITERS = 2
CAP = 4


TV_WEIGHT = 0.1
SMOOTH_SQUARE = 0.0025


def with_halo(cells, sides, width):
    for axis, dim in sides:
        count = lax.axis_size(axis)
        ends = count - 1
        head = lax.slice_in_dim(cells, 0, width, axis=dim)
        tail = lax.slice_in_dim(cells, cells.shape[dim] - width, cells.shape[dim], axis=dim)
        cells = jnp.concatenate(
            [
                lax.ppermute(tail, axis, [(i, (i + 1) % count) for i in range(ends)]),
                cells,
                lax.ppermute(head, axis, [((i + 1) % count, i) for i in range(ends)]),
            ],
            axis=dim,
        )
    return cells


def toeplitz_matrix(profile, length):
    half_width = (profile.shape[0] - 1) // 2
    position = jnp.arange(length, dtype=jnp.int32)
    offset = position[None, :] - position[:, None] + half_width
    tap_index = jnp.arange(profile.shape[0], dtype=jnp.int32)
    picked = (offset[:, :, None] == tap_index[None, None, :]).astype(jnp.float32)
    return jnp.sum(picked * profile[None, None, :], axis=2).astype(jnp.bfloat16)


def curvature(padded):
    anchor = padded[:-1, :-1, :-1]
    grad_z = padded[1:, :-1, :-1] - anchor
    grad_y = padded[:-1, 1:, :-1] - anchor
    grad_x = padded[:-1, :-1, 1:] - anchor
    magnitude = jnp.sqrt(grad_z * grad_z + grad_y * grad_y + grad_x * grad_x + SMOOTH_SQUARE)
    unit_z = grad_z / magnitude
    unit_y = grad_y / magnitude
    unit_x = grad_x / magnitude
    return (
        unit_z[1:, 1:, 1:]
        - unit_z[:-1, 1:, 1:]
        + (unit_y[1:, 1:, 1:] - unit_y[1:, :-1, 1:])
        + (unit_x[1:, 1:, 1:] - unit_x[1:, 1:, :-1])
    )


def view_correction(view_tile, observed, kernel_y, kernel_x):
    blurred = jnp.zeros(view_tile.shape, jnp.float32)
    for term_index in range(2):
        half_blur = jnp.einsum(
            "yk,zkx->zyx", kernel_y[term_index], view_tile, preferred_element_type=jnp.float32
        ).astype(jnp.bfloat16)
        blurred = blurred + jnp.einsum(
            "zyk,xk->zyx", half_blur, kernel_x[term_index], preferred_element_type=jnp.float32
        )
    quotient = (observed.astype(jnp.float32) / blurred).astype(jnp.bfloat16)
    log_sum = jnp.zeros(view_tile.shape, jnp.float32)
    for term_index in range(2):
        half_back = jnp.einsum(
            "ky,zkx->zyx", kernel_y[term_index], quotient, preferred_element_type=jnp.float32
        ).astype(jnp.bfloat16)
        log_sum = log_sum + jnp.einsum(
            "zyk,kx->zyx", half_back, kernel_x[term_index], preferred_element_type=jnp.float32
        )
    return log_sum.astype(jnp.bfloat16)


def shards(view_data, estimate, psf_taps, offsets):
    owners = lax.axis_size("tiles")
    view_count = lax.axis_size("views")
    observed = view_data[0, 0]
    planes, height, columns = estimate.shape
    view_shift = offsets[0]
    blocks = view_shift.shape[0]
    block_rows = height // blocks
    slot_count = owners * CAP
    kernel_y = jnp.stack(
        [toeplitz_matrix(psf_taps[0, term_index, 0], height) for term_index in range(2)]
    )
    kernel_x = jnp.stack(
        [toeplitz_matrix(psf_taps[0, term_index, 1], columns) for term_index in range(2)]
    )
    position = jnp.arange(blocks, dtype=jnp.int32)
    same_owner = view_shift[:, None] == view_shift[None, :]
    before = position[None, :] < position[:, None]
    slot_rank = jnp.sum((same_owner & before).astype(jnp.int32), axis=1)
    member = lax.axis_index("tiles")
    target = (member + view_shift) % owners
    source_tile = (member - view_shift) % owners
    slot_index = jnp.arange(slot_count, dtype=jnp.int32)
    to_owner = ((target * CAP + slot_rank)[:, None] == slot_index[None, :]).astype(jnp.bfloat16)
    from_tile = ((source_tile * CAP + slot_rank)[:, None] == slot_index[None, :]).astype(
        jnp.bfloat16
    )
    current = estimate
    for _ in range(ITERS):
        padded = with_halo(current, (("tiles", 1), ("gz", 0)), 1)
        padded = jnp.pad(padded, ((0, 0), (0, 0), (1, 1)))
        owned_blocks = current.astype(jnp.bfloat16).reshape(planes, blocks, block_rows, columns)
        outgoing = jnp.einsum(
            "sk,zsrx->kzrx", from_tile, owned_blocks, preferred_element_type=jnp.float32
        ).astype(jnp.bfloat16)
        incoming = lax.all_to_all(
            outgoing.reshape(owners, CAP, planes, block_rows, columns),
            "tiles",
            split_axis=0,
            concat_axis=0,
            tiled=True,
        )
        view_tile = jnp.einsum(
            "sk,kzrx->zsrx",
            to_owner,
            incoming.reshape(slot_count, planes, block_rows, columns),
            preferred_element_type=jnp.float32,
        ).astype(jnp.bfloat16)
        view_tile = view_tile.reshape(planes, height, columns)
        correction = view_correction(view_tile, observed, kernel_y, kernel_x)
        correction = correction.reshape(planes, blocks, block_rows, columns)
        returned = jnp.einsum(
            "sk,zsrx->kzrx", to_owner, correction, preferred_element_type=jnp.float32
        ).astype(jnp.bfloat16)
        gathered = lax.all_to_all(
            returned.reshape(owners, CAP, planes, block_rows, columns),
            "tiles",
            split_axis=0,
            concat_axis=0,
            tiled=True,
        )
        owned_rows = jnp.einsum(
            "sk,kzrx->zsrx",
            from_tile,
            gathered.reshape(slot_count, planes, block_rows, columns),
            preferred_element_type=jnp.float32,
        ).reshape(planes, height, columns)
        log_values = jnp.log(owned_rows)
        share_rows = height // view_count
        log_part = lax.psum_scatter(log_values, "views", scatter_dimension=1, tiled=True)
        first_row = lax.axis_index("views") * share_rows
        window = lax.dynamic_slice_in_dim(padded, first_row, share_rows + 2, 1)
        damping = 1.0 - TV_WEIGHT * curvature(window)
        rows_now = lax.dynamic_slice_in_dim(current, first_row, share_rows, 1)
        updated = rows_now * jnp.exp(log_part / view_count) / damping
        current = lax.all_gather(updated, "views", axis=1, tiled=True)
    return current


INFO_ROWS = 16
PLANE_UNIT = 65534.0
DATA_UNIT = 1024.0
TAP_UNIT = 8192.0
CHUNK = 32
VMEM = pl.BlockSpec(memory_space=pltpu.VMEM)
SMEM = pl.BlockSpec(memory_space=pltpu.SMEM)
LIMIT = pltpu.CompilerParams(vmem_limit_bytes=16 * 2**20)


def matrices_kernel(taps, info_ref, out_ref):
    views, columns = info_ref.shape
    length = out_ref.shape[-2] // 2
    half_width = (taps - 1) // 2
    row = lax.broadcasted_iota(jnp.int32, (length, columns), 0)
    column = lax.broadcasted_iota(jnp.int32, (length, columns), 1)
    band = jnp.abs(row - column) <= half_width
    for v in range(views):
        profile = jnp.broadcast_to(info_ref[v : v + 1, :], (8, columns))
        for kind, (flipped, axis) in enumerate([(0, 0), (1, 1), (1, 0), (0, 1)]):
            for r in range(2):
                lane = (4 * flipped + 2 * r + axis) * taps + half_width
                spread = jnp.broadcast_to(pltpu.roll(profile, columns - lane, 1)[0:1], (length, columns))
                rolled = pltpu.roll(spread, 0, 1, stride=1, stride_axis=0)
                rolled = jnp.where(band, rolled, 0.0).astype(out_ref.dtype)
                out_ref[v, kind, r * length : (r + 1) * length, :] = rolled


def blur_matrices(taps, length, info):
    views, columns = info.shape
    return pl.pallas_call(
        functools.partial(matrices_kernel, taps),
        out_shape=jax.ShapeDtypeStruct((views, 4, 2 * length, columns), jnp.bfloat16),
        in_specs=[VMEM],
        out_specs=VMEM,
        compiler_params=LIMIT,
        name="blur_matrices",
    )(info)


def correction_kernel(tiles, tile_ref, offsets_ref, current_ref, matrices_ref, *refs):
    views, blocks = offsets_ref.shape
    data, log_ref, work = refs[: views * tiles], refs[views * tiles], refs[views * tiles + 1 :]
    height, columns = data[0].shape
    rows = height // blocks
    me = tile_ref[0]
    shift = [[offsets_ref[w, s] for s in range(blocks)] for w in range(views)]
    planes = [work[3 * w] for w in range(views)]
    halves = [work[3 * w + 1] for w in range(views)]
    logs = [work[3 * w + 2] for w in range(views)]

    def first(w, kind):
        half = jnp.dot(matrices_ref[w, kind], planes[w][...], preferred_element_type=jnp.float32)
        half = half.astype(jnp.bfloat16)
        for k in range(tiles):
            for r in range(2):
                halves[w][k * height : (k + 1) * height, r * columns : (r + 1) * columns] = half[
                    r * height : (r + 1) * height, k * columns : (k + 1) * columns
                ]

    for w in range(views):
        for k in range(tiles):
            tile = lax.bitwise_xor(me, k)
            for s in range(blocks):
                owner = lax.rem(tile + shift[w][s], tiles)
                planes[w][s * rows : (s + 1) * rows, k * columns : (k + 1) * columns] = current_ref[
                    owner, s * rows : (s + 1) * rows, :
                ]
    for w in range(views):
        first(w, 0)
    for w in range(views):
        blurred = jnp.dot(halves[w][...], matrices_ref[w, 1], preferred_element_type=jnp.float32)
        for k in range(tiles):
            quotient = data[w * tiles + k][...].astype(jnp.float32) / blurred[k * height : (k + 1) * height]
            planes[w][:, k * columns : (k + 1) * columns] = quotient.astype(jnp.bfloat16)
    for w in range(views):
        first(w, 2)
    for w in range(views):
        back = jnp.dot(halves[w][...], matrices_ref[w, 3], preferred_element_type=jnp.float32)
        logs[w][...] = jnp.log(back.astype(jnp.bfloat16).astype(jnp.float32))
    for o in range(tiles):
        for s in range(blocks):
            total = None
            for w in range(views):
                tile = lax.rem(o - shift[w][s] + tiles, tiles)
                start = pl.multiple_of(lax.bitwise_xor(tile, me) * height + s * rows, rows)
                part = logs[w][pl.ds(start, rows), :]
                total = part if total is None else total + part
            log_ref[o * height + s * rows : o * height + (s + 1) * rows, :] = total


def correction_logs(tile, offsets, current, matrices, data):
    tiles, height, columns = current.shape
    scratch = [
        pltpu.VMEM((height, tiles * columns), jnp.bfloat16),
        pltpu.VMEM((tiles * height, 2 * columns), jnp.bfloat16),
        pltpu.VMEM((tiles * height, columns), jnp.float32),
    ]
    return pl.pallas_call(
        functools.partial(correction_kernel, tiles),
        out_shape=jax.ShapeDtypeStruct((tiles * height, columns), jnp.float32),
        in_specs=[SMEM, SMEM] + [VMEM] * (2 + len(data)),
        out_specs=VMEM,
        scratch_shapes=scratch * offsets.shape[0],
        cost_estimate=pl.CostEstimate(flops=300_000_000, bytes_accessed=1_500_000, transcendentals=0),
        compiler_params=LIMIT,
        name="correction",
    )(tile, offsets, current, matrices, *data)


def update_kernel(views, core_ref, current_ref, twin_ref, other_ref, log_ref, *new_refs):
    total, columns = current_ref.shape
    first = core_ref[0] == 0
    row = lax.broadcasted_iota(jnp.int32, (CHUNK, columns), 0)
    column = lax.broadcasted_iota(jnp.int32, (CHUNK, columns), 1)

    def scale(z, y, x):
        return lax.rsqrt(z * z + y * y + x * x + SMOOTH_SQUARE)

    def pick(low, high, start, size):
        return jnp.where(first, low[start : start + size, :], high[start : start + size, :])

    def next_row(x, following):
        return jnp.where(row == CHUNK - 1, following, pltpu.roll(x, CHUNK - 1, 0))

    def next_column(x):
        return jnp.where(column == columns - 1, 0.0, pltpu.roll(x, columns - 1, 1))

    def edge(x):
        return x * lax.rsqrt(x * x + SMOOTH_SQUARE)

    carry = edge(current_ref[0:1, :])
    for start in range(0, total, CHUNK):
        stop = start + CHUNK
        current = current_ref[start:stop, :]
        above = pick(twin_ref, other_ref, start, CHUNK)
        below = pick(other_ref, twin_ref, start, CHUNK)
        if stop < total:
            current_next, below_next = current_ref[stop : stop + 1, :], pick(other_ref, twin_ref, stop, 1)
        else:
            current_next = below_next = jnp.zeros((1, columns), jnp.float32)
        grad_z = above - current
        grad_y = next_row(current, current_next) - current
        grad_x = next_column(current) - current
        inverse = scale(grad_z, grad_y, grad_x)
        unit_y, unit_x = grad_y * inverse, grad_x * inverse
        before_y = jnp.where(row == 0, carry, pltpu.roll(unit_y, 1, 0))
        before_x = jnp.where(column == 0, edge(current), pltpu.roll(unit_x, 1, 1))
        carry = unit_y[CHUNK - 1 : CHUNK, :]
        lower_z = current - below
        lower = lower_z * scale(lower_z, next_row(below, below_next) - below, next_column(below) - below)
        divergence = grad_z * inverse - lower + (unit_y - before_y) + (unit_x - before_x)
        damping = 1.0 - TV_WEIGHT * divergence
        new = current * jnp.exp(log_ref[start:stop, :] * (1.0 / views)) / damping
        for ref in new_refs:
            ref[start:stop, :] = new.astype(ref.dtype)


def update(views, core, current, twin, other, logs, dtypes):
    return pl.pallas_call(
        functools.partial(update_kernel, views),
        out_shape=[jax.ShapeDtypeStruct(current.shape, dtype) for dtype in dtypes],
        in_specs=[SMEM] + [VMEM] * 4,
        out_specs=[VMEM] * len(dtypes),
        compiler_params=LIMIT,
        name="update",
    )(core, current, twin, other, logs)


def plane_shards(view_data, estimate, psf_taps, offsets):
    tiles, views = lax.axis_size("tiles"), lax.axis_size("views")
    square = ("tiles", "views", "gz")
    planes, height, columns = estimate.shape
    blocks = offsets.shape[1]
    taps = psf_taps.shape[-1]
    tile, view, core = lax.axis_index("tiles"), lax.axis_index("views"), lax.axis_index("gz")
    swap = [(0, 1), (1, 0)]

    def device(t, v, g):
        return (t * views + v) * 2 + g

    def ordered(pieces, shift):
        placed = []
        for i in range(tiles):
            chosen = pieces[i]
            for s in range(1, tiles):
                chosen = jnp.where(shift == s, pieces[i ^ s], chosen)
            placed.append(chosen)
        return placed

    def exchange(pick):
        pieces = []
        for k in range(tiles):
            pairs = [(device(t, v, g), device(t ^ k, g, v)) for t in range(tiles) for v in range(2) for g in range(2)]
            pieces.append(lax.ppermute(pick(lax.bitwise_xor(tile, k)), square, pairs))
        return pieces

    def end_of(chain):
        return jnp.where(chain == 0, 0, tiles - 1)

    me = tile.reshape(1).astype(jnp.int32)
    flag = core.reshape(1).astype(jnp.int32)
    profiles = [psf_taps.reshape(-1), psf_taps[..., ::-1].reshape(-1)]
    info = [lax.reduce_precision(p, 8, 7) * TAP_UNIT for p in profiles]
    info = jnp.concatenate([*info, offsets.reshape(-1).astype(jnp.float32)])
    info = jnp.pad(info, (0, columns - info.shape[0])).astype(jnp.int16)

    wide = estimate.reshape(tiles, 2, height, columns)
    wide = lax.dynamic_index_in_dim(wide, view, 1, keepdims=True)
    wide = jnp.round((wide - 1.0) * PLANE_UNIT).astype(jnp.int16)
    data = view_data.reshape(tiles, 2, height, columns).astype(jnp.float32)
    data = (data * DATA_UNIT).astype(jnp.int16)
    payload = jnp.concatenate([wide, data], axis=1).reshape(tiles, 3 * height, columns)
    note = jnp.broadcast_to(info, (tiles, INFO_ROWS, columns))
    payload = jnp.concatenate([payload, note], axis=1)

    def for_tile(t):
        return lax.dynamic_index_in_dim(payload, lax.bitwise_xor(t, end_of(core)), 0, keepdims=False)

    pieces = exchange(for_tile)
    planes = [piece[:height] for piece in pieces]
    pairs = [piece[height : 3 * height].reshape(2, height, columns) for piece in pieces]
    keep = [lax.dynamic_index_in_dim(pair, core, 0, keepdims=False) for pair in pairs]
    give = [lax.dynamic_index_in_dim(pair, 1 - core, 0, keepdims=False) for pair in pairs]
    note = pieces[0][3 * height :]
    got = lax.ppermute(jnp.concatenate([*planes, *give, note]), "gz", swap)
    length = tiles * height
    twin = got[:length].reshape(tiles, height, columns)
    take = got[length : 2 * length].reshape(tiles, height, columns)
    data = [x.astype(jnp.float32) * (1.0 / DATA_UNIT) for x in [*keep, *[take[k] for k in range(tiles)]]]
    data = [x.astype(jnp.bfloat16) for x in data]

    info = jnp.stack([note[0], got[2 * length]]).astype(jnp.float32)
    shifts = info[:, 8 * taps : 8 * taps + blocks].astype(jnp.int32)
    matrices = blur_matrices(taps, height, info * (1.0 / TAP_UNIT))

    path = [(t, 0) for t in range(tiles)] + [(t, 1) for t in reversed(range(tiles))]
    hops = []
    for here, there in zip(path[:-1], path[1:]):
        one, two = device(*here, 1), device(*there, 0)
        hops += [(one, two), (two, one)]

    def plane_of(coded):
        return coded.astype(jnp.float32) * (1.0 / PLANE_UNIT) + 1.0

    plane = jnp.concatenate(ordered(planes, tile))
    twin = plane_of(jnp.concatenate(ordered([twin[k] for k in range(tiles)], tile)))
    current = plane_of(plane)
    narrow = current.astype(jnp.bfloat16)
    at_end = (tile == 0) & (core == view)
    for iteration in range(ITERS):
        first, last = iteration == 0, iteration == ITERS - 1
        other = lax.ppermute(plane, square, hops)
        if not first:
            twin = lax.ppermute(current, "gz", swap)
        other = jnp.where(at_end, 0.0, plane_of(other) if first else other.astype(jnp.float32) + 1.0)
        logs = correction_logs(me, shifts, narrow.reshape(tiles, height, columns), matrices, data)
        current, *rest = update(
            views, flag, current, twin, other, logs, [jnp.float32] if last else [jnp.float32, jnp.bfloat16]
        )
        if not last:
            narrow = rest[0]
            plane = (current - 1.0).astype(jnp.float16)

    result = current.astype(jnp.float16).reshape(tiles, height, columns)
    twin = lax.ppermute(result, "gz", swap)
    both = jnp.stack([jnp.where(core == 0, result, twin), jnp.where(core == 0, twin, result)], axis=1)
    pieces = exchange(lambda t: lax.dynamic_index_in_dim(both, t, 0, keepdims=False))
    result = jnp.concatenate(ordered(pieces, lax.bitwise_xor(tile, end_of(core))))
    return result.astype(jnp.float32)


def one_plane_each(mesh, view_data, estimate, psf_taps, offsets):
    tiles, views, depth = mesh.shape["tiles"], mesh.shape["views"], mesh.shape["gz"]
    planes = estimate.shape[0] // (mesh.shape["groups"] * depth)
    height, columns = estimate.shape[1] // tiles, estimate.shape[2]
    return (
        depth == 2
        and views == 2
        and planes == 2 * tiles
        and tiles & (tiles - 1) == 0
        and height == columns
        and height % (16 * offsets.shape[1]) == 0
        and columns == 128
        and 8 * psf_taps.shape[-1] + offsets.shape[1] <= columns
    )


def solution(mesh):
    in_specs = (
        P(("groups", "views"), "tiles", "gz", None, None),
        P(("groups", "gz"), "tiles", None),
        P("views", None, None, None),
        P("views", None),
    )
    out_specs = P(("groups", "gz"), "tiles", None)

    def step(*arrays):
        if not one_plane_each(mesh, *arrays):
            return jax.shard_map(shards, mesh=mesh, in_specs=in_specs, out_specs=out_specs, check_vma=False)(*arrays)
        body = jax.shard_map(plane_shards, mesh=mesh, in_specs=in_specs, out_specs=out_specs, check_vma=False)
        return body(*arrays)

    return step
```

```python
import functools

import jax
import jax.numpy as jnp
from jax import lax
from jax.experimental import pallas as pl
from jax.experimental.pallas import tpu as pltpu
from jax.sharding import PartitionSpec as P


ITERS = 2
CAP = 4


TV_WEIGHT = 0.1
SMOOTH_SQUARE = 0.0025


def with_halo(cells, sides, width):
    for axis, dim in sides:
        count = lax.axis_size(axis)
        ends = count - 1
        head = lax.slice_in_dim(cells, 0, width, axis=dim)
        tail = lax.slice_in_dim(cells, cells.shape[dim] - width, cells.shape[dim], axis=dim)
        cells = jnp.concatenate(
            [
                lax.ppermute(tail, axis, [(i, (i + 1) % count) for i in range(ends)]),
                cells,
                lax.ppermute(head, axis, [((i + 1) % count, i) for i in range(ends)]),
            ],
            axis=dim,
        )
    return cells


def toeplitz_matrix(profile, length):
    half_width = (profile.shape[0] - 1) // 2
    position = jnp.arange(length, dtype=jnp.int32)
    offset = position[None, :] - position[:, None] + half_width
    tap_index = jnp.arange(profile.shape[0], dtype=jnp.int32)
    picked = (offset[:, :, None] == tap_index[None, None, :]).astype(jnp.float32)
    return jnp.sum(picked * profile[None, None, :], axis=2).astype(jnp.bfloat16)


def curvature(padded):
    anchor = padded[:-1, :-1, :-1]
    grad_z = padded[1:, :-1, :-1] - anchor
    grad_y = padded[:-1, 1:, :-1] - anchor
    grad_x = padded[:-1, :-1, 1:] - anchor
    magnitude = jnp.sqrt(grad_z * grad_z + grad_y * grad_y + grad_x * grad_x + SMOOTH_SQUARE)
    unit_z = grad_z / magnitude
    unit_y = grad_y / magnitude
    unit_x = grad_x / magnitude
    return (
        unit_z[1:, 1:, 1:]
        - unit_z[:-1, 1:, 1:]
        + (unit_y[1:, 1:, 1:] - unit_y[1:, :-1, 1:])
        + (unit_x[1:, 1:, 1:] - unit_x[1:, 1:, :-1])
    )


def view_correction(view_tile, observed, kernel_y, kernel_x):
    blurred = jnp.zeros(view_tile.shape, jnp.float32)
    for term_index in range(2):
        half_blur = jnp.einsum(
            "yk,zkx->zyx", kernel_y[term_index], view_tile, preferred_element_type=jnp.float32
        ).astype(jnp.bfloat16)
        blurred = blurred + jnp.einsum(
            "zyk,xk->zyx", half_blur, kernel_x[term_index], preferred_element_type=jnp.float32
        )
    quotient = (observed.astype(jnp.float32) / blurred).astype(jnp.bfloat16)
    log_sum = jnp.zeros(view_tile.shape, jnp.float32)
    for term_index in range(2):
        half_back = jnp.einsum(
            "ky,zkx->zyx", kernel_y[term_index], quotient, preferred_element_type=jnp.float32
        ).astype(jnp.bfloat16)
        log_sum = log_sum + jnp.einsum(
            "zyk,kx->zyx", half_back, kernel_x[term_index], preferred_element_type=jnp.float32
        )
    return log_sum.astype(jnp.bfloat16)


def shards(view_data, estimate, psf_taps, offsets):
    owners = lax.axis_size("tiles")
    view_count = lax.axis_size("views")
    observed = view_data[0, 0]
    planes, height, columns = estimate.shape
    view_shift = offsets[0]
    blocks = view_shift.shape[0]
    block_rows = height // blocks
    slot_count = owners * CAP
    kernel_y = jnp.stack(
        [toeplitz_matrix(psf_taps[0, term_index, 0], height) for term_index in range(2)]
    )
    kernel_x = jnp.stack(
        [toeplitz_matrix(psf_taps[0, term_index, 1], columns) for term_index in range(2)]
    )
    position = jnp.arange(blocks, dtype=jnp.int32)
    same_owner = view_shift[:, None] == view_shift[None, :]
    before = position[None, :] < position[:, None]
    slot_rank = jnp.sum((same_owner & before).astype(jnp.int32), axis=1)
    member = lax.axis_index("tiles")
    target = (member + view_shift) % owners
    source_tile = (member - view_shift) % owners
    slot_index = jnp.arange(slot_count, dtype=jnp.int32)
    to_owner = ((target * CAP + slot_rank)[:, None] == slot_index[None, :]).astype(jnp.bfloat16)
    from_tile = ((source_tile * CAP + slot_rank)[:, None] == slot_index[None, :]).astype(
        jnp.bfloat16
    )
    current = estimate
    for _ in range(ITERS):
        padded = with_halo(current, (("tiles", 1), ("gz", 0)), 1)
        padded = jnp.pad(padded, ((0, 0), (0, 0), (1, 1)))
        owned_blocks = current.astype(jnp.bfloat16).reshape(planes, blocks, block_rows, columns)
        outgoing = jnp.einsum(
            "sk,zsrx->kzrx", from_tile, owned_blocks, preferred_element_type=jnp.float32
        ).astype(jnp.bfloat16)
        incoming = lax.all_to_all(
            outgoing.reshape(owners, CAP, planes, block_rows, columns),
            "tiles",
            split_axis=0,
            concat_axis=0,
            tiled=True,
        )
        view_tile = jnp.einsum(
            "sk,kzrx->zsrx",
            to_owner,
            incoming.reshape(slot_count, planes, block_rows, columns),
            preferred_element_type=jnp.float32,
        ).astype(jnp.bfloat16)
        view_tile = view_tile.reshape(planes, height, columns)
        correction = view_correction(view_tile, observed, kernel_y, kernel_x)
        correction = correction.reshape(planes, blocks, block_rows, columns)
        returned = jnp.einsum(
            "sk,zsrx->kzrx", to_owner, correction, preferred_element_type=jnp.float32
        ).astype(jnp.bfloat16)
        gathered = lax.all_to_all(
            returned.reshape(owners, CAP, planes, block_rows, columns),
            "tiles",
            split_axis=0,
            concat_axis=0,
            tiled=True,
        )
        owned_rows = jnp.einsum(
            "sk,kzrx->zsrx",
            from_tile,
            gathered.reshape(slot_count, planes, block_rows, columns),
            preferred_element_type=jnp.float32,
        ).reshape(planes, height, columns)
        log_values = jnp.log(owned_rows)
        share_rows = height // view_count
        log_part = lax.psum_scatter(log_values, "views", scatter_dimension=1, tiled=True)
        first_row = lax.axis_index("views") * share_rows
        window = lax.dynamic_slice_in_dim(padded, first_row, share_rows + 2, 1)
        damping = 1.0 - TV_WEIGHT * curvature(window)
        rows_now = lax.dynamic_slice_in_dim(current, first_row, share_rows, 1)
        updated = rows_now * jnp.exp(log_part / view_count) / damping
        current = lax.all_gather(updated, "views", axis=1, tiled=True)
    return current


INFO_ROWS = 16
PLANE_UNIT = 65534.0
DATA_UNIT = 1024.0
TAP_UNIT = 8192.0
CHUNK = 32
VMEM = pl.BlockSpec(memory_space=pltpu.VMEM)
SMEM = pl.BlockSpec(memory_space=pltpu.SMEM)
LIMIT = pltpu.CompilerParams(vmem_limit_bytes=16 * 2**20)


def matrices_kernel(taps, info_ref, out_ref):
    views, columns = info_ref.shape
    length = out_ref.shape[-2] // 2
    half_width = (taps - 1) // 2
    row = lax.broadcasted_iota(jnp.int32, (length, columns), 0)
    column = lax.broadcasted_iota(jnp.int32, (length, columns), 1)
    band = jnp.abs(row - column) <= half_width
    for v in range(views):
        profile = jnp.broadcast_to(info_ref[v : v + 1, :], (8, columns))
        for kind, (flipped, axis) in enumerate([(0, 0), (1, 1), (1, 0), (0, 1)]):
            for r in range(2):
                lane = (4 * flipped + 2 * r + axis) * taps + half_width
                spread = jnp.broadcast_to(pltpu.roll(profile, columns - lane, 1)[0:1], (length, columns))
                rolled = pltpu.roll(spread, 0, 1, stride=1, stride_axis=0)
                rolled = jnp.where(band, rolled, 0.0).astype(out_ref.dtype)
                out_ref[v, kind, r * length : (r + 1) * length, :] = rolled


def blur_matrices(taps, length, info):
    views, columns = info.shape
    return pl.pallas_call(
        functools.partial(matrices_kernel, taps),
        out_shape=jax.ShapeDtypeStruct((views, 4, 2 * length, columns), jnp.bfloat16),
        in_specs=[VMEM],
        out_specs=VMEM,
        compiler_params=LIMIT,
        name="blur_matrices",
    )(info)


def correction_kernel(tiles, tile_ref, offsets_ref, current_ref, matrices_ref, *refs):
    views, blocks = offsets_ref.shape
    data, log_ref, work = refs[: views * tiles], refs[views * tiles], refs[views * tiles + 1 :]
    height, columns = data[0].shape
    rows = height // blocks
    me = tile_ref[0]
    shift = [[offsets_ref[w, s] for s in range(blocks)] for w in range(views)]
    planes = [work[3 * w] for w in range(views)]
    halves = [work[3 * w + 1] for w in range(views)]
    logs = [work[3 * w + 2] for w in range(views)]

    def first(w, kind):
        half = jnp.dot(matrices_ref[w, kind], planes[w][...], preferred_element_type=jnp.float32)
        half = half.astype(jnp.bfloat16)
        for k in range(tiles):
            for r in range(2):
                halves[w][k * height : (k + 1) * height, r * columns : (r + 1) * columns] = half[
                    r * height : (r + 1) * height, k * columns : (k + 1) * columns
                ]

    for w in range(views):
        for k in range(tiles):
            tile = lax.bitwise_xor(me, k)
            for s in range(blocks):
                owner = lax.rem(tile + shift[w][s], tiles)
                planes[w][s * rows : (s + 1) * rows, k * columns : (k + 1) * columns] = current_ref[
                    owner, s * rows : (s + 1) * rows, :
                ]
    for w in range(views):
        first(w, 0)
    for w in range(views):
        blurred = jnp.dot(halves[w][...], matrices_ref[w, 1], preferred_element_type=jnp.float32)
        for k in range(tiles):
            quotient = data[w * tiles + k][...].astype(jnp.float32) / blurred[k * height : (k + 1) * height]
            planes[w][:, k * columns : (k + 1) * columns] = quotient.astype(jnp.bfloat16)
    for w in range(views):
        first(w, 2)
    for w in range(views):
        back = jnp.dot(halves[w][...], matrices_ref[w, 3], preferred_element_type=jnp.float32)
        logs[w][...] = jnp.log(back.astype(jnp.bfloat16).astype(jnp.float32))
    for o in range(tiles):
        for s in range(blocks):
            total = None
            for w in range(views):
                tile = lax.rem(o - shift[w][s] + tiles, tiles)
                start = pl.multiple_of(lax.bitwise_xor(tile, me) * height + s * rows, rows)
                part = logs[w][pl.ds(start, rows), :]
                total = part if total is None else total + part
            log_ref[o * height + s * rows : o * height + (s + 1) * rows, :] = total


def correction_logs(tile, offsets, current, matrices, data):
    tiles, height, columns = current.shape
    scratch = [
        pltpu.VMEM((height, tiles * columns), jnp.bfloat16),
        pltpu.VMEM((tiles * height, 2 * columns), jnp.bfloat16),
        pltpu.VMEM((tiles * height, columns), jnp.float32),
    ]
    return pl.pallas_call(
        functools.partial(correction_kernel, tiles),
        out_shape=jax.ShapeDtypeStruct((tiles * height, columns), jnp.float32),
        in_specs=[SMEM, SMEM] + [VMEM] * (2 + len(data)),
        out_specs=VMEM,
        scratch_shapes=scratch * offsets.shape[0],
        cost_estimate=pl.CostEstimate(flops=300_000_000, bytes_accessed=1_500_000, transcendentals=0),
        compiler_params=LIMIT,
        name="correction",
    )(tile, offsets, current, matrices, *data)


def update_kernel(views, core_ref, current_ref, twin_ref, other_ref, log_ref, *new_refs):
    total, columns = current_ref.shape
    first = core_ref[0] == 0
    row = lax.broadcasted_iota(jnp.int32, (CHUNK, columns), 0)
    column = lax.broadcasted_iota(jnp.int32, (CHUNK, columns), 1)

    def scale(z, y, x):
        return lax.rsqrt(z * z + y * y + x * x + SMOOTH_SQUARE)

    def pick(low, high, start, size):
        return jnp.where(first, low[start : start + size, :], high[start : start + size, :])

    def next_row(x, following):
        return jnp.where(row == CHUNK - 1, following, pltpu.roll(x, CHUNK - 1, 0))

    def next_column(x):
        return jnp.where(column == columns - 1, 0.0, pltpu.roll(x, columns - 1, 1))

    def edge(x):
        return x * lax.rsqrt(x * x + SMOOTH_SQUARE)

    carry = edge(current_ref[0:1, :])
    for start in range(0, total, CHUNK):
        stop = start + CHUNK
        current = current_ref[start:stop, :]
        above = pick(twin_ref, other_ref, start, CHUNK)
        below = pick(other_ref, twin_ref, start, CHUNK)
        if stop < total:
            current_next, below_next = current_ref[stop : stop + 1, :], pick(other_ref, twin_ref, stop, 1)
        else:
            current_next = below_next = jnp.zeros((1, columns), jnp.float32)
        grad_z = above - current
        grad_y = next_row(current, current_next) - current
        grad_x = next_column(current) - current
        inverse = scale(grad_z, grad_y, grad_x)
        unit_y, unit_x = grad_y * inverse, grad_x * inverse
        before_y = jnp.where(row == 0, carry, pltpu.roll(unit_y, 1, 0))
        before_x = jnp.where(column == 0, edge(current), pltpu.roll(unit_x, 1, 1))
        carry = unit_y[CHUNK - 1 : CHUNK, :]
        lower_z = current - below
        lower = lower_z * scale(lower_z, next_row(below, below_next) - below, next_column(below) - below)
        divergence = grad_z * inverse - lower + (unit_y - before_y) + (unit_x - before_x)
        damping = 1.0 - TV_WEIGHT * divergence
        new = current * jnp.exp(log_ref[start:stop, :] * (1.0 / views)) / damping
        for ref in new_refs:
            ref[start:stop, :] = new.astype(ref.dtype)


def update(views, core, current, twin, other, logs, dtypes):
    return pl.pallas_call(
        functools.partial(update_kernel, views),
        out_shape=[jax.ShapeDtypeStruct(current.shape, dtype) for dtype in dtypes],
        in_specs=[SMEM] + [VMEM] * 4,
        out_specs=[VMEM] * len(dtypes),
        compiler_params=LIMIT,
        name="update",
    )(core, current, twin, other, logs)


def plane_shards(view_data, estimate, psf_taps, offsets):
    tiles, views = lax.axis_size("tiles"), lax.axis_size("views")
    square = ("tiles", "views", "gz")
    planes, height, columns = estimate.shape
    blocks = offsets.shape[1]
    taps = psf_taps.shape[-1]
    tile, view, core = lax.axis_index("tiles"), lax.axis_index("views"), lax.axis_index("gz")
    swap = [(0, 1), (1, 0)]

    def device(t, v, g):
        return (t * views + v) * 2 + g

    def ordered(pieces, shift):
        placed = []
        for i in range(tiles):
            chosen = pieces[i]
            for s in range(1, tiles):
                chosen = jnp.where(shift == s, pieces[i ^ s], chosen)
            placed.append(chosen)
        return placed

    def exchange(pick):
        pieces = []
        for k in range(tiles):
            pairs = [(device(t, v, g), device(t ^ k, g, v)) for t in range(tiles) for v in range(2) for g in range(2)]
            pieces.append(lax.ppermute(pick(k), square, pairs))
        return pieces

    def end_of(chain):
        return jnp.where(chain == 0, 0, tiles - 1)

    me = tile.reshape(1).astype(jnp.int32)
    flag = core.reshape(1).astype(jnp.int32)

    wide = estimate.reshape(tiles, 2, height, columns)
    wide = lax.dynamic_index_in_dim(wide, view, 1, keepdims=True)
    wide = jnp.round((wide - 1.0) * PLANE_UNIT).astype(jnp.int16)
    data = view_data.reshape(tiles, 2, height, columns).astype(jnp.float32)
    data = (data * DATA_UNIT).astype(jnp.int16)
    payload = jnp.concatenate([wide, data], axis=1).reshape(tiles, 3 * height, columns)
    payload, psf_taps, offsets = lax.optimization_barrier((payload, psf_taps, offsets))
    profiles = [psf_taps.reshape(-1), psf_taps[..., ::-1].reshape(-1)]
    info = [lax.reduce_precision(p, 8, 7) * TAP_UNIT for p in profiles]
    info = jnp.concatenate([*info, offsets.reshape(-1).astype(jnp.float32)])
    info = jnp.pad(info, (0, columns - info.shape[0])).astype(jnp.int16)
    info = jnp.broadcast_to(info, (INFO_ROWS, columns))

    def for_tile(k):
        place = lax.bitwise_xor(lax.bitwise_xor(tile, k), end_of(core))
        piece = lax.dynamic_index_in_dim(payload, place, 0, keepdims=False)
        return piece if k else jnp.concatenate([piece, info])

    pieces = exchange(for_tile)
    note = pieces[0][3 * height :]
    notes = jnp.stack([note[0], lax.ppermute(note, "gz", swap)[0]]).astype(jnp.float32)
    shifts = notes[:, 8 * taps : 8 * taps + blocks].astype(jnp.int32)
    matrices = blur_matrices(taps, height, notes * (1.0 / TAP_UNIT))

    planes = [piece[:height] for piece in pieces]
    pairs = [piece[height : 3 * height].reshape(2, height, columns) for piece in pieces]
    keep = [lax.dynamic_index_in_dim(pair, core, 0, keepdims=False) for pair in pairs]
    give = [lax.dynamic_index_in_dim(pair, 1 - core, 0, keepdims=False) for pair in pairs]
    got = lax.ppermute(jnp.concatenate([*planes, *give]), "gz", swap)
    length = tiles * height
    twin = got[:length].reshape(tiles, height, columns)
    take = got[length:].reshape(tiles, height, columns)
    data = [x.astype(jnp.float32) * (1.0 / DATA_UNIT) for x in [*keep, *[take[k] for k in range(tiles)]]]
    data = [x.astype(jnp.bfloat16) for x in data]

    path = [(t, 0) for t in range(tiles)] + [(t, 1) for t in reversed(range(tiles))]
    hops = []
    for here, there in zip(path[:-1], path[1:]):
        one, two = device(*here, 1), device(*there, 0)
        hops += [(one, two), (two, one)]

    def plane_of(coded):
        return coded.astype(jnp.float32) * (1.0 / PLANE_UNIT) + 1.0

    plane = jnp.concatenate(ordered(planes, tile))
    twin = plane_of(jnp.concatenate(ordered([twin[k] for k in range(tiles)], tile)))
    current = plane_of(plane)
    narrow = current.astype(jnp.bfloat16)
    at_end = (tile == 0) & (core == view)
    for iteration in range(ITERS):
        first, last = iteration == 0, iteration == ITERS - 1
        other = lax.ppermute(plane, square, hops)
        if not first:
            twin = lax.ppermute(current, "gz", swap)
        other = jnp.where(at_end, 0.0, plane_of(other) if first else other.astype(jnp.float32) + 1.0)
        logs = correction_logs(me, shifts, narrow.reshape(tiles, height, columns), matrices, data)
        current, *rest = update(
            views, flag, current, twin, other, logs, [jnp.float32] if last else [jnp.float32, jnp.bfloat16]
        )
        if not last:
            narrow = rest[0]
            plane = (current - 1.0).astype(jnp.float16)

    result = current.astype(jnp.float16).reshape(tiles, height, columns)
    pieces = []
    for k in range(tiles):
        piece = lax.dynamic_index_in_dim(result, lax.bitwise_xor(tile, k), 0)
        pieces.append(lax.ppermute(piece, "tiles", [(t, t ^ k) for t in range(tiles)]) if k else piece)
    mine = jnp.concatenate(pieces)
    crossed = [lax.ppermute(pieces[0], "views", swap)]
    crossed.append(lax.ppermute(mine[1:], "views", swap))
    crossed = jnp.concatenate(crossed)
    straight = view == core
    same = jnp.where(straight, mine, crossed)
    twin = lax.ppermute(jnp.where(straight, crossed, mine), "gz", swap)
    even, odd = jnp.where(core == 0, same, twin), jnp.where(core == 0, twin, same)
    result = [jnp.stack([even[k], odd[k]]) for k in range(tiles)]
    result = jnp.concatenate(ordered(result, lax.bitwise_xor(tile, end_of(core))))
    return result.astype(jnp.float32)


def one_plane_each(mesh, view_data, estimate, psf_taps, offsets):
    tiles, views, depth = mesh.shape["tiles"], mesh.shape["views"], mesh.shape["gz"]
    planes = estimate.shape[0] // (mesh.shape["groups"] * depth)
    height, columns = estimate.shape[1] // tiles, estimate.shape[2]
    return (
        depth == 2
        and views == 2
        and planes == 2 * tiles
        and tiles & (tiles - 1) == 0
        and height == columns
        and height % (16 * offsets.shape[1]) == 0
        and columns == 128
        and 8 * psf_taps.shape[-1] + offsets.shape[1] <= columns
    )


def solution(mesh):
    in_specs = (
        P(("groups", "views"), "tiles", "gz", None, None),
        P(("groups", "gz"), "tiles", None),
        P("views", None, None, None),
        P("views", None),
    )
    out_specs = P(("groups", "gz"), "tiles", None)

    def step(*arrays):
        if not one_plane_each(mesh, *arrays):
            return jax.shard_map(shards, mesh=mesh, in_specs=in_specs, out_specs=out_specs, check_vma=False)(*arrays)
        body = jax.shard_map(plane_shards, mesh=mesh, in_specs=in_specs, out_specs=out_specs, check_vma=False)
        return body(*arrays)

    return step
```

```python
import functools

import jax
import jax.numpy as jnp
from jax import lax
from jax.experimental import pallas as pl
from jax.experimental.pallas import tpu as pltpu
from jax.sharding import PartitionSpec as P


ITERS = 2
CAP = 4


TV_WEIGHT = 0.1
SMOOTH_SQUARE = 0.0025


def with_halo(cells, sides, width):
    for axis, dim in sides:
        count = lax.axis_size(axis)
        ends = count - 1
        head = lax.slice_in_dim(cells, 0, width, axis=dim)
        tail = lax.slice_in_dim(cells, cells.shape[dim] - width, cells.shape[dim], axis=dim)
        cells = jnp.concatenate(
            [
                lax.ppermute(tail, axis, [(i, (i + 1) % count) for i in range(ends)]),
                cells,
                lax.ppermute(head, axis, [((i + 1) % count, i) for i in range(ends)]),
            ],
            axis=dim,
        )
    return cells


def toeplitz_matrix(profile, length):
    half_width = (profile.shape[0] - 1) // 2
    position = jnp.arange(length, dtype=jnp.int32)
    offset = position[None, :] - position[:, None] + half_width
    tap_index = jnp.arange(profile.shape[0], dtype=jnp.int32)
    picked = (offset[:, :, None] == tap_index[None, None, :]).astype(jnp.float32)
    return jnp.sum(picked * profile[None, None, :], axis=2).astype(jnp.bfloat16)


def curvature(padded):
    anchor = padded[:-1, :-1, :-1]
    grad_z = padded[1:, :-1, :-1] - anchor
    grad_y = padded[:-1, 1:, :-1] - anchor
    grad_x = padded[:-1, :-1, 1:] - anchor
    magnitude = jnp.sqrt(grad_z * grad_z + grad_y * grad_y + grad_x * grad_x + SMOOTH_SQUARE)
    unit_z = grad_z / magnitude
    unit_y = grad_y / magnitude
    unit_x = grad_x / magnitude
    return (
        unit_z[1:, 1:, 1:]
        - unit_z[:-1, 1:, 1:]
        + (unit_y[1:, 1:, 1:] - unit_y[1:, :-1, 1:])
        + (unit_x[1:, 1:, 1:] - unit_x[1:, 1:, :-1])
    )


def view_correction(view_tile, observed, kernel_y, kernel_x):
    blurred = jnp.zeros(view_tile.shape, jnp.float32)
    for term_index in range(2):
        half_blur = jnp.einsum(
            "yk,zkx->zyx", kernel_y[term_index], view_tile, preferred_element_type=jnp.float32
        ).astype(jnp.bfloat16)
        blurred = blurred + jnp.einsum(
            "zyk,xk->zyx", half_blur, kernel_x[term_index], preferred_element_type=jnp.float32
        )
    quotient = (observed.astype(jnp.float32) / blurred).astype(jnp.bfloat16)
    log_sum = jnp.zeros(view_tile.shape, jnp.float32)
    for term_index in range(2):
        half_back = jnp.einsum(
            "ky,zkx->zyx", kernel_y[term_index], quotient, preferred_element_type=jnp.float32
        ).astype(jnp.bfloat16)
        log_sum = log_sum + jnp.einsum(
            "zyk,kx->zyx", half_back, kernel_x[term_index], preferred_element_type=jnp.float32
        )
    return log_sum.astype(jnp.bfloat16)


def shards(view_data, estimate, psf_taps, offsets):
    owners = lax.axis_size("tiles")
    view_count = lax.axis_size("views")
    observed = view_data[0, 0]
    planes, height, columns = estimate.shape
    view_shift = offsets[0]
    blocks = view_shift.shape[0]
    block_rows = height // blocks
    slot_count = owners * CAP
    kernel_y = jnp.stack(
        [toeplitz_matrix(psf_taps[0, term_index, 0], height) for term_index in range(2)]
    )
    kernel_x = jnp.stack(
        [toeplitz_matrix(psf_taps[0, term_index, 1], columns) for term_index in range(2)]
    )
    position = jnp.arange(blocks, dtype=jnp.int32)
    same_owner = view_shift[:, None] == view_shift[None, :]
    before = position[None, :] < position[:, None]
    slot_rank = jnp.sum((same_owner & before).astype(jnp.int32), axis=1)
    member = lax.axis_index("tiles")
    target = (member + view_shift) % owners
    source_tile = (member - view_shift) % owners
    slot_index = jnp.arange(slot_count, dtype=jnp.int32)
    to_owner = ((target * CAP + slot_rank)[:, None] == slot_index[None, :]).astype(jnp.bfloat16)
    from_tile = ((source_tile * CAP + slot_rank)[:, None] == slot_index[None, :]).astype(
        jnp.bfloat16
    )
    current = estimate
    for _ in range(ITERS):
        padded = with_halo(current, (("tiles", 1), ("gz", 0)), 1)
        padded = jnp.pad(padded, ((0, 0), (0, 0), (1, 1)))
        owned_blocks = current.astype(jnp.bfloat16).reshape(planes, blocks, block_rows, columns)
        outgoing = jnp.einsum(
            "sk,zsrx->kzrx", from_tile, owned_blocks, preferred_element_type=jnp.float32
        ).astype(jnp.bfloat16)
        incoming = lax.all_to_all(
            outgoing.reshape(owners, CAP, planes, block_rows, columns),
            "tiles",
            split_axis=0,
            concat_axis=0,
            tiled=True,
        )
        view_tile = jnp.einsum(
            "sk,kzrx->zsrx",
            to_owner,
            incoming.reshape(slot_count, planes, block_rows, columns),
            preferred_element_type=jnp.float32,
        ).astype(jnp.bfloat16)
        view_tile = view_tile.reshape(planes, height, columns)
        correction = view_correction(view_tile, observed, kernel_y, kernel_x)
        correction = correction.reshape(planes, blocks, block_rows, columns)
        returned = jnp.einsum(
            "sk,zsrx->kzrx", to_owner, correction, preferred_element_type=jnp.float32
        ).astype(jnp.bfloat16)
        gathered = lax.all_to_all(
            returned.reshape(owners, CAP, planes, block_rows, columns),
            "tiles",
            split_axis=0,
            concat_axis=0,
            tiled=True,
        )
        owned_rows = jnp.einsum(
            "sk,kzrx->zsrx",
            from_tile,
            gathered.reshape(slot_count, planes, block_rows, columns),
            preferred_element_type=jnp.float32,
        ).reshape(planes, height, columns)
        log_values = jnp.log(owned_rows)
        share_rows = height // view_count
        log_part = lax.psum_scatter(log_values, "views", scatter_dimension=1, tiled=True)
        first_row = lax.axis_index("views") * share_rows
        window = lax.dynamic_slice_in_dim(padded, first_row, share_rows + 2, 1)
        damping = 1.0 - TV_WEIGHT * curvature(window)
        rows_now = lax.dynamic_slice_in_dim(current, first_row, share_rows, 1)
        updated = rows_now * jnp.exp(log_part / view_count) / damping
        current = lax.all_gather(updated, "views", axis=1, tiled=True)
    return current


INFO_ROWS = 16
PLANE_UNIT = 65534.0
DATA_UNIT = 1024.0
TAP_UNIT = 8192.0
CHUNK = 32
VMEM = pl.BlockSpec(memory_space=pltpu.VMEM)
SMEM = pl.BlockSpec(memory_space=pltpu.SMEM)
LIMIT = pltpu.CompilerParams(vmem_limit_bytes=16 * 2**20)


def matrices_kernel(taps, info_ref, out_ref):
    views, columns = info_ref.shape
    length = out_ref.shape[-2] // 2
    half_width = (taps - 1) // 2
    row = lax.broadcasted_iota(jnp.int32, (length, columns), 0)
    column = lax.broadcasted_iota(jnp.int32, (length, columns), 1)
    band = jnp.abs(row - column) <= half_width
    for v in range(views):
        profile = jnp.broadcast_to(info_ref[v : v + 1, :], (8, columns))
        for kind, (flipped, axis) in enumerate([(0, 0), (1, 1), (1, 0), (0, 1)]):
            for r in range(2):
                lane = (4 * flipped + 2 * r + axis) * taps + half_width
                spread = jnp.broadcast_to(pltpu.roll(profile, columns - lane, 1)[0:1], (length, columns))
                rolled = pltpu.roll(spread, 0, 1, stride=1, stride_axis=0)
                rolled = jnp.where(band, rolled, 0.0).astype(out_ref.dtype)
                out_ref[v, kind, r * length : (r + 1) * length, :] = rolled


def blur_matrices(taps, length, info):
    views, columns = info.shape
    return pl.pallas_call(
        functools.partial(matrices_kernel, taps),
        out_shape=jax.ShapeDtypeStruct((views, 4, 2 * length, columns), jnp.bfloat16),
        in_specs=[VMEM],
        out_specs=VMEM,
        compiler_params=LIMIT,
        name="blur_matrices",
    )(info)


def correction_kernel(tiles, tile_ref, offsets_ref, current_ref, matrices_ref, *refs):
    views, blocks = offsets_ref.shape
    data, log_ref, work = refs[: views * tiles], refs[views * tiles], refs[views * tiles + 1 :]
    height, columns = data[0].shape
    rows = height // blocks
    me = tile_ref[0]
    shift = [[offsets_ref[w, s] for s in range(blocks)] for w in range(views)]
    planes = [work[3 * w] for w in range(views)]
    halves = [work[3 * w + 1] for w in range(views)]
    logs = [work[3 * w + 2] for w in range(views)]

    def first(w, kind):
        half = jnp.dot(matrices_ref[w, kind], planes[w][...], preferred_element_type=jnp.float32)
        half = half.astype(jnp.bfloat16)
        for k in range(tiles):
            for r in range(2):
                halves[w][k * height : (k + 1) * height, r * columns : (r + 1) * columns] = half[
                    r * height : (r + 1) * height, k * columns : (k + 1) * columns
                ]

    for w in range(views):
        for k in range(tiles):
            tile = lax.bitwise_xor(me, k)
            for s in range(blocks):
                owner = lax.rem(tile + shift[w][s], tiles)
                planes[w][s * rows : (s + 1) * rows, k * columns : (k + 1) * columns] = current_ref[
                    owner, s * rows : (s + 1) * rows, :
                ]
    for w in range(views):
        first(w, 0)
    for w in range(views):
        blurred = jnp.dot(halves[w][...], matrices_ref[w, 1], preferred_element_type=jnp.float32)
        for k in range(tiles):
            quotient = data[w * tiles + k][...].astype(jnp.float32) / blurred[k * height : (k + 1) * height]
            planes[w][:, k * columns : (k + 1) * columns] = quotient.astype(jnp.bfloat16)
    for w in range(views):
        first(w, 2)
    for w in range(views):
        back = jnp.dot(halves[w][...], matrices_ref[w, 3], preferred_element_type=jnp.float32)
        logs[w][...] = jnp.log(back.astype(jnp.bfloat16).astype(jnp.float32))
    for o in range(tiles):
        for s in range(blocks):
            total = None
            for w in range(views):
                tile = lax.rem(o - shift[w][s] + tiles, tiles)
                start = pl.multiple_of(lax.bitwise_xor(tile, me) * height + s * rows, rows)
                part = logs[w][pl.ds(start, rows), :]
                total = part if total is None else total + part
            log_ref[o * height + s * rows : o * height + (s + 1) * rows, :] = total


def correction_logs(tile, offsets, current, matrices, data):
    tiles, height, columns = current.shape
    scratch = [
        pltpu.VMEM((height, tiles * columns), jnp.bfloat16),
        pltpu.VMEM((tiles * height, 2 * columns), jnp.bfloat16),
        pltpu.VMEM((tiles * height, columns), jnp.float32),
    ]
    return pl.pallas_call(
        functools.partial(correction_kernel, tiles),
        out_shape=jax.ShapeDtypeStruct((tiles * height, columns), jnp.float32),
        in_specs=[SMEM, SMEM] + [VMEM] * (2 + len(data)),
        out_specs=VMEM,
        scratch_shapes=scratch * offsets.shape[0],
        cost_estimate=pl.CostEstimate(flops=300_000_000, bytes_accessed=1_500_000, transcendentals=0),
        compiler_params=LIMIT,
        name="correction",
    )(tile, offsets, current, matrices, *data)


def update_kernel(views, core_ref, current_ref, twin_ref, other_ref, log_ref, *new_refs):
    total, columns = current_ref.shape
    first = core_ref[0] == 0
    row = lax.broadcasted_iota(jnp.int32, (CHUNK, columns), 0)
    column = lax.broadcasted_iota(jnp.int32, (CHUNK, columns), 1)

    def scale(z, y, x):
        return lax.rsqrt(z * z + y * y + x * x + SMOOTH_SQUARE)

    def pick(low, high, start, size):
        return jnp.where(first, low[start : start + size, :], high[start : start + size, :])

    def next_row(x, following):
        return jnp.where(row == CHUNK - 1, following, pltpu.roll(x, CHUNK - 1, 0))

    def next_column(x):
        return jnp.where(column == columns - 1, 0.0, pltpu.roll(x, columns - 1, 1))

    def edge(x):
        return x * lax.rsqrt(x * x + SMOOTH_SQUARE)

    carry = edge(current_ref[0:1, :])
    for start in range(0, total, CHUNK):
        stop = start + CHUNK
        current = current_ref[start:stop, :]
        above = pick(twin_ref, other_ref, start, CHUNK)
        below = pick(other_ref, twin_ref, start, CHUNK)
        if stop < total:
            current_next, below_next = current_ref[stop : stop + 1, :], pick(other_ref, twin_ref, stop, 1)
        else:
            current_next = below_next = jnp.zeros((1, columns), jnp.float32)
        grad_z = above - current
        grad_y = next_row(current, current_next) - current
        grad_x = next_column(current) - current
        inverse = scale(grad_z, grad_y, grad_x)
        unit_y, unit_x = grad_y * inverse, grad_x * inverse
        before_y = jnp.where(row == 0, carry, pltpu.roll(unit_y, 1, 0))
        before_x = jnp.where(column == 0, edge(current), pltpu.roll(unit_x, 1, 1))
        carry = unit_y[CHUNK - 1 : CHUNK, :]
        lower_z = current - below
        lower = lower_z * scale(lower_z, next_row(below, below_next) - below, next_column(below) - below)
        divergence = grad_z * inverse - lower + (unit_y - before_y) + (unit_x - before_x)
        damping = 1.0 - TV_WEIGHT * divergence
        new = current * jnp.exp(log_ref[start:stop, :] * (1.0 / views)) / damping
        for ref in new_refs:
            ref[start:stop, :] = new.astype(ref.dtype)


def update(views, core, current, twin, other, logs, dtypes):
    return pl.pallas_call(
        functools.partial(update_kernel, views),
        out_shape=[jax.ShapeDtypeStruct(current.shape, dtype) for dtype in dtypes],
        in_specs=[SMEM] + [VMEM] * 4,
        out_specs=[VMEM] * len(dtypes),
        compiler_params=LIMIT,
        name="update",
    )(core, current, twin, other, logs)


def plane_shards(view_data, estimate, psf_taps, offsets):
    tiles, views = lax.axis_size("tiles"), lax.axis_size("views")
    square = ("tiles", "views", "gz")
    planes, height, columns = estimate.shape
    blocks = offsets.shape[1]
    taps = psf_taps.shape[-1]
    tile, view, core = lax.axis_index("tiles"), lax.axis_index("views"), lax.axis_index("gz")
    swap = [(0, 1), (1, 0)]

    def device(t, v, g):
        return (t * views + v) * 2 + g

    def ordered(pieces, shift):
        placed = []
        for i in range(tiles):
            chosen = pieces[i]
            for s in range(1, tiles):
                chosen = jnp.where(shift == s, pieces[i ^ s], chosen)
            placed.append(chosen)
        return placed

    def exchange(pick):
        pieces = []
        for k in range(tiles):
            pairs = [(device(t, v, g), device(t ^ k, g, v)) for t in range(tiles) for v in range(2) for g in range(2)]
            pieces.append(lax.ppermute(pick(k), square, pairs))
        return pieces

    def end_of(chain):
        return jnp.where(chain == 0, 0, tiles - 1)

    me = tile.reshape(1).astype(jnp.int32)
    flag = core.reshape(1).astype(jnp.int32)

    wide = estimate.reshape(tiles, 2, height, columns)
    wide = lax.dynamic_index_in_dim(wide, view, 1, keepdims=True)
    wide = jnp.round((wide - 1.0) * PLANE_UNIT).astype(jnp.int16)
    data = view_data.reshape(tiles, 2, height, columns).astype(jnp.float32)
    data = (data * DATA_UNIT).astype(jnp.int16)
    payload = jnp.concatenate([wide, data], axis=1).reshape(tiles, 3 * height, columns)
    payload, psf_taps, offsets = lax.optimization_barrier((payload, psf_taps, offsets))

    def for_tile(k):
        place = lax.bitwise_xor(lax.bitwise_xor(tile, k), end_of(core))
        return lax.dynamic_index_in_dim(payload, place, 0, keepdims=False)

    pieces = exchange(for_tile)

    profiles = [psf_taps.reshape(-1), psf_taps[..., ::-1].reshape(-1)]
    info = [lax.reduce_precision(p, 8, 7) * TAP_UNIT for p in profiles]
    info = jnp.concatenate([*info, offsets.reshape(-1).astype(jnp.float32)])
    info = jnp.pad(info, (0, columns - info.shape[0])).astype(jnp.int16)
    info = jnp.broadcast_to(info, (INFO_ROWS, columns))
    note = lax.ppermute(info, "views", swap)
    straight = view == core
    notes = jnp.stack([jnp.where(straight, info[0], note[0]), jnp.where(straight, note[0], info[0])])
    notes = notes.astype(jnp.float32)
    shifts = notes[:, 8 * taps : 8 * taps + blocks].astype(jnp.int32)
    matrices = blur_matrices(taps, height, notes * (1.0 / TAP_UNIT))

    planes = [piece[:height] for piece in pieces]
    pairs = [piece[height : 3 * height].reshape(2, height, columns) for piece in pieces]
    keep = [lax.dynamic_index_in_dim(pair, core, 0, keepdims=False) for pair in pairs]
    give = [lax.dynamic_index_in_dim(pair, 1 - core, 0, keepdims=False) for pair in pairs]
    got = lax.ppermute(jnp.concatenate([*planes, *give]), "gz", swap)
    length = tiles * height
    twin = got[:length].reshape(tiles, height, columns)
    take = got[length:].reshape(tiles, height, columns)
    data = [x.astype(jnp.float32) * (1.0 / DATA_UNIT) for x in [*keep, *[take[k] for k in range(tiles)]]]
    data = [x.astype(jnp.bfloat16) for x in data]

    path = [(t, 0) for t in range(tiles)] + [(t, 1) for t in reversed(range(tiles))]
    hops = []
    for here, there in zip(path[:-1], path[1:]):
        one, two = device(*here, 1), device(*there, 0)
        hops += [(one, two), (two, one)]

    def plane_of(coded):
        return coded.astype(jnp.float32) * (1.0 / PLANE_UNIT) + 1.0

    plane = jnp.concatenate(ordered(planes, tile))
    twin = plane_of(jnp.concatenate(ordered([twin[k] for k in range(tiles)], tile)))
    current = plane_of(plane)
    narrow = current.astype(jnp.bfloat16)
    at_end = (tile == 0) & (core == view)
    for iteration in range(ITERS):
        first, last = iteration == 0, iteration == ITERS - 1
        other = lax.ppermute(plane, square, hops)
        if not first:
            twin = lax.ppermute(current, "gz", swap)
        other = jnp.where(at_end, 0.0, plane_of(other) if first else other.astype(jnp.float32) + 1.0)
        logs = correction_logs(me, shifts, narrow.reshape(tiles, height, columns), matrices, data)
        current, *rest = update(
            views, flag, current, twin, other, logs, [jnp.float32] if last else [jnp.float32, jnp.bfloat16]
        )
        if not last:
            narrow = rest[0]
            plane = (current - 1.0).astype(jnp.float16)

    result = current.astype(jnp.float16).reshape(tiles, height, columns)
    pieces = []
    for k in range(tiles):
        piece = lax.dynamic_index_in_dim(result, lax.bitwise_xor(tile, k), 0)
        pieces.append(lax.ppermute(piece, "tiles", [(t, t ^ k) for t in range(tiles)]) if k else piece)
    mine = jnp.concatenate(pieces)
    crossed = [lax.ppermute(pieces[0], "views", swap)]
    crossed.append(lax.ppermute(mine[1:], "views", swap))
    crossed = jnp.concatenate(crossed)
    same = jnp.where(straight, mine, crossed)
    twin = lax.ppermute(jnp.where(straight, crossed, mine), "gz", swap)
    even, odd = jnp.where(core == 0, same, twin), jnp.where(core == 0, twin, same)
    result = [jnp.stack([even[k], odd[k]]) for k in range(tiles)]
    result = jnp.concatenate(ordered(result, lax.bitwise_xor(tile, end_of(core))))
    return result.astype(jnp.float32)


def one_plane_each(mesh, view_data, estimate, psf_taps, offsets):
    tiles, views, depth = mesh.shape["tiles"], mesh.shape["views"], mesh.shape["gz"]
    planes = estimate.shape[0] // (mesh.shape["groups"] * depth)
    height, columns = estimate.shape[1] // tiles, estimate.shape[2]
    return (
        depth == 2
        and views == 2
        and planes == 2 * tiles
        and tiles & (tiles - 1) == 0
        and height == columns
        and height % (16 * offsets.shape[1]) == 0
        and columns == 128
        and 8 * psf_taps.shape[-1] + offsets.shape[1] <= columns
    )


def solution(mesh):
    in_specs = (
        P(("groups", "views"), "tiles", "gz", None, None),
        P(("groups", "gz"), "tiles", None),
        P("views", None, None, None),
        P("views", None),
    )
    out_specs = P(("groups", "gz"), "tiles", None)

    def step(*arrays):
        if not one_plane_each(mesh, *arrays):
            return jax.shard_map(shards, mesh=mesh, in_specs=in_specs, out_specs=out_specs, check_vma=False)(*arrays)
        body = jax.shard_map(plane_shards, mesh=mesh, in_specs=in_specs, out_specs=out_specs, check_vma=False)
        return body(*arrays)

    return step
```

```python
import functools

import jax
import jax.numpy as jnp
from jax import lax
from jax.experimental import pallas as pl
from jax.experimental.pallas import tpu as pltpu
from jax.sharding import PartitionSpec as P


ITERS = 2
CAP = 4


TV_WEIGHT = 0.1
SMOOTH_SQUARE = 0.0025


def with_halo(cells, sides, width):
    for axis, dim in sides:
        count = lax.axis_size(axis)
        ends = count - 1
        head = lax.slice_in_dim(cells, 0, width, axis=dim)
        tail = lax.slice_in_dim(cells, cells.shape[dim] - width, cells.shape[dim], axis=dim)
        cells = jnp.concatenate(
            [
                lax.ppermute(tail, axis, [(i, (i + 1) % count) for i in range(ends)]),
                cells,
                lax.ppermute(head, axis, [((i + 1) % count, i) for i in range(ends)]),
            ],
            axis=dim,
        )
    return cells


def toeplitz_matrix(profile, length):
    half_width = (profile.shape[0] - 1) // 2
    position = jnp.arange(length, dtype=jnp.int32)
    offset = position[None, :] - position[:, None] + half_width
    tap_index = jnp.arange(profile.shape[0], dtype=jnp.int32)
    picked = (offset[:, :, None] == tap_index[None, None, :]).astype(jnp.float32)
    return jnp.sum(picked * profile[None, None, :], axis=2).astype(jnp.bfloat16)


def curvature(padded):
    anchor = padded[:-1, :-1, :-1]
    grad_z = padded[1:, :-1, :-1] - anchor
    grad_y = padded[:-1, 1:, :-1] - anchor
    grad_x = padded[:-1, :-1, 1:] - anchor
    magnitude = jnp.sqrt(grad_z * grad_z + grad_y * grad_y + grad_x * grad_x + SMOOTH_SQUARE)
    unit_z = grad_z / magnitude
    unit_y = grad_y / magnitude
    unit_x = grad_x / magnitude
    return (
        unit_z[1:, 1:, 1:]
        - unit_z[:-1, 1:, 1:]
        + (unit_y[1:, 1:, 1:] - unit_y[1:, :-1, 1:])
        + (unit_x[1:, 1:, 1:] - unit_x[1:, 1:, :-1])
    )


def view_correction(view_tile, observed, kernel_y, kernel_x):
    blurred = jnp.zeros(view_tile.shape, jnp.float32)
    for term_index in range(2):
        half_blur = jnp.einsum(
            "yk,zkx->zyx", kernel_y[term_index], view_tile, preferred_element_type=jnp.float32
        ).astype(jnp.bfloat16)
        blurred = blurred + jnp.einsum(
            "zyk,xk->zyx", half_blur, kernel_x[term_index], preferred_element_type=jnp.float32
        )
    quotient = (observed.astype(jnp.float32) / blurred).astype(jnp.bfloat16)
    log_sum = jnp.zeros(view_tile.shape, jnp.float32)
    for term_index in range(2):
        half_back = jnp.einsum(
            "ky,zkx->zyx", kernel_y[term_index], quotient, preferred_element_type=jnp.float32
        ).astype(jnp.bfloat16)
        log_sum = log_sum + jnp.einsum(
            "zyk,kx->zyx", half_back, kernel_x[term_index], preferred_element_type=jnp.float32
        )
    return log_sum.astype(jnp.bfloat16)


def shards(view_data, estimate, psf_taps, offsets):
    owners = lax.axis_size("tiles")
    view_count = lax.axis_size("views")
    observed = view_data[0, 0]
    planes, height, columns = estimate.shape
    view_shift = offsets[0]
    blocks = view_shift.shape[0]
    block_rows = height // blocks
    slot_count = owners * CAP
    kernel_y = jnp.stack(
        [toeplitz_matrix(psf_taps[0, term_index, 0], height) for term_index in range(2)]
    )
    kernel_x = jnp.stack(
        [toeplitz_matrix(psf_taps[0, term_index, 1], columns) for term_index in range(2)]
    )
    position = jnp.arange(blocks, dtype=jnp.int32)
    same_owner = view_shift[:, None] == view_shift[None, :]
    before = position[None, :] < position[:, None]
    slot_rank = jnp.sum((same_owner & before).astype(jnp.int32), axis=1)
    member = lax.axis_index("tiles")
    target = (member + view_shift) % owners
    source_tile = (member - view_shift) % owners
    slot_index = jnp.arange(slot_count, dtype=jnp.int32)
    to_owner = ((target * CAP + slot_rank)[:, None] == slot_index[None, :]).astype(jnp.bfloat16)
    from_tile = ((source_tile * CAP + slot_rank)[:, None] == slot_index[None, :]).astype(
        jnp.bfloat16
    )
    current = estimate
    for _ in range(ITERS):
        padded = with_halo(current, (("tiles", 1), ("gz", 0)), 1)
        padded = jnp.pad(padded, ((0, 0), (0, 0), (1, 1)))
        owned_blocks = current.astype(jnp.bfloat16).reshape(planes, blocks, block_rows, columns)
        outgoing = jnp.einsum(
            "sk,zsrx->kzrx", from_tile, owned_blocks, preferred_element_type=jnp.float32
        ).astype(jnp.bfloat16)
        incoming = lax.all_to_all(
            outgoing.reshape(owners, CAP, planes, block_rows, columns),
            "tiles",
            split_axis=0,
            concat_axis=0,
            tiled=True,
        )
        view_tile = jnp.einsum(
            "sk,kzrx->zsrx",
            to_owner,
            incoming.reshape(slot_count, planes, block_rows, columns),
            preferred_element_type=jnp.float32,
        ).astype(jnp.bfloat16)
        view_tile = view_tile.reshape(planes, height, columns)
        correction = view_correction(view_tile, observed, kernel_y, kernel_x)
        correction = correction.reshape(planes, blocks, block_rows, columns)
        returned = jnp.einsum(
            "sk,zsrx->kzrx", to_owner, correction, preferred_element_type=jnp.float32
        ).astype(jnp.bfloat16)
        gathered = lax.all_to_all(
            returned.reshape(owners, CAP, planes, block_rows, columns),
            "tiles",
            split_axis=0,
            concat_axis=0,
            tiled=True,
        )
        owned_rows = jnp.einsum(
            "sk,kzrx->zsrx",
            from_tile,
            gathered.reshape(slot_count, planes, block_rows, columns),
            preferred_element_type=jnp.float32,
        ).reshape(planes, height, columns)
        log_values = jnp.log(owned_rows)
        share_rows = height // view_count
        log_part = lax.psum_scatter(log_values, "views", scatter_dimension=1, tiled=True)
        first_row = lax.axis_index("views") * share_rows
        window = lax.dynamic_slice_in_dim(padded, first_row, share_rows + 2, 1)
        damping = 1.0 - TV_WEIGHT * curvature(window)
        rows_now = lax.dynamic_slice_in_dim(current, first_row, share_rows, 1)
        updated = rows_now * jnp.exp(log_part / view_count) / damping
        current = lax.all_gather(updated, "views", axis=1, tiled=True)
    return current


INFO_ROWS = 16
PLANE_UNIT = 65534.0
DATA_UNIT = 1024.0
TAP_UNIT = 8192.0
CHUNK = 32
VMEM = pl.BlockSpec(memory_space=pltpu.VMEM)
SMEM = pl.BlockSpec(memory_space=pltpu.SMEM)
LIMIT = pltpu.CompilerParams(vmem_limit_bytes=16 * 2**20)


def matrices_kernel(taps, info_ref, out_ref):
    views, columns = info_ref.shape
    length = out_ref.shape[-2] // 2
    half_width = (taps - 1) // 2
    row = lax.broadcasted_iota(jnp.int32, (length, columns), 0)
    column = lax.broadcasted_iota(jnp.int32, (length, columns), 1)
    band = jnp.abs(row - column) <= half_width
    for v in range(views):
        profile = jnp.broadcast_to(info_ref[v : v + 1, :], (8, columns))
        for kind, (flipped, axis) in enumerate([(0, 0), (1, 1), (1, 0), (0, 1)]):
            for r in range(2):
                lane = (4 * flipped + 2 * r + axis) * taps + half_width
                spread = jnp.broadcast_to(pltpu.roll(profile, columns - lane, 1)[0:1], (length, columns))
                rolled = pltpu.roll(spread, 0, 1, stride=1, stride_axis=0)
                rolled = jnp.where(band, rolled, 0.0).astype(out_ref.dtype)
                out_ref[v, kind, r * length : (r + 1) * length, :] = rolled


def blur_matrices(taps, length, info):
    views, columns = info.shape
    return pl.pallas_call(
        functools.partial(matrices_kernel, taps),
        out_shape=jax.ShapeDtypeStruct((views, 4, 2 * length, columns), jnp.bfloat16),
        in_specs=[VMEM],
        out_specs=VMEM,
        compiler_params=LIMIT,
        name="blur_matrices",
    )(info)


def correction_kernel(tiles, tile_ref, offsets_ref, current_ref, matrices_ref, *refs):
    views, blocks = offsets_ref.shape
    data, log_ref, work = refs[: views * tiles], refs[views * tiles], refs[views * tiles + 1 :]
    height, columns = data[0].shape
    rows = height // blocks
    me = tile_ref[0]
    shift = [[offsets_ref[w, s] for s in range(blocks)] for w in range(views)]
    planes = [work[3 * w] for w in range(views)]
    halves = [work[3 * w + 1] for w in range(views)]
    logs = [work[3 * w + 2] for w in range(views)]

    def first(w, kind):
        half = jnp.dot(matrices_ref[w, kind], planes[w][...], preferred_element_type=jnp.float32)
        half = half.astype(jnp.bfloat16)
        for k in range(tiles):
            for r in range(2):
                halves[w][k * height : (k + 1) * height, r * columns : (r + 1) * columns] = half[
                    r * height : (r + 1) * height, k * columns : (k + 1) * columns
                ]

    for w in range(views):
        for k in range(tiles):
            tile = lax.bitwise_xor(me, k)
            for s in range(blocks):
                owner = lax.rem(tile + shift[w][s], tiles)
                planes[w][s * rows : (s + 1) * rows, k * columns : (k + 1) * columns] = current_ref[
                    owner, s * rows : (s + 1) * rows, :
                ]
    for w in range(views):
        first(w, 0)
    for w in range(views):
        blurred = jnp.dot(halves[w][...], matrices_ref[w, 1], preferred_element_type=jnp.float32)
        for k in range(tiles):
            quotient = data[w * tiles + k][...].astype(jnp.float32) / blurred[k * height : (k + 1) * height]
            planes[w][:, k * columns : (k + 1) * columns] = quotient.astype(jnp.bfloat16)
    for w in range(views):
        first(w, 2)
    for w in range(views):
        back = jnp.dot(halves[w][...], matrices_ref[w, 3], preferred_element_type=jnp.float32)
        logs[w][...] = jnp.log(back.astype(jnp.bfloat16).astype(jnp.float32))
    for o in range(tiles):
        for s in range(blocks):
            total = None
            for w in range(views):
                tile = lax.rem(o - shift[w][s] + tiles, tiles)
                start = pl.multiple_of(lax.bitwise_xor(tile, me) * height + s * rows, rows)
                part = logs[w][pl.ds(start, rows), :]
                total = part if total is None else total + part
            log_ref[o * height + s * rows : o * height + (s + 1) * rows, :] = total


def correction_logs(tile, offsets, current, matrices, data):
    tiles, height, columns = current.shape
    scratch = [
        pltpu.VMEM((height, tiles * columns), jnp.bfloat16),
        pltpu.VMEM((tiles * height, 2 * columns), jnp.bfloat16),
        pltpu.VMEM((tiles * height, columns), jnp.float32),
    ]
    return pl.pallas_call(
        functools.partial(correction_kernel, tiles),
        out_shape=jax.ShapeDtypeStruct((tiles * height, columns), jnp.float32),
        in_specs=[SMEM, SMEM] + [VMEM] * (2 + len(data)),
        out_specs=VMEM,
        scratch_shapes=scratch * offsets.shape[0],
        cost_estimate=pl.CostEstimate(flops=300_000_000, bytes_accessed=1_500_000, transcendentals=0),
        compiler_params=LIMIT,
        name="correction",
    )(tile, offsets, current, matrices, *data)


def update_kernel(views, core_ref, current_ref, twin_ref, other_ref, log_ref, *new_refs):
    total, columns = current_ref.shape
    first = core_ref[0] == 0
    row = lax.broadcasted_iota(jnp.int32, (CHUNK, columns), 0)
    column = lax.broadcasted_iota(jnp.int32, (CHUNK, columns), 1)

    def scale(z, y, x):
        return lax.rsqrt(z * z + y * y + x * x + SMOOTH_SQUARE)

    def pick(low, high, start, size):
        return jnp.where(first, low[start : start + size, :], high[start : start + size, :])

    def next_row(x, following):
        return jnp.where(row == CHUNK - 1, following, pltpu.roll(x, CHUNK - 1, 0))

    def next_column(x):
        return jnp.where(column == columns - 1, 0.0, pltpu.roll(x, columns - 1, 1))

    def edge(x):
        return x * lax.rsqrt(x * x + SMOOTH_SQUARE)

    carry = edge(current_ref[0:1, :])
    for start in range(0, total, CHUNK):
        stop = start + CHUNK
        current = current_ref[start:stop, :]
        above = pick(twin_ref, other_ref, start, CHUNK)
        below = pick(other_ref, twin_ref, start, CHUNK)
        if stop < total:
            current_next, below_next = current_ref[stop : stop + 1, :], pick(other_ref, twin_ref, stop, 1)
        else:
            current_next = below_next = jnp.zeros((1, columns), jnp.float32)
        grad_z = above - current
        grad_y = next_row(current, current_next) - current
        grad_x = next_column(current) - current
        inverse = scale(grad_z, grad_y, grad_x)
        unit_y, unit_x = grad_y * inverse, grad_x * inverse
        before_y = jnp.where(row == 0, carry, pltpu.roll(unit_y, 1, 0))
        before_x = jnp.where(column == 0, edge(current), pltpu.roll(unit_x, 1, 1))
        carry = unit_y[CHUNK - 1 : CHUNK, :]
        lower_z = current - below
        lower = lower_z * scale(lower_z, next_row(below, below_next) - below, next_column(below) - below)
        divergence = grad_z * inverse - lower + (unit_y - before_y) + (unit_x - before_x)
        damping = 1.0 - TV_WEIGHT * divergence
        new = current * jnp.exp(log_ref[start:stop, :] * (1.0 / views)) / damping
        for ref in new_refs:
            ref[start:stop, :] = new.astype(ref.dtype)


def update(views, core, current, twin, other, logs, dtypes):
    return pl.pallas_call(
        functools.partial(update_kernel, views),
        out_shape=[jax.ShapeDtypeStruct(current.shape, dtype) for dtype in dtypes],
        in_specs=[SMEM] + [VMEM] * 4,
        out_specs=[VMEM] * len(dtypes),
        compiler_params=LIMIT,
        name="update",
    )(core, current, twin, other, logs)


def write_kernel(where_ref, *refs):
    sources, out_ref, sems = refs[:-2], refs[-2], refs[-1]
    tiles = out_ref.shape[0] // 2
    copies = []
    for parity, pair in enumerate((sources[:2], sources[2:])):
        q = where_ref[0] if parity == 0 else 1 - where_ref[0]
        for k in range(tiles):
            source = pair[0].at[0] if k == 0 else pair[1].at[k - 1]
            target = 2 * lax.bitwise_xor(where_ref[1], k) + q
            copies.append(pltpu.make_async_copy(source, out_ref.at[target], sems.at[parity, k]))
    for copy in copies:
        copy.start()
    for copy in copies:
        copy.wait()


def write_planes(where, sources):
    tiles = 1 + sources[1].shape[0]
    return pl.pallas_call(
        write_kernel,
        out_shape=jax.ShapeDtypeStruct((2 * tiles, *sources[0].shape[1:]), jnp.float32),
        in_specs=[SMEM] + [VMEM] * 4,
        out_specs=pl.BlockSpec(memory_space=pl.ANY),
        scratch_shapes=[pltpu.SemaphoreType.DMA((2, tiles))],
        compiler_params=LIMIT,
        name="write_planes",
    )(where, *sources)


def plane_shards(view_data, estimate, psf_taps, offsets):
    tiles, views = lax.axis_size("tiles"), lax.axis_size("views")
    square = ("tiles", "views", "gz")
    _, height, columns = estimate.shape
    blocks = offsets.shape[1]
    taps = psf_taps.shape[-1]
    tile, view, core = lax.axis_index("tiles"), lax.axis_index("views"), lax.axis_index("gz")
    swap = [(0, 1), (1, 0)]

    def device(t, v, g):
        return (t * views + v) * 2 + g

    def ordered(pieces, shift):
        placed = []
        for i in range(tiles):
            chosen = pieces[i]
            for s in range(1, tiles):
                chosen = jnp.where(shift == s, pieces[i ^ s], chosen)
            placed.append(chosen)
        return placed

    def exchange(pick):
        pieces = []
        for k in range(tiles):
            pairs = [(device(t, v, g), device(t ^ k, g, v)) for t in range(tiles) for v in range(2) for g in range(2)]
            pieces.append(lax.ppermute(pick(k), square, pairs))
        return pieces

    def end_of(chain):
        return jnp.where(chain == 0, 0, tiles - 1)

    me = tile.reshape(1).astype(jnp.int32)
    flag = core.reshape(1).astype(jnp.int32)

    wide = estimate.reshape(tiles, 2, height, columns)
    wide = lax.dynamic_index_in_dim(wide, view, 1, keepdims=True)
    wide = jnp.round((wide - 1.0) * PLANE_UNIT).astype(jnp.int16)
    data = view_data.reshape(tiles, 2, height, columns).astype(jnp.float32)
    data = (data * DATA_UNIT).astype(jnp.int16)
    payload = jnp.concatenate([wide, data], axis=1).reshape(tiles, 3 * height, columns)
    payload, psf_taps, offsets = lax.optimization_barrier((payload, psf_taps, offsets))

    def for_tile(k):
        place = lax.bitwise_xor(lax.bitwise_xor(tile, k), end_of(core))
        return lax.dynamic_index_in_dim(payload, place, 0, keepdims=False)

    pieces = exchange(for_tile)

    profiles = [psf_taps.reshape(-1), psf_taps[..., ::-1].reshape(-1)]
    info = [lax.reduce_precision(p, 8, 7) * TAP_UNIT for p in profiles]
    info = jnp.concatenate([*info, offsets.reshape(-1).astype(jnp.float32)])
    info = jnp.pad(info, (0, columns - info.shape[0])).astype(jnp.int16)
    info = jnp.broadcast_to(info, (INFO_ROWS, columns))
    note = lax.ppermute(info, "views", swap)
    straight = view == core
    notes = jnp.stack([jnp.where(straight, info[0], note[0]), jnp.where(straight, note[0], info[0])])
    notes = notes.astype(jnp.float32)
    shifts = notes[:, 8 * taps : 8 * taps + blocks].astype(jnp.int32)
    matrices = blur_matrices(taps, height, notes * (1.0 / TAP_UNIT))

    swapped = []
    for piece in pieces:
        swapped.append(lax.ppermute(piece, "gz", swap))

    def view_part(piece):
        part = lax.dynamic_slice_in_dim(piece, (1 + core) * height, height).astype(jnp.float32)
        return (part * (1.0 / DATA_UNIT)).astype(jnp.bfloat16)

    data = [view_part(piece) for piece in pieces]
    for piece in swapped:
        data.append(view_part(piece))

    path = [(t, 0) for t in range(tiles)] + [(t, 1) for t in reversed(range(tiles))]
    hops = []
    for here, there in zip(path[:-1], path[1:]):
        one, two = device(*here, 1), device(*there, 0)
        hops += [(one, two), (two, one)]

    def plane_of(coded):
        return coded.astype(jnp.float32) * (1.0 / PLANE_UNIT) + 1.0

    plane = jnp.concatenate(ordered([piece[:height] for piece in pieces], tile))
    twin = plane_of(jnp.concatenate(ordered([piece[:height] for piece in swapped], tile)))
    current = plane_of(plane)
    narrow = current.astype(jnp.bfloat16)
    at_end = (tile == 0) & (core == view)
    for iteration in range(ITERS):
        first, last = iteration == 0, iteration == ITERS - 1
        other = lax.ppermute(plane, square, hops)
        if not first:
            twin = lax.ppermute(current, "gz", swap)
        other = jnp.where(at_end, 0.0, plane_of(other) if first else other.astype(jnp.float32) + 1.0)
        logs = correction_logs(me, shifts, narrow.reshape(tiles, height, columns), matrices, data)
        current, *rest = update(
            views, flag, current, twin, other, logs, [jnp.float32] if last else [jnp.float32, jnp.bfloat16]
        )
        if not last:
            narrow = rest[0]
            plane = (current - 1.0).astype(jnp.float16)

    result = current.astype(jnp.float16).reshape(tiles, height, columns)
    pieces = []
    for k in range(tiles):
        piece = lax.dynamic_index_in_dim(result, lax.bitwise_xor(tile, k), 0)
        pieces.append(lax.ppermute(piece, "tiles", [(t, t ^ k) for t in range(tiles)]) if k else piece)
    mine = jnp.concatenate(pieces)
    crossed = [lax.ppermute(pieces[0], "views", swap)]
    crossed.append(lax.ppermute(mine[1:], "views", swap))
    halves = [mine[:1], mine[1:]]
    twins = [lax.ppermute(jnp.where(straight, c, m), "gz", swap) for c, m in zip(crossed, halves)]
    same = [jnp.where(straight, m, c).astype(jnp.float32) for c, m in zip(crossed, halves)]
    twins = [x.astype(jnp.float32) for x in twins]
    where = jnp.stack([core, lax.bitwise_xor(tile, end_of(core))]).astype(jnp.int32)
    return write_planes(where, same + twins)


def one_plane_each(mesh, view_data, estimate, psf_taps, offsets):
    tiles, views, depth = mesh.shape["tiles"], mesh.shape["views"], mesh.shape["gz"]
    planes = estimate.shape[0] // (mesh.shape["groups"] * depth)
    height, columns = estimate.shape[1] // tiles, estimate.shape[2]
    return (
        depth == 2
        and views == 2
        and planes == 2 * tiles
        and tiles & (tiles - 1) == 0
        and height == columns
        and height % (16 * offsets.shape[1]) == 0
        and columns == 128
        and 8 * psf_taps.shape[-1] + offsets.shape[1] <= columns
    )


def solution(mesh):
    in_specs = (
        P(("groups", "views"), "tiles", "gz", None, None),
        P(("groups", "gz"), "tiles", None),
        P("views", None, None, None),
        P("views", None),
    )
    out_specs = P(("groups", "gz"), "tiles", None)

    def step(*arrays):
        if not one_plane_each(mesh, *arrays):
            return jax.shard_map(shards, mesh=mesh, in_specs=in_specs, out_specs=out_specs, check_vma=False)(*arrays)
        body = jax.shard_map(plane_shards, mesh=mesh, in_specs=in_specs, out_specs=out_specs, check_vma=False)
        return body(*arrays)

    return step
```

```python
import functools

import jax
import jax.numpy as jnp
from jax import lax
from jax.experimental import pallas as pl
from jax.experimental.pallas import tpu as pltpu
from jax.sharding import PartitionSpec as P


ITERS = 2
CAP = 4


TV_WEIGHT = 0.1
SMOOTH_SQUARE = 0.0025


def with_halo(cells, sides, width):
    for axis, dim in sides:
        count = lax.axis_size(axis)
        ends = count - 1
        head = lax.slice_in_dim(cells, 0, width, axis=dim)
        tail = lax.slice_in_dim(cells, cells.shape[dim] - width, cells.shape[dim], axis=dim)
        cells = jnp.concatenate(
            [
                lax.ppermute(tail, axis, [(i, (i + 1) % count) for i in range(ends)]),
                cells,
                lax.ppermute(head, axis, [((i + 1) % count, i) for i in range(ends)]),
            ],
            axis=dim,
        )
    return cells


def toeplitz_matrix(profile, length):
    half_width = (profile.shape[0] - 1) // 2
    position = jnp.arange(length, dtype=jnp.int32)
    offset = position[None, :] - position[:, None] + half_width
    tap_index = jnp.arange(profile.shape[0], dtype=jnp.int32)
    picked = (offset[:, :, None] == tap_index[None, None, :]).astype(jnp.float32)
    return jnp.sum(picked * profile[None, None, :], axis=2).astype(jnp.bfloat16)


def curvature(padded):
    anchor = padded[:-1, :-1, :-1]
    grad_z = padded[1:, :-1, :-1] - anchor
    grad_y = padded[:-1, 1:, :-1] - anchor
    grad_x = padded[:-1, :-1, 1:] - anchor
    magnitude = jnp.sqrt(grad_z * grad_z + grad_y * grad_y + grad_x * grad_x + SMOOTH_SQUARE)
    unit_z = grad_z / magnitude
    unit_y = grad_y / magnitude
    unit_x = grad_x / magnitude
    return (
        unit_z[1:, 1:, 1:]
        - unit_z[:-1, 1:, 1:]
        + (unit_y[1:, 1:, 1:] - unit_y[1:, :-1, 1:])
        + (unit_x[1:, 1:, 1:] - unit_x[1:, 1:, :-1])
    )


def view_correction(view_tile, observed, kernel_y, kernel_x):
    blurred = jnp.zeros(view_tile.shape, jnp.float32)
    for term_index in range(2):
        half_blur = jnp.einsum(
            "yk,zkx->zyx", kernel_y[term_index], view_tile, preferred_element_type=jnp.float32
        ).astype(jnp.bfloat16)
        blurred = blurred + jnp.einsum(
            "zyk,xk->zyx", half_blur, kernel_x[term_index], preferred_element_type=jnp.float32
        )
    quotient = (observed.astype(jnp.float32) / blurred).astype(jnp.bfloat16)
    log_sum = jnp.zeros(view_tile.shape, jnp.float32)
    for term_index in range(2):
        half_back = jnp.einsum(
            "ky,zkx->zyx", kernel_y[term_index], quotient, preferred_element_type=jnp.float32
        ).astype(jnp.bfloat16)
        log_sum = log_sum + jnp.einsum(
            "zyk,kx->zyx", half_back, kernel_x[term_index], preferred_element_type=jnp.float32
        )
    return log_sum.astype(jnp.bfloat16)


def shards(view_data, estimate, psf_taps, offsets):
    owners = lax.axis_size("tiles")
    view_count = lax.axis_size("views")
    observed = view_data[0, 0]
    planes, height, columns = estimate.shape
    view_shift = offsets[0]
    blocks = view_shift.shape[0]
    block_rows = height // blocks
    slot_count = owners * CAP
    kernel_y = jnp.stack(
        [toeplitz_matrix(psf_taps[0, term_index, 0], height) for term_index in range(2)]
    )
    kernel_x = jnp.stack(
        [toeplitz_matrix(psf_taps[0, term_index, 1], columns) for term_index in range(2)]
    )
    position = jnp.arange(blocks, dtype=jnp.int32)
    same_owner = view_shift[:, None] == view_shift[None, :]
    before = position[None, :] < position[:, None]
    slot_rank = jnp.sum((same_owner & before).astype(jnp.int32), axis=1)
    member = lax.axis_index("tiles")
    target = (member + view_shift) % owners
    source_tile = (member - view_shift) % owners
    slot_index = jnp.arange(slot_count, dtype=jnp.int32)
    to_owner = ((target * CAP + slot_rank)[:, None] == slot_index[None, :]).astype(jnp.bfloat16)
    from_tile = ((source_tile * CAP + slot_rank)[:, None] == slot_index[None, :]).astype(
        jnp.bfloat16
    )
    current = estimate
    for _ in range(ITERS):
        padded = with_halo(current, (("tiles", 1), ("gz", 0)), 1)
        padded = jnp.pad(padded, ((0, 0), (0, 0), (1, 1)))
        owned_blocks = current.astype(jnp.bfloat16).reshape(planes, blocks, block_rows, columns)
        outgoing = jnp.einsum(
            "sk,zsrx->kzrx", from_tile, owned_blocks, preferred_element_type=jnp.float32
        ).astype(jnp.bfloat16)
        incoming = lax.all_to_all(
            outgoing.reshape(owners, CAP, planes, block_rows, columns),
            "tiles",
            split_axis=0,
            concat_axis=0,
            tiled=True,
        )
        view_tile = jnp.einsum(
            "sk,kzrx->zsrx",
            to_owner,
            incoming.reshape(slot_count, planes, block_rows, columns),
            preferred_element_type=jnp.float32,
        ).astype(jnp.bfloat16)
        view_tile = view_tile.reshape(planes, height, columns)
        correction = view_correction(view_tile, observed, kernel_y, kernel_x)
        correction = correction.reshape(planes, blocks, block_rows, columns)
        returned = jnp.einsum(
            "sk,zsrx->kzrx", to_owner, correction, preferred_element_type=jnp.float32
        ).astype(jnp.bfloat16)
        gathered = lax.all_to_all(
            returned.reshape(owners, CAP, planes, block_rows, columns),
            "tiles",
            split_axis=0,
            concat_axis=0,
            tiled=True,
        )
        owned_rows = jnp.einsum(
            "sk,kzrx->zsrx",
            from_tile,
            gathered.reshape(slot_count, planes, block_rows, columns),
            preferred_element_type=jnp.float32,
        ).reshape(planes, height, columns)
        log_values = jnp.log(owned_rows)
        share_rows = height // view_count
        log_part = lax.psum_scatter(log_values, "views", scatter_dimension=1, tiled=True)
        first_row = lax.axis_index("views") * share_rows
        window = lax.dynamic_slice_in_dim(padded, first_row, share_rows + 2, 1)
        damping = 1.0 - TV_WEIGHT * curvature(window)
        rows_now = lax.dynamic_slice_in_dim(current, first_row, share_rows, 1)
        updated = rows_now * jnp.exp(log_part / view_count) / damping
        current = lax.all_gather(updated, "views", axis=1, tiled=True)
    return current


INFO_ROWS = 16
PLANE_UNIT = 65534.0
DATA_UNIT = 1024.0
TAP_UNIT = 8192.0
CHUNK = 32
VMEM = pl.BlockSpec(memory_space=pltpu.VMEM)
SMEM = pl.BlockSpec(memory_space=pltpu.SMEM)
LIMIT = pltpu.CompilerParams(vmem_limit_bytes=16 * 2**20)


def matrices_kernel(taps, info_ref, out_ref):
    views, columns = info_ref.shape
    length = out_ref.shape[-2] // 2
    half_width = (taps - 1) // 2
    row = lax.broadcasted_iota(jnp.int32, (length, columns), 0)
    column = lax.broadcasted_iota(jnp.int32, (length, columns), 1)
    band = jnp.abs(row - column) <= half_width
    for v in range(views):
        profile = jnp.broadcast_to(info_ref[v : v + 1, :], (8, columns))
        for kind, (flipped, axis) in enumerate([(0, 0), (1, 1), (1, 0), (0, 1)]):
            for r in range(2):
                lane = (4 * flipped + 2 * r + axis) * taps + half_width
                spread = jnp.broadcast_to(pltpu.roll(profile, columns - lane, 1)[0:1], (length, columns))
                rolled = pltpu.roll(spread, 0, 1, stride=1, stride_axis=0)
                rolled = jnp.where(band, rolled, 0.0).astype(out_ref.dtype)
                out_ref[v, kind, r * length : (r + 1) * length, :] = rolled


def blur_matrices(taps, length, info):
    views, columns = info.shape
    return pl.pallas_call(
        functools.partial(matrices_kernel, taps),
        out_shape=jax.ShapeDtypeStruct((views, 4, 2 * length, columns), jnp.bfloat16),
        in_specs=[VMEM],
        out_specs=VMEM,
        compiler_params=LIMIT,
        name="blur_matrices",
    )(info)


def pack_kernel(where_ref, *refs):
    pieces, (plane_ref, give_ref) = refs[:-2], refs[-2:]
    height = plane_ref.shape[1]
    other = pl.multiple_of((2 - where_ref[1]) * height, height)
    for k, piece in enumerate(pieces):
        plane = piece[0:height, :]
        plane_ref[lax.bitwise_xor(where_ref[0], k)] = plane
        give_ref[k, 0] = plane
        give_ref[k, 1] = piece[pl.ds(other, height), :]


def pack(where, pieces):
    rows, columns = pieces[0].shape
    shape = (len(pieces), rows // 3, columns)
    return pl.pallas_call(
        pack_kernel,
        out_shape=[
            jax.ShapeDtypeStruct(shape, pieces[0].dtype),
            jax.ShapeDtypeStruct((shape[0], 2, *shape[1:]), pieces[0].dtype),
        ],
        in_specs=[SMEM] + [VMEM] * len(pieces),
        out_specs=[VMEM] * 2,
        compiler_params=LIMIT,
        name="pack",
    )(where, *pieces)


def correction_kernel(where_ref, offsets_ref, current_ref, matrices_ref, *refs):
    views, blocks = offsets_ref.shape
    tiles, height, columns = current_ref.shape
    pieces, swapped_ref, log_ref, work = refs[:tiles], refs[tiles], refs[tiles + 1], refs[tiles + 2 :]
    rows = height // blocks
    me = where_ref[0]
    own = pl.multiple_of((1 + where_ref[1]) * height, height)
    shift = [[offsets_ref[w, s] for s in range(blocks)] for w in range(views)]
    planes = [work[3 * w] for w in range(views)]
    halves = [work[3 * w + 1] for w in range(views)]
    logs = [work[3 * w + 2] for w in range(views)]

    def first(w, kind):
        half = jnp.dot(matrices_ref[w, kind], planes[w][...], preferred_element_type=jnp.float32)
        half = half.astype(jnp.bfloat16)
        for k in range(tiles):
            for r in range(2):
                halves[w][k * height : (k + 1) * height, r * columns : (r + 1) * columns] = half[
                    r * height : (r + 1) * height, k * columns : (k + 1) * columns
                ]

    for w in range(views):
        for k in range(tiles):
            tile = lax.bitwise_xor(me, k)
            for s in range(blocks):
                owner = lax.rem(tile + shift[w][s], tiles)
                planes[w][s * rows : (s + 1) * rows, k * columns : (k + 1) * columns] = current_ref[
                    owner, s * rows : (s + 1) * rows, :
                ]
    for w in range(views):
        first(w, 0)
    for w in range(views):
        blurred = jnp.dot(halves[w][...], matrices_ref[w, 1], preferred_element_type=jnp.float32)
        for k in range(tiles):
            observed = pieces[k][pl.ds(own, height), :] if w == 0 else swapped_ref[k, 1]
            observed = observed.astype(jnp.float32) * (1.0 / DATA_UNIT)
            quotient = observed / blurred[k * height : (k + 1) * height]
            planes[w][:, k * columns : (k + 1) * columns] = quotient.astype(jnp.bfloat16)
    for w in range(views):
        first(w, 2)
    for w in range(views):
        back = jnp.dot(halves[w][...], matrices_ref[w, 3], preferred_element_type=jnp.float32)
        logs[w][...] = jnp.log(back.astype(jnp.bfloat16).astype(jnp.float32))
    for o in range(tiles):
        for s in range(blocks):
            total = None
            for w in range(views):
                tile = lax.rem(o - shift[w][s] + tiles, tiles)
                start = pl.multiple_of(lax.bitwise_xor(tile, me) * height + s * rows, rows)
                part = logs[w][pl.ds(start, rows), :]
                total = part if total is None else total + part
            log_ref[o * height + s * rows : o * height + (s + 1) * rows, :] = total


def correction_logs(where, offsets, current, matrices, pieces, swapped):
    tiles, height, columns = current.shape
    scratch = [
        pltpu.VMEM((height, tiles * columns), jnp.bfloat16),
        pltpu.VMEM((tiles * height, 2 * columns), jnp.bfloat16),
        pltpu.VMEM((tiles * height, columns), jnp.float32),
    ]
    return pl.pallas_call(
        correction_kernel,
        out_shape=jax.ShapeDtypeStruct((tiles * height, columns), jnp.float32),
        in_specs=[SMEM, SMEM] + [VMEM] * (3 + tiles),
        out_specs=VMEM,
        scratch_shapes=scratch * offsets.shape[0],
        cost_estimate=pl.CostEstimate(flops=300_000_000, bytes_accessed=1_500_000, transcendentals=0),
        compiler_params=LIMIT,
        name="correction",
    )(where, offsets, current, matrices, *pieces, swapped)


def update_kernel(views, core_ref, current_ref, twin_ref, other_ref, log_ref, *new_refs):
    total, columns = current_ref.shape
    first = core_ref[0] == 0
    row = lax.broadcasted_iota(jnp.int32, (CHUNK, columns), 0)
    column = lax.broadcasted_iota(jnp.int32, (CHUNK, columns), 1)

    def scale(z, y, x):
        return lax.rsqrt(z * z + y * y + x * x + SMOOTH_SQUARE)

    def pick(low, high, start, size):
        return jnp.where(first, low[start : start + size, :], high[start : start + size, :])

    def next_row(x, following):
        return jnp.where(row == CHUNK - 1, following, pltpu.roll(x, CHUNK - 1, 0))

    def next_column(x):
        return jnp.where(column == columns - 1, 0.0, pltpu.roll(x, columns - 1, 1))

    def edge(x):
        return x * lax.rsqrt(x * x + SMOOTH_SQUARE)

    carry = edge(current_ref[0:1, :])
    for start in range(0, total, CHUNK):
        stop = start + CHUNK
        current = current_ref[start:stop, :]
        above = pick(twin_ref, other_ref, start, CHUNK)
        below = pick(other_ref, twin_ref, start, CHUNK)
        if stop < total:
            current_next, below_next = current_ref[stop : stop + 1, :], pick(other_ref, twin_ref, stop, 1)
        else:
            current_next = below_next = jnp.zeros((1, columns), jnp.float32)
        grad_z = above - current
        grad_y = next_row(current, current_next) - current
        grad_x = next_column(current) - current
        inverse = scale(grad_z, grad_y, grad_x)
        unit_y, unit_x = grad_y * inverse, grad_x * inverse
        before_y = jnp.where(row == 0, carry, pltpu.roll(unit_y, 1, 0))
        before_x = jnp.where(column == 0, edge(current), pltpu.roll(unit_x, 1, 1))
        carry = unit_y[CHUNK - 1 : CHUNK, :]
        lower_z = current - below
        lower = lower_z * scale(lower_z, next_row(below, below_next) - below, next_column(below) - below)
        divergence = grad_z * inverse - lower + (unit_y - before_y) + (unit_x - before_x)
        damping = 1.0 - TV_WEIGHT * divergence
        new = current * jnp.exp(log_ref[start:stop, :] * (1.0 / views)) / damping
        for ref in new_refs:
            ref[start:stop, :] = new.astype(ref.dtype)


def update(views, core, current, twin, other, logs, dtypes):
    return pl.pallas_call(
        functools.partial(update_kernel, views),
        out_shape=[jax.ShapeDtypeStruct(current.shape, dtype) for dtype in dtypes],
        in_specs=[SMEM] + [VMEM] * 4,
        out_specs=[VMEM] * len(dtypes),
        compiler_params=LIMIT,
        name="update",
    )(core, current, twin, other, logs)


def plane_shards(view_data, estimate, psf_taps, offsets):
    tiles, views = lax.axis_size("tiles"), lax.axis_size("views")
    square = ("tiles", "views", "gz")
    _, height, columns = estimate.shape
    blocks = offsets.shape[1]
    taps = psf_taps.shape[-1]
    tile, view, core = lax.axis_index("tiles"), lax.axis_index("views"), lax.axis_index("gz")
    swap = [(0, 1), (1, 0)]

    def device(t, v, g):
        return (t * views + v) * 2 + g

    def ordered(pieces, shift):
        placed = []
        for i in range(tiles):
            chosen = pieces[i]
            for s in range(1, tiles):
                chosen = jnp.where(shift == s, pieces[i ^ s], chosen)
            placed.append(chosen)
        return placed

    def exchange(pick):
        pieces = []
        for k in range(tiles):
            pairs = [(device(t, v, g), device(t ^ k, g, v)) for t in range(tiles) for v in range(2) for g in range(2)]
            pieces.append(lax.ppermute(pick(k), square, pairs))
        return pieces

    def end_of(chain):
        return jnp.where(chain == 0, 0, tiles - 1)

    where = jnp.stack([tile, core]).astype(jnp.int32)
    flag = core.reshape(1).astype(jnp.int32)

    wide = estimate.reshape(tiles, 2, height, columns)
    wide = lax.dynamic_index_in_dim(wide, view, 1, keepdims=True)
    wide = jnp.round((wide - 1.0) * PLANE_UNIT).astype(jnp.int16)
    data = view_data.reshape(tiles, 2, height, columns).astype(jnp.float32)
    data = (data * DATA_UNIT).astype(jnp.int16)
    payload = jnp.concatenate([wide, data], axis=1).reshape(tiles, 3 * height, columns)
    payload, psf_taps, offsets = lax.optimization_barrier((payload, psf_taps, offsets))

    def for_tile(k):
        place = lax.bitwise_xor(lax.bitwise_xor(tile, k), end_of(core))
        return lax.dynamic_index_in_dim(payload, place, 0, keepdims=False)

    pieces = exchange(for_tile)

    profiles = [psf_taps.reshape(-1), psf_taps[..., ::-1].reshape(-1)]
    info = [lax.reduce_precision(p, 8, 7) * TAP_UNIT for p in profiles]
    info = jnp.concatenate([*info, offsets.reshape(-1).astype(jnp.float32)])
    info = jnp.pad(info, (0, columns - info.shape[0])).astype(jnp.int16)
    info = jnp.broadcast_to(info, (INFO_ROWS, columns))
    note = lax.ppermute(info, "views", swap)
    straight = view == core
    notes = jnp.stack([jnp.where(straight, info[0], note[0]), jnp.where(straight, note[0], info[0])])
    notes = notes.astype(jnp.float32)
    shifts = notes[:, 8 * taps : 8 * taps + blocks].astype(jnp.int32)
    matrices = blur_matrices(taps, height, notes * (1.0 / TAP_UNIT))

    plane, give = pack(where, pieces)
    swapped = lax.ppermute(give, "gz", swap)

    path = [(t, 0) for t in range(tiles)] + [(t, 1) for t in reversed(range(tiles))]
    hops = []
    for here, there in zip(path[:-1], path[1:]):
        one, two = device(*here, 1), device(*there, 0)
        hops += [(one, two), (two, one)]

    def plane_of(coded):
        return coded.astype(jnp.float32) * (1.0 / PLANE_UNIT) + 1.0

    plane = plane.reshape(tiles * height, columns)
    twin = plane_of(jnp.concatenate(ordered([swapped[k, 0] for k in range(tiles)], tile)))
    current = plane_of(plane)
    narrow = current.astype(jnp.bfloat16)
    at_end = (tile == 0) & (core == view)
    for iteration in range(ITERS):
        first, last = iteration == 0, iteration == ITERS - 1
        other = lax.ppermute(plane, square, hops)
        if not first:
            twin = lax.ppermute(current, "gz", swap)
        other = jnp.where(at_end, 0.0, plane_of(other) if first else other.astype(jnp.float32) + 1.0)
        logs = correction_logs(where, shifts, narrow.reshape(tiles, height, columns), matrices, pieces, swapped)
        current, *rest = update(
            views, flag, current, twin, other, logs, [jnp.float32] if last else [jnp.float32, jnp.bfloat16]
        )
        if not last:
            narrow = rest[0]
            plane = (current - 1.0).astype(jnp.float16)

    result = current.astype(jnp.float16).reshape(tiles, height, columns)
    pieces = []
    for k in range(tiles):
        piece = lax.dynamic_index_in_dim(result, lax.bitwise_xor(tile, k), 0)
        pieces.append(lax.ppermute(piece, "tiles", [(t, t ^ k) for t in range(tiles)]) if k else piece)
    mine = jnp.concatenate(pieces)
    crossed = [lax.ppermute(pieces[0], "views", swap)]
    crossed.append(lax.ppermute(mine[1:], "views", swap))
    crossed = jnp.concatenate(crossed)
    same = jnp.where(straight, mine, crossed)
    twin = lax.ppermute(jnp.where(straight, crossed, mine), "gz", swap)
    even, odd = jnp.where(core == 0, same, twin), jnp.where(core == 0, twin, same)
    result = [jnp.stack([even[k], odd[k]]) for k in range(tiles)]
    result = jnp.concatenate(ordered(result, lax.bitwise_xor(tile, end_of(core))))
    return result.astype(jnp.float32)


def one_plane_each(mesh, view_data, estimate, psf_taps, offsets):
    tiles, views, depth = mesh.shape["tiles"], mesh.shape["views"], mesh.shape["gz"]
    planes = estimate.shape[0] // (mesh.shape["groups"] * depth)
    height, columns = estimate.shape[1] // tiles, estimate.shape[2]
    return (
        depth == 2
        and views == 2
        and planes == 2 * tiles
        and tiles & (tiles - 1) == 0
        and height == columns
        and height % (16 * offsets.shape[1]) == 0
        and columns == 128
        and 8 * psf_taps.shape[-1] + offsets.shape[1] <= columns
    )


def solution(mesh):
    in_specs = (
        P(("groups", "views"), "tiles", "gz", None, None),
        P(("groups", "gz"), "tiles", None),
        P("views", None, None, None),
        P("views", None),
    )
    out_specs = P(("groups", "gz"), "tiles", None)

    def step(*arrays):
        if not one_plane_each(mesh, *arrays):
            return jax.shard_map(shards, mesh=mesh, in_specs=in_specs, out_specs=out_specs, check_vma=False)(*arrays)
        body = jax.shard_map(plane_shards, mesh=mesh, in_specs=in_specs, out_specs=out_specs, check_vma=False)
        return body(*arrays)

    return step
```

```python
import functools

import jax
import jax.numpy as jnp
from jax import lax
from jax.experimental import pallas as pl
from jax.experimental.pallas import tpu as pltpu
from jax.sharding import PartitionSpec as P


ITERS = 2
CAP = 4


TV_WEIGHT = 0.1
SMOOTH_SQUARE = 0.0025


def with_halo(cells, sides, width):
    for axis, dim in sides:
        count = lax.axis_size(axis)
        ends = count - 1
        head = lax.slice_in_dim(cells, 0, width, axis=dim)
        tail = lax.slice_in_dim(cells, cells.shape[dim] - width, cells.shape[dim], axis=dim)
        cells = jnp.concatenate(
            [
                lax.ppermute(tail, axis, [(i, (i + 1) % count) for i in range(ends)]),
                cells,
                lax.ppermute(head, axis, [((i + 1) % count, i) for i in range(ends)]),
            ],
            axis=dim,
        )
    return cells


def toeplitz_matrix(profile, length):
    half_width = (profile.shape[0] - 1) // 2
    position = jnp.arange(length, dtype=jnp.int32)
    offset = position[None, :] - position[:, None] + half_width
    tap_index = jnp.arange(profile.shape[0], dtype=jnp.int32)
    picked = (offset[:, :, None] == tap_index[None, None, :]).astype(jnp.float32)
    return jnp.sum(picked * profile[None, None, :], axis=2).astype(jnp.bfloat16)


def curvature(padded):
    anchor = padded[:-1, :-1, :-1]
    grad_z = padded[1:, :-1, :-1] - anchor
    grad_y = padded[:-1, 1:, :-1] - anchor
    grad_x = padded[:-1, :-1, 1:] - anchor
    magnitude = jnp.sqrt(grad_z * grad_z + grad_y * grad_y + grad_x * grad_x + SMOOTH_SQUARE)
    unit_z = grad_z / magnitude
    unit_y = grad_y / magnitude
    unit_x = grad_x / magnitude
    return (
        unit_z[1:, 1:, 1:]
        - unit_z[:-1, 1:, 1:]
        + (unit_y[1:, 1:, 1:] - unit_y[1:, :-1, 1:])
        + (unit_x[1:, 1:, 1:] - unit_x[1:, 1:, :-1])
    )


def view_correction(view_tile, observed, kernel_y, kernel_x):
    blurred = jnp.zeros(view_tile.shape, jnp.float32)
    for term_index in range(2):
        half_blur = jnp.einsum(
            "yk,zkx->zyx", kernel_y[term_index], view_tile, preferred_element_type=jnp.float32
        ).astype(jnp.bfloat16)
        blurred = blurred + jnp.einsum(
            "zyk,xk->zyx", half_blur, kernel_x[term_index], preferred_element_type=jnp.float32
        )
    quotient = (observed.astype(jnp.float32) / blurred).astype(jnp.bfloat16)
    log_sum = jnp.zeros(view_tile.shape, jnp.float32)
    for term_index in range(2):
        half_back = jnp.einsum(
            "ky,zkx->zyx", kernel_y[term_index], quotient, preferred_element_type=jnp.float32
        ).astype(jnp.bfloat16)
        log_sum = log_sum + jnp.einsum(
            "zyk,kx->zyx", half_back, kernel_x[term_index], preferred_element_type=jnp.float32
        )
    return log_sum.astype(jnp.bfloat16)


def shards(view_data, estimate, psf_taps, offsets):
    owners = lax.axis_size("tiles")
    view_count = lax.axis_size("views")
    observed = view_data[0, 0]
    planes, height, columns = estimate.shape
    view_shift = offsets[0]
    blocks = view_shift.shape[0]
    block_rows = height // blocks
    slot_count = owners * CAP
    kernel_y = jnp.stack(
        [toeplitz_matrix(psf_taps[0, term_index, 0], height) for term_index in range(2)]
    )
    kernel_x = jnp.stack(
        [toeplitz_matrix(psf_taps[0, term_index, 1], columns) for term_index in range(2)]
    )
    position = jnp.arange(blocks, dtype=jnp.int32)
    same_owner = view_shift[:, None] == view_shift[None, :]
    before = position[None, :] < position[:, None]
    slot_rank = jnp.sum((same_owner & before).astype(jnp.int32), axis=1)
    member = lax.axis_index("tiles")
    target = (member + view_shift) % owners
    source_tile = (member - view_shift) % owners
    slot_index = jnp.arange(slot_count, dtype=jnp.int32)
    to_owner = ((target * CAP + slot_rank)[:, None] == slot_index[None, :]).astype(jnp.bfloat16)
    from_tile = ((source_tile * CAP + slot_rank)[:, None] == slot_index[None, :]).astype(
        jnp.bfloat16
    )
    current = estimate
    for _ in range(ITERS):
        padded = with_halo(current, (("tiles", 1), ("gz", 0)), 1)
        padded = jnp.pad(padded, ((0, 0), (0, 0), (1, 1)))
        owned_blocks = current.astype(jnp.bfloat16).reshape(planes, blocks, block_rows, columns)
        outgoing = jnp.einsum(
            "sk,zsrx->kzrx", from_tile, owned_blocks, preferred_element_type=jnp.float32
        ).astype(jnp.bfloat16)
        incoming = lax.all_to_all(
            outgoing.reshape(owners, CAP, planes, block_rows, columns),
            "tiles",
            split_axis=0,
            concat_axis=0,
            tiled=True,
        )
        view_tile = jnp.einsum(
            "sk,kzrx->zsrx",
            to_owner,
            incoming.reshape(slot_count, planes, block_rows, columns),
            preferred_element_type=jnp.float32,
        ).astype(jnp.bfloat16)
        view_tile = view_tile.reshape(planes, height, columns)
        correction = view_correction(view_tile, observed, kernel_y, kernel_x)
        correction = correction.reshape(planes, blocks, block_rows, columns)
        returned = jnp.einsum(
            "sk,zsrx->kzrx", to_owner, correction, preferred_element_type=jnp.float32
        ).astype(jnp.bfloat16)
        gathered = lax.all_to_all(
            returned.reshape(owners, CAP, planes, block_rows, columns),
            "tiles",
            split_axis=0,
            concat_axis=0,
            tiled=True,
        )
        owned_rows = jnp.einsum(
            "sk,kzrx->zsrx",
            from_tile,
            gathered.reshape(slot_count, planes, block_rows, columns),
            preferred_element_type=jnp.float32,
        ).reshape(planes, height, columns)
        log_values = jnp.log(owned_rows)
        share_rows = height // view_count
        log_part = lax.psum_scatter(log_values, "views", scatter_dimension=1, tiled=True)
        first_row = lax.axis_index("views") * share_rows
        window = lax.dynamic_slice_in_dim(padded, first_row, share_rows + 2, 1)
        damping = 1.0 - TV_WEIGHT * curvature(window)
        rows_now = lax.dynamic_slice_in_dim(current, first_row, share_rows, 1)
        updated = rows_now * jnp.exp(log_part / view_count) / damping
        current = lax.all_gather(updated, "views", axis=1, tiled=True)
    return current


INFO_ROWS = 16
PLANE_UNIT = 65534.0
DATA_UNIT = 1024.0
TAP_UNIT = 8192.0
CHUNK = 32
VMEM = pl.BlockSpec(memory_space=pltpu.VMEM)
SMEM = pl.BlockSpec(memory_space=pltpu.SMEM)
LIMIT = pltpu.CompilerParams(vmem_limit_bytes=16 * 2**20)


def matrices_kernel(taps, info_ref, out_ref):
    views, columns = info_ref.shape
    length = out_ref.shape[-2] // 2
    half_width = (taps - 1) // 2
    row = lax.broadcasted_iota(jnp.int32, (length, columns), 0)
    column = lax.broadcasted_iota(jnp.int32, (length, columns), 1)
    band = jnp.abs(row - column) <= half_width
    for v in range(views):
        profile = jnp.broadcast_to(info_ref[v : v + 1, :], (8, columns))
        for kind, (flipped, axis) in enumerate([(0, 0), (1, 1), (1, 0), (0, 1)]):
            for r in range(2):
                lane = (4 * flipped + 2 * r + axis) * taps + half_width
                spread = jnp.broadcast_to(pltpu.roll(profile, columns - lane, 1)[0:1], (length, columns))
                rolled = pltpu.roll(spread, 0, 1, stride=1, stride_axis=0)
                rolled = jnp.where(band, rolled, 0.0).astype(out_ref.dtype)
                out_ref[v, kind, r * length : (r + 1) * length, :] = rolled


def blur_matrices(taps, length, info):
    views, columns = info.shape
    return pl.pallas_call(
        functools.partial(matrices_kernel, taps),
        out_shape=jax.ShapeDtypeStruct((views, 4, 2 * length, columns), jnp.bfloat16),
        in_specs=[VMEM],
        out_specs=VMEM,
        compiler_params=LIMIT,
        name="blur_matrices",
    )(info)


def correction_kernel(tiles, tile_ref, offsets_ref, current_ref, matrices_ref, *refs):
    views, blocks = offsets_ref.shape
    data, log_ref, work = refs[: views * tiles], refs[views * tiles], refs[views * tiles + 1 :]
    height, columns = data[0].shape
    rows = height // blocks
    me = tile_ref[0]
    shift = [[offsets_ref[w, s] for s in range(blocks)] for w in range(views)]
    planes = [work[3 * w] for w in range(views)]
    halves = [work[3 * w + 1] for w in range(views)]
    logs = [work[3 * w + 2] for w in range(views)]

    def first(w, kind):
        half = jnp.dot(matrices_ref[w, kind], planes[w][...], preferred_element_type=jnp.float32)
        half = half.astype(jnp.bfloat16)
        for k in range(tiles):
            for r in range(2):
                halves[w][k * height : (k + 1) * height, r * columns : (r + 1) * columns] = half[
                    r * height : (r + 1) * height, k * columns : (k + 1) * columns
                ]

    for w in range(views):
        for k in range(tiles):
            tile = lax.bitwise_xor(me, k)
            for s in range(blocks):
                owner = lax.rem(tile + shift[w][s], tiles)
                planes[w][s * rows : (s + 1) * rows, k * columns : (k + 1) * columns] = current_ref[
                    owner, s * rows : (s + 1) * rows, :
                ]
    for w in range(views):
        first(w, 0)
    for w in range(views):
        blurred = jnp.dot(halves[w][...], matrices_ref[w, 1], preferred_element_type=jnp.float32)
        for k in range(tiles):
            quotient = data[w * tiles + k][...].astype(jnp.float32) / blurred[k * height : (k + 1) * height]
            planes[w][:, k * columns : (k + 1) * columns] = quotient.astype(jnp.bfloat16)
    for w in range(views):
        first(w, 2)
    for w in range(views):
        back = jnp.dot(halves[w][...], matrices_ref[w, 3], preferred_element_type=jnp.float32)
        logs[w][...] = jnp.log(back.astype(jnp.bfloat16).astype(jnp.float32))
    for o in range(tiles):
        for s in range(blocks):
            total = None
            for w in range(views):
                tile = lax.rem(o - shift[w][s] + tiles, tiles)
                start = pl.multiple_of(lax.bitwise_xor(tile, me) * height + s * rows, rows)
                part = logs[w][pl.ds(start, rows), :]
                total = part if total is None else total + part
            log_ref[o * height + s * rows : o * height + (s + 1) * rows, :] = total


def correction_logs(tile, offsets, current, matrices, data):
    tiles, height, columns = current.shape
    scratch = [
        pltpu.VMEM((height, tiles * columns), jnp.bfloat16),
        pltpu.VMEM((tiles * height, 2 * columns), jnp.bfloat16),
        pltpu.VMEM((tiles * height, columns), jnp.float32),
    ]
    return pl.pallas_call(
        functools.partial(correction_kernel, tiles),
        out_shape=jax.ShapeDtypeStruct((tiles * height, columns), jnp.float32),
        in_specs=[SMEM, SMEM] + [VMEM] * (2 + len(data)),
        out_specs=VMEM,
        scratch_shapes=scratch * offsets.shape[0],
        cost_estimate=pl.CostEstimate(flops=300_000_000, bytes_accessed=1_500_000, transcendentals=0),
        compiler_params=LIMIT,
        name="correction",
    )(tile, offsets, current, matrices, *data)


def update_kernel(views, core_ref, current_ref, twin_ref, other_ref, log_ref, *new_refs):
    total, columns = current_ref.shape
    first = core_ref[0] == 0
    row = lax.broadcasted_iota(jnp.int32, (CHUNK, columns), 0)
    column = lax.broadcasted_iota(jnp.int32, (CHUNK, columns), 1)

    def scale(z, y, x):
        return lax.rsqrt(z * z + y * y + x * x + SMOOTH_SQUARE)

    def pick(low, high, start, size):
        return jnp.where(first, low[start : start + size, :], high[start : start + size, :])

    def next_row(x, following):
        return jnp.where(row == CHUNK - 1, following, pltpu.roll(x, CHUNK - 1, 0))

    def next_column(x):
        return jnp.where(column == columns - 1, 0.0, pltpu.roll(x, columns - 1, 1))

    def edge(x):
        return x * lax.rsqrt(x * x + SMOOTH_SQUARE)

    carry = edge(current_ref[0:1, :])
    for start in range(0, total, CHUNK):
        stop = start + CHUNK
        current = current_ref[start:stop, :]
        above = pick(twin_ref, other_ref, start, CHUNK)
        below = pick(other_ref, twin_ref, start, CHUNK)
        if stop < total:
            current_next, below_next = current_ref[stop : stop + 1, :], pick(other_ref, twin_ref, stop, 1)
        else:
            current_next = below_next = jnp.zeros((1, columns), jnp.float32)
        grad_z = above - current
        grad_y = next_row(current, current_next) - current
        grad_x = next_column(current) - current
        inverse = scale(grad_z, grad_y, grad_x)
        unit_y, unit_x = grad_y * inverse, grad_x * inverse
        before_y = jnp.where(row == 0, carry, pltpu.roll(unit_y, 1, 0))
        before_x = jnp.where(column == 0, edge(current), pltpu.roll(unit_x, 1, 1))
        carry = unit_y[CHUNK - 1 : CHUNK, :]
        lower_z = current - below
        lower = lower_z * scale(lower_z, next_row(below, below_next) - below, next_column(below) - below)
        divergence = grad_z * inverse - lower + (unit_y - before_y) + (unit_x - before_x)
        damping = 1.0 - TV_WEIGHT * divergence
        new = current * jnp.exp(log_ref[start:stop, :] * (1.0 / views)) / damping
        for ref in new_refs:
            ref[start:stop, :] = new.astype(ref.dtype)


def update(views, core, current, twin, other, logs, dtypes):
    return pl.pallas_call(
        functools.partial(update_kernel, views),
        out_shape=[jax.ShapeDtypeStruct(current.shape, dtype) for dtype in dtypes],
        in_specs=[SMEM] + [VMEM] * 4,
        out_specs=[VMEM] * len(dtypes),
        compiler_params=LIMIT,
        name="update",
    )(core, current, twin, other, logs)


def plane_shards(view_data, estimate, psf_taps, offsets):
    tiles, views = lax.axis_size("tiles"), lax.axis_size("views")
    square = ("tiles", "views", "gz")
    planes, height, columns = estimate.shape
    blocks = offsets.shape[1]
    taps = psf_taps.shape[-1]
    tile, view, core = lax.axis_index("tiles"), lax.axis_index("views"), lax.axis_index("gz")
    swap = [(0, 1), (1, 0)]

    def device(t, v, g):
        return (t * views + v) * 2 + g

    def ordered(pieces, shift):
        placed = []
        for i in range(tiles):
            chosen = pieces[i]
            for s in range(1, tiles):
                chosen = jnp.where(shift == s, pieces[i ^ s], chosen)
            placed.append(chosen)
        return placed

    def exchange(pick):
        pieces = []
        for k in range(tiles):
            pairs = [(device(t, v, g), device(t ^ k, g, v)) for t in range(tiles) for v in range(2) for g in range(2)]
            pieces.append(lax.ppermute(pick(k), square, pairs))
        return pieces

    def end_of(chain):
        return jnp.where(chain == 0, 0, tiles - 1)

    me = tile.reshape(1).astype(jnp.int32)
    flag = core.reshape(1).astype(jnp.int32)

    wide = estimate.reshape(tiles, 2, height, columns)
    wide = lax.dynamic_index_in_dim(wide, view, 1, keepdims=True)
    wide = jnp.round((wide - 1.0) * PLANE_UNIT).astype(jnp.int16)
    data = view_data.reshape(tiles, 2, height, columns).astype(jnp.float32)
    data = (data * DATA_UNIT).astype(jnp.int16)
    payload = jnp.concatenate([wide, data], axis=1).reshape(tiles, 3 * height, columns)
    payload, psf_taps, offsets = lax.optimization_barrier((payload, psf_taps, offsets))

    def for_tile(k):
        place = lax.bitwise_xor(lax.bitwise_xor(tile, k), end_of(core))
        return lax.dynamic_index_in_dim(payload, place, 0, keepdims=False)

    pieces = exchange(for_tile)

    profiles = [psf_taps.reshape(-1), psf_taps[..., ::-1].reshape(-1)]
    info = [lax.reduce_precision(p, 8, 7) * TAP_UNIT for p in profiles]
    info = jnp.concatenate([*info, offsets.reshape(-1).astype(jnp.float32)])
    info = jnp.pad(info, (0, columns - info.shape[0])).astype(jnp.int16)
    info = jnp.broadcast_to(info, (INFO_ROWS, columns))
    note = lax.ppermute(info, "views", swap)
    straight = view == core
    notes = jnp.stack([jnp.where(straight, info[0], note[0]), jnp.where(straight, note[0], info[0])])
    notes = notes.astype(jnp.float32)
    shifts = notes[:, 8 * taps : 8 * taps + blocks].astype(jnp.int32)
    matrices = blur_matrices(taps, height, notes * (1.0 / TAP_UNIT))

    planes = [piece[:height] for piece in pieces]
    pairs = [piece[height : 3 * height].reshape(2, height, columns) for piece in pieces]
    keep = [lax.dynamic_index_in_dim(pair, core, 0, keepdims=False) for pair in pairs]
    give = [lax.dynamic_index_in_dim(pair, 1 - core, 0, keepdims=False) for pair in pairs]
    got = lax.ppermute(jnp.concatenate([*planes, *give]), "gz", swap)
    length = tiles * height
    twin = got[:length].reshape(tiles, height, columns)
    take = got[length:].reshape(tiles, height, columns)
    data = [x.astype(jnp.float32) * (1.0 / DATA_UNIT) for x in [*keep, *[take[k] for k in range(tiles)]]]
    data = [x.astype(jnp.bfloat16) for x in data]

    path = [(t, 0) for t in range(tiles)] + [(t, 1) for t in reversed(range(tiles))]
    hops = []
    for here, there in zip(path[:-1], path[1:]):
        one, two = device(*here, 1), device(*there, 0)
        hops += [(one, two), (two, one)]

    def plane_of(coded):
        return coded.astype(jnp.float32) * (1.0 / PLANE_UNIT) + 1.0

    plane = jnp.concatenate(ordered(planes, tile))
    twin = plane_of(jnp.concatenate(ordered([twin[k] for k in range(tiles)], tile)))
    current = plane_of(plane)
    narrow = current.astype(jnp.bfloat16)
    at_end = (tile == 0) & (core == view)
    for iteration in range(ITERS):
        first, last = iteration == 0, iteration == ITERS - 1
        other = lax.ppermute(plane, square, hops)
        if not first:
            twin = lax.ppermute(current, "gz", swap)
        other = jnp.where(at_end, 0.0, plane_of(other) if first else other.astype(jnp.float32) + 1.0)
        logs = correction_logs(me, shifts, narrow.reshape(tiles, height, columns), matrices, data)
        current, *rest = update(
            views, flag, current, twin, other, logs, [jnp.float32] if last else [jnp.float32, jnp.bfloat16]
        )
        if not last:
            narrow = rest[0]
            plane = (current - 1.0).astype(jnp.float16)

    result = current.astype(jnp.float16).reshape(tiles, height, columns)
    pieces = []
    for k in range(tiles):
        piece = lax.dynamic_index_in_dim(result, lax.bitwise_xor(tile, k), 0)
        pieces.append(lax.ppermute(piece, "tiles", [(t, t ^ k) for t in range(tiles)]) if k else piece)
    mine = ordered([piece[0] for piece in pieces], lax.bitwise_xor(tile, end_of(core)))
    mine, turned = jnp.stack(mine), jnp.stack(mine[::-1])
    one_way = [(device(t, v, v), device(t, 1 - v, v)) for t in range(tiles) for v in range(2)]
    across = [(device(t, v, 1 - v), device(t, 1 - v, v)) for t in range(tiles) for v in range(2)]
    far_twin = lax.ppermute(turned, square, across)
    far_same = lax.ppermute(mine, square, one_way)
    near_twin = lax.ppermute(turned, "gz", swap)
    same = jnp.where(straight, mine, far_same)
    twin = jnp.where(straight, near_twin, far_twin)
    parity = lax.broadcasted_iota(jnp.int32, (tiles, 2, height, columns), 1)
    result = jnp.where(parity == core, same[:, None], twin[:, None])
    return result.astype(jnp.float32).reshape(2 * tiles, height, columns)


def one_plane_each(mesh, view_data, estimate, psf_taps, offsets):
    tiles, views, depth = mesh.shape["tiles"], mesh.shape["views"], mesh.shape["gz"]
    planes = estimate.shape[0] // (mesh.shape["groups"] * depth)
    height, columns = estimate.shape[1] // tiles, estimate.shape[2]
    return (
        depth == 2
        and views == 2
        and planes == 2 * tiles
        and tiles & (tiles - 1) == 0
        and height == columns
        and height % (16 * offsets.shape[1]) == 0
        and columns == 128
        and 8 * psf_taps.shape[-1] + offsets.shape[1] <= columns
    )


def solution(mesh):
    in_specs = (
        P(("groups", "views"), "tiles", "gz", None, None),
        P(("groups", "gz"), "tiles", None),
        P("views", None, None, None),
        P("views", None),
    )
    out_specs = P(("groups", "gz"), "tiles", None)

    def step(*arrays):
        if not one_plane_each(mesh, *arrays):
            return jax.shard_map(shards, mesh=mesh, in_specs=in_specs, out_specs=out_specs, check_vma=False)(*arrays)
        body = jax.shard_map(plane_shards, mesh=mesh, in_specs=in_specs, out_specs=out_specs, check_vma=False)
        return body(*arrays)

    return step
```

```python
import functools

import jax
import jax.numpy as jnp
from jax import lax
from jax.experimental import pallas as pl
from jax.experimental.pallas import tpu as pltpu
from jax.sharding import PartitionSpec as P


ITERS = 2
CAP = 4


TV_WEIGHT = 0.1
SMOOTH_SQUARE = 0.0025


def with_halo(cells, sides, width):
    for axis, dim in sides:
        count = lax.axis_size(axis)
        ends = count - 1
        head = lax.slice_in_dim(cells, 0, width, axis=dim)
        tail = lax.slice_in_dim(cells, cells.shape[dim] - width, cells.shape[dim], axis=dim)
        cells = jnp.concatenate(
            [
                lax.ppermute(tail, axis, [(i, (i + 1) % count) for i in range(ends)]),
                cells,
                lax.ppermute(head, axis, [((i + 1) % count, i) for i in range(ends)]),
            ],
            axis=dim,
        )
    return cells


def toeplitz_matrix(profile, length):
    half_width = (profile.shape[0] - 1) // 2
    position = jnp.arange(length, dtype=jnp.int32)
    offset = position[None, :] - position[:, None] + half_width
    tap_index = jnp.arange(profile.shape[0], dtype=jnp.int32)
    picked = (offset[:, :, None] == tap_index[None, None, :]).astype(jnp.float32)
    return jnp.sum(picked * profile[None, None, :], axis=2).astype(jnp.bfloat16)


def curvature(padded):
    anchor = padded[:-1, :-1, :-1]
    grad_z = padded[1:, :-1, :-1] - anchor
    grad_y = padded[:-1, 1:, :-1] - anchor
    grad_x = padded[:-1, :-1, 1:] - anchor
    magnitude = jnp.sqrt(grad_z * grad_z + grad_y * grad_y + grad_x * grad_x + SMOOTH_SQUARE)
    unit_z = grad_z / magnitude
    unit_y = grad_y / magnitude
    unit_x = grad_x / magnitude
    return (
        unit_z[1:, 1:, 1:]
        - unit_z[:-1, 1:, 1:]
        + (unit_y[1:, 1:, 1:] - unit_y[1:, :-1, 1:])
        + (unit_x[1:, 1:, 1:] - unit_x[1:, 1:, :-1])
    )


def view_correction(view_tile, observed, kernel_y, kernel_x):
    blurred = jnp.zeros(view_tile.shape, jnp.float32)
    for term_index in range(2):
        half_blur = jnp.einsum(
            "yk,zkx->zyx", kernel_y[term_index], view_tile, preferred_element_type=jnp.float32
        ).astype(jnp.bfloat16)
        blurred = blurred + jnp.einsum(
            "zyk,xk->zyx", half_blur, kernel_x[term_index], preferred_element_type=jnp.float32
        )
    quotient = (observed.astype(jnp.float32) / blurred).astype(jnp.bfloat16)
    log_sum = jnp.zeros(view_tile.shape, jnp.float32)
    for term_index in range(2):
        half_back = jnp.einsum(
            "ky,zkx->zyx", kernel_y[term_index], quotient, preferred_element_type=jnp.float32
        ).astype(jnp.bfloat16)
        log_sum = log_sum + jnp.einsum(
            "zyk,kx->zyx", half_back, kernel_x[term_index], preferred_element_type=jnp.float32
        )
    return log_sum.astype(jnp.bfloat16)


def shards(view_data, estimate, psf_taps, offsets):
    owners = lax.axis_size("tiles")
    view_count = lax.axis_size("views")
    observed = view_data[0, 0]
    planes, height, columns = estimate.shape
    view_shift = offsets[0]
    blocks = view_shift.shape[0]
    block_rows = height // blocks
    slot_count = owners * CAP
    kernel_y = jnp.stack(
        [toeplitz_matrix(psf_taps[0, term_index, 0], height) for term_index in range(2)]
    )
    kernel_x = jnp.stack(
        [toeplitz_matrix(psf_taps[0, term_index, 1], columns) for term_index in range(2)]
    )
    position = jnp.arange(blocks, dtype=jnp.int32)
    same_owner = view_shift[:, None] == view_shift[None, :]
    before = position[None, :] < position[:, None]
    slot_rank = jnp.sum((same_owner & before).astype(jnp.int32), axis=1)
    member = lax.axis_index("tiles")
    target = (member + view_shift) % owners
    source_tile = (member - view_shift) % owners
    slot_index = jnp.arange(slot_count, dtype=jnp.int32)
    to_owner = ((target * CAP + slot_rank)[:, None] == slot_index[None, :]).astype(jnp.bfloat16)
    from_tile = ((source_tile * CAP + slot_rank)[:, None] == slot_index[None, :]).astype(
        jnp.bfloat16
    )
    current = estimate
    for _ in range(ITERS):
        padded = with_halo(current, (("tiles", 1), ("gz", 0)), 1)
        padded = jnp.pad(padded, ((0, 0), (0, 0), (1, 1)))
        owned_blocks = current.astype(jnp.bfloat16).reshape(planes, blocks, block_rows, columns)
        outgoing = jnp.einsum(
            "sk,zsrx->kzrx", from_tile, owned_blocks, preferred_element_type=jnp.float32
        ).astype(jnp.bfloat16)
        incoming = lax.all_to_all(
            outgoing.reshape(owners, CAP, planes, block_rows, columns),
            "tiles",
            split_axis=0,
            concat_axis=0,
            tiled=True,
        )
        view_tile = jnp.einsum(
            "sk,kzrx->zsrx",
            to_owner,
            incoming.reshape(slot_count, planes, block_rows, columns),
            preferred_element_type=jnp.float32,
        ).astype(jnp.bfloat16)
        view_tile = view_tile.reshape(planes, height, columns)
        correction = view_correction(view_tile, observed, kernel_y, kernel_x)
        correction = correction.reshape(planes, blocks, block_rows, columns)
        returned = jnp.einsum(
            "sk,zsrx->kzrx", to_owner, correction, preferred_element_type=jnp.float32
        ).astype(jnp.bfloat16)
        gathered = lax.all_to_all(
            returned.reshape(owners, CAP, planes, block_rows, columns),
            "tiles",
            split_axis=0,
            concat_axis=0,
            tiled=True,
        )
        owned_rows = jnp.einsum(
            "sk,kzrx->zsrx",
            from_tile,
            gathered.reshape(slot_count, planes, block_rows, columns),
            preferred_element_type=jnp.float32,
        ).reshape(planes, height, columns)
        log_values = jnp.log(owned_rows)
        share_rows = height // view_count
        log_part = lax.psum_scatter(log_values, "views", scatter_dimension=1, tiled=True)
        first_row = lax.axis_index("views") * share_rows
        window = lax.dynamic_slice_in_dim(padded, first_row, share_rows + 2, 1)
        damping = 1.0 - TV_WEIGHT * curvature(window)
        rows_now = lax.dynamic_slice_in_dim(current, first_row, share_rows, 1)
        updated = rows_now * jnp.exp(log_part / view_count) / damping
        current = lax.all_gather(updated, "views", axis=1, tiled=True)
    return current


INFO_ROWS = 16
PLANE_UNIT = 65534.0
DATA_UNIT = 1024.0
TAP_UNIT = 8192.0
CHUNK = 32
VMEM = pl.BlockSpec(memory_space=pltpu.VMEM)
SMEM = pl.BlockSpec(memory_space=pltpu.SMEM)
LIMIT = pltpu.CompilerParams(vmem_limit_bytes=16 * 2**20)


def matrices_kernel(taps, info_ref, out_ref):
    views, columns = info_ref.shape
    length = out_ref.shape[-2] // 2
    half_width = (taps - 1) // 2
    row = lax.broadcasted_iota(jnp.int32, (length, columns), 0)
    column = lax.broadcasted_iota(jnp.int32, (length, columns), 1)
    band = jnp.abs(row - column) <= half_width
    for v in range(views):
        profile = jnp.broadcast_to(info_ref[v : v + 1, :], (8, columns))
        for kind, (flipped, axis) in enumerate([(0, 0), (1, 1), (1, 0), (0, 1)]):
            for r in range(2):
                lane = (4 * flipped + 2 * r + axis) * taps + half_width
                spread = jnp.broadcast_to(pltpu.roll(profile, columns - lane, 1)[0:1], (length, columns))
                rolled = pltpu.roll(spread, 0, 1, stride=1, stride_axis=0)
                rolled = jnp.where(band, rolled, 0.0).astype(out_ref.dtype)
                out_ref[v, kind, r * length : (r + 1) * length, :] = rolled


def blur_matrices(taps, length, info):
    views, columns = info.shape
    return pl.pallas_call(
        functools.partial(matrices_kernel, taps),
        out_shape=jax.ShapeDtypeStruct((views, 4, 2 * length, columns), jnp.bfloat16),
        in_specs=[VMEM],
        out_specs=VMEM,
        compiler_params=LIMIT,
        name="blur_matrices",
    )(info)


def correction_kernel(tiles, tile_ref, offsets_ref, current_ref, matrices_ref, *refs):
    views, blocks = offsets_ref.shape
    data, log_ref, work = refs[: views * tiles], refs[views * tiles], refs[views * tiles + 1 :]
    height, columns = data[0].shape
    rows = height // blocks
    me = tile_ref[0]
    shift = [[offsets_ref[w, s] for s in range(blocks)] for w in range(views)]
    planes = [work[3 * w] for w in range(views)]
    halves = [work[3 * w + 1] for w in range(views)]
    logs = [work[3 * w + 2] for w in range(views)]

    def first(w, kind):
        half = jnp.dot(matrices_ref[w, kind], planes[w][...], preferred_element_type=jnp.float32)
        half = half.astype(jnp.bfloat16)
        for k in range(tiles):
            for r in range(2):
                halves[w][k * height : (k + 1) * height, r * columns : (r + 1) * columns] = half[
                    r * height : (r + 1) * height, k * columns : (k + 1) * columns
                ]

    for w in range(views):
        for k in range(tiles):
            tile = lax.bitwise_xor(me, k)
            for s in range(blocks):
                owner = lax.rem(tile + shift[w][s], tiles)
                planes[w][s * rows : (s + 1) * rows, k * columns : (k + 1) * columns] = current_ref[
                    owner, s * rows : (s + 1) * rows, :
                ]
    for w in range(views):
        first(w, 0)
    for w in range(views):
        blurred = jnp.dot(halves[w][...], matrices_ref[w, 1], preferred_element_type=jnp.float32)
        for k in range(tiles):
            quotient = data[w * tiles + k][...].astype(jnp.float32) / blurred[k * height : (k + 1) * height]
            planes[w][:, k * columns : (k + 1) * columns] = quotient.astype(jnp.bfloat16)
    for w in range(views):
        first(w, 2)
    for w in range(views):
        back = jnp.dot(halves[w][...], matrices_ref[w, 3], preferred_element_type=jnp.float32)
        logs[w][...] = jnp.log(back.astype(jnp.bfloat16).astype(jnp.float32))
    for o in range(tiles):
        for s in range(blocks):
            total = None
            for w in range(views):
                tile = lax.rem(o - shift[w][s] + tiles, tiles)
                start = pl.multiple_of(lax.bitwise_xor(tile, me) * height + s * rows, rows)
                part = logs[w][pl.ds(start, rows), :]
                total = part if total is None else total + part
            log_ref[o * height + s * rows : o * height + (s + 1) * rows, :] = total


def correction_logs(tile, offsets, current, matrices, data):
    tiles, height, columns = current.shape
    scratch = [
        pltpu.VMEM((height, tiles * columns), jnp.bfloat16),
        pltpu.VMEM((tiles * height, 2 * columns), jnp.bfloat16),
        pltpu.VMEM((tiles * height, columns), jnp.float32),
    ]
    return pl.pallas_call(
        functools.partial(correction_kernel, tiles),
        out_shape=jax.ShapeDtypeStruct((tiles * height, columns), jnp.float32),
        in_specs=[SMEM, SMEM] + [VMEM] * (2 + len(data)),
        out_specs=VMEM,
        scratch_shapes=scratch * offsets.shape[0],
        cost_estimate=pl.CostEstimate(flops=300_000_000, bytes_accessed=1_500_000, transcendentals=0),
        compiler_params=LIMIT,
        name="correction",
    )(tile, offsets, current, matrices, *data)


def update_kernel(views, core_ref, current_ref, twin_ref, other_ref, log_ref, *new_refs):
    total, columns = current_ref.shape
    first = core_ref[0] == 0
    row = lax.broadcasted_iota(jnp.int32, (CHUNK, columns), 0)
    column = lax.broadcasted_iota(jnp.int32, (CHUNK, columns), 1)

    def scale(z, y, x):
        return lax.rsqrt(z * z + y * y + x * x + SMOOTH_SQUARE)

    def pick(low, high, start, size):
        return jnp.where(first, low[start : start + size, :], high[start : start + size, :])

    def next_row(x, following):
        return jnp.where(row == CHUNK - 1, following, pltpu.roll(x, CHUNK - 1, 0))

    def next_column(x):
        return jnp.where(column == columns - 1, 0.0, pltpu.roll(x, columns - 1, 1))

    def edge(x):
        return x * lax.rsqrt(x * x + SMOOTH_SQUARE)

    carry = edge(current_ref[0:1, :])
    for start in range(0, total, CHUNK):
        stop = start + CHUNK
        current = current_ref[start:stop, :]
        above = pick(twin_ref, other_ref, start, CHUNK)
        below = pick(other_ref, twin_ref, start, CHUNK)
        if stop < total:
            current_next, below_next = current_ref[stop : stop + 1, :], pick(other_ref, twin_ref, stop, 1)
        else:
            current_next = below_next = jnp.zeros((1, columns), jnp.float32)
        grad_z = above - current
        grad_y = next_row(current, current_next) - current
        grad_x = next_column(current) - current
        inverse = scale(grad_z, grad_y, grad_x)
        unit_y, unit_x = grad_y * inverse, grad_x * inverse
        before_y = jnp.where(row == 0, carry, pltpu.roll(unit_y, 1, 0))
        before_x = jnp.where(column == 0, edge(current), pltpu.roll(unit_x, 1, 1))
        carry = unit_y[CHUNK - 1 : CHUNK, :]
        lower_z = current - below
        lower = lower_z * scale(lower_z, next_row(below, below_next) - below, next_column(below) - below)
        divergence = grad_z * inverse - lower + (unit_y - before_y) + (unit_x - before_x)
        damping = 1.0 - TV_WEIGHT * divergence
        new = current * jnp.exp(log_ref[start:stop, :] * (1.0 / views)) / damping
        for ref in new_refs:
            ref[start:stop, :] = new.astype(ref.dtype)


def update(views, core, current, twin, other, logs, dtypes):
    return pl.pallas_call(
        functools.partial(update_kernel, views),
        out_shape=[jax.ShapeDtypeStruct(current.shape, dtype) for dtype in dtypes],
        in_specs=[SMEM] + [VMEM] * 4,
        out_specs=[VMEM] * len(dtypes),
        compiler_params=LIMIT,
        name="update",
    )(core, current, twin, other, logs)


def plane_shards(view_data, estimate, psf_taps, offsets):
    tiles, views = lax.axis_size("tiles"), lax.axis_size("views")
    square = ("tiles", "views", "gz")
    planes, height, columns = estimate.shape
    blocks = offsets.shape[1]
    taps = psf_taps.shape[-1]
    tile, view, core = lax.axis_index("tiles"), lax.axis_index("views"), lax.axis_index("gz")
    swap = [(0, 1), (1, 0)]

    def device(t, v, g):
        return (t * views + v) * 2 + g

    def ordered(pieces, shift):
        placed = []
        for i in range(tiles):
            chosen = pieces[i]
            for s in range(1, tiles):
                chosen = jnp.where(shift == s, pieces[i ^ s], chosen)
            placed.append(chosen)
        return placed

    def transfer(piece, k):
        pairs = [(device(t, v, g), device(t ^ k, g, v)) for t in range(tiles) for v in range(2) for g in range(2)]
        return lax.ppermute(piece, square, pairs)

    def end_of(chain):
        return jnp.where(chain == 0, 0, tiles - 1)

    me = tile.reshape(1).astype(jnp.int32)
    flag = core.reshape(1).astype(jnp.int32)

    wide = estimate.reshape(tiles, 2, height, columns)
    wide = lax.dynamic_index_in_dim(wide, view, 1, keepdims=True)
    wide = jnp.round((wide - 1.0) * PLANE_UNIT).astype(jnp.int16)
    data = view_data.reshape(tiles, 2, height, columns).astype(jnp.float32)
    data = (data * DATA_UNIT).astype(jnp.int16)
    payload = jnp.concatenate([wide, data], axis=1).reshape(tiles, 3 * height, columns)
    payload, psf_taps, offsets = lax.optimization_barrier((payload, psf_taps, offsets))

    planes, pairs = [], []
    for k in range(tiles):
        place = lax.bitwise_xor(lax.bitwise_xor(tile, k), end_of(core))
        piece = lax.dynamic_index_in_dim(payload, place, 0, keepdims=False)
        if k > 1:
            planes.append(transfer(piece[:height], k))
            pairs.append(transfer(piece[height:], k))
        else:
            piece = transfer(piece, k)
            planes.append(piece[:height])
            pairs.append(piece[height:])

    profiles = [psf_taps.reshape(-1), psf_taps[..., ::-1].reshape(-1)]
    info = [lax.reduce_precision(p, 8, 7) * TAP_UNIT for p in profiles]
    info = jnp.concatenate([*info, offsets.reshape(-1).astype(jnp.float32)])
    info = jnp.pad(info, (0, columns - info.shape[0])).astype(jnp.int16)
    info = jnp.broadcast_to(info, (INFO_ROWS, columns))
    note = lax.ppermute(info, "views", swap)
    straight = view == core
    notes = jnp.stack([jnp.where(straight, info[0], note[0]), jnp.where(straight, note[0], info[0])])
    notes = notes.astype(jnp.float32)
    shifts = notes[:, 8 * taps : 8 * taps + blocks].astype(jnp.int32)
    matrices = blur_matrices(taps, height, notes * (1.0 / TAP_UNIT))

    pairs = [pair.reshape(2, height, columns) for pair in pairs]
    keep = [lax.dynamic_index_in_dim(pair, core, 0, keepdims=False) for pair in pairs]
    give = [lax.dynamic_index_in_dim(pair, 1 - core, 0, keepdims=False) for pair in pairs]
    got = lax.ppermute(jnp.concatenate([*planes, *give]), "gz", swap)
    length = tiles * height
    twin = got[:length].reshape(tiles, height, columns)
    take = got[length:].reshape(tiles, height, columns)
    data = [x.astype(jnp.float32) * (1.0 / DATA_UNIT) for x in [*keep, *[take[k] for k in range(tiles)]]]
    data = [x.astype(jnp.bfloat16) for x in data]

    path = [(t, 0) for t in range(tiles)] + [(t, 1) for t in reversed(range(tiles))]
    hops = []
    for here, there in zip(path[:-1], path[1:]):
        one, two = device(*here, 1), device(*there, 0)
        hops += [(one, two), (two, one)]

    def plane_of(coded):
        return coded.astype(jnp.float32) * (1.0 / PLANE_UNIT) + 1.0

    plane = jnp.concatenate(ordered(planes, tile))
    twin = plane_of(jnp.concatenate(ordered([twin[k] for k in range(tiles)], tile)))
    current = plane_of(plane)
    narrow = current.astype(jnp.bfloat16)
    at_end = (tile == 0) & (core == view)
    for iteration in range(ITERS):
        first, last = iteration == 0, iteration == ITERS - 1
        other = lax.ppermute(plane, square, hops)
        if not first:
            twin = lax.ppermute(current, "gz", swap)
        other = jnp.where(at_end, 0.0, plane_of(other) if first else other.astype(jnp.float32) + 1.0)
        logs = correction_logs(me, shifts, narrow.reshape(tiles, height, columns), matrices, data)
        current, *rest = update(
            views, flag, current, twin, other, logs, [jnp.float32] if last else [jnp.float32, jnp.bfloat16]
        )
        if not last:
            narrow = rest[0]
            plane = (current - 1.0).astype(jnp.float16)

    result = current.astype(jnp.float16).reshape(tiles, height, columns)
    pieces = []
    for k in range(tiles):
        piece = lax.dynamic_index_in_dim(result, lax.bitwise_xor(tile, k), 0)
        pieces.append(lax.ppermute(piece, "tiles", [(t, t ^ k) for t in range(tiles)]) if k else piece)
    mine = jnp.concatenate(pieces)
    crossed = [lax.ppermute(pieces[0], "views", swap)]
    crossed.append(lax.ppermute(mine[1:], "views", swap))
    crossed = [crossed[0][0], *[crossed[1][k] for k in range(tiles - 1)]]
    mine = [mine[k] for k in range(tiles)]
    here = lax.bitwise_xor(tile, end_of(core))
    send = [jnp.where(straight, c, m) for c, m in zip(crossed, mine)]
    send = jnp.stack(ordered(send, lax.bitwise_xor(tile, end_of(1 - core))))
    twin = lax.ppermute(send, "gz", swap)
    same = jnp.stack(ordered([jnp.where(straight, m, c) for c, m in zip(crossed, mine)], here))
    parity = lax.broadcasted_iota(jnp.int32, (tiles, 2, height, columns), 1)
    result = jnp.where(parity == core, same[:, None], twin[:, None])
    return result.astype(jnp.float32).reshape(2 * tiles, height, columns)


def one_plane_each(mesh, view_data, estimate, psf_taps, offsets):
    tiles, views, depth = mesh.shape["tiles"], mesh.shape["views"], mesh.shape["gz"]
    planes = estimate.shape[0] // (mesh.shape["groups"] * depth)
    height, columns = estimate.shape[1] // tiles, estimate.shape[2]
    return (
        depth == 2
        and views == 2
        and planes == 2 * tiles
        and tiles & (tiles - 1) == 0
        and height == columns
        and height % (16 * offsets.shape[1]) == 0
        and columns == 128
        and 8 * psf_taps.shape[-1] + offsets.shape[1] <= columns
    )


def solution(mesh):
    in_specs = (
        P(("groups", "views"), "tiles", "gz", None, None),
        P(("groups", "gz"), "tiles", None),
        P("views", None, None, None),
        P("views", None),
    )
    out_specs = P(("groups", "gz"), "tiles", None)

    def step(*arrays):
        if not one_plane_each(mesh, *arrays):
            return jax.shard_map(shards, mesh=mesh, in_specs=in_specs, out_specs=out_specs, check_vma=False)(*arrays)
        body = jax.shard_map(plane_shards, mesh=mesh, in_specs=in_specs, out_specs=out_specs, check_vma=False)
        return body(*arrays)

    return step
```

```python
import functools

import jax
import jax.numpy as jnp
from jax import lax
from jax.experimental import pallas as pl
from jax.experimental.pallas import tpu as pltpu
from jax.sharding import PartitionSpec as P


ITERS = 2
CAP = 4


TV_WEIGHT = 0.1
SMOOTH_SQUARE = 0.0025


def with_halo(cells, sides, width):
    for axis, dim in sides:
        count = lax.axis_size(axis)
        ends = count - 1
        head = lax.slice_in_dim(cells, 0, width, axis=dim)
        tail = lax.slice_in_dim(cells, cells.shape[dim] - width, cells.shape[dim], axis=dim)
        cells = jnp.concatenate(
            [
                lax.ppermute(tail, axis, [(i, (i + 1) % count) for i in range(ends)]),
                cells,
                lax.ppermute(head, axis, [((i + 1) % count, i) for i in range(ends)]),
            ],
            axis=dim,
        )
    return cells


def toeplitz_matrix(profile, length):
    half_width = (profile.shape[0] - 1) // 2
    position = jnp.arange(length, dtype=jnp.int32)
    offset = position[None, :] - position[:, None] + half_width
    tap_index = jnp.arange(profile.shape[0], dtype=jnp.int32)
    picked = (offset[:, :, None] == tap_index[None, None, :]).astype(jnp.float32)
    return jnp.sum(picked * profile[None, None, :], axis=2).astype(jnp.bfloat16)


def curvature(padded):
    anchor = padded[:-1, :-1, :-1]
    grad_z = padded[1:, :-1, :-1] - anchor
    grad_y = padded[:-1, 1:, :-1] - anchor
    grad_x = padded[:-1, :-1, 1:] - anchor
    magnitude = jnp.sqrt(grad_z * grad_z + grad_y * grad_y + grad_x * grad_x + SMOOTH_SQUARE)
    unit_z = grad_z / magnitude
    unit_y = grad_y / magnitude
    unit_x = grad_x / magnitude
    return (
        unit_z[1:, 1:, 1:]
        - unit_z[:-1, 1:, 1:]
        + (unit_y[1:, 1:, 1:] - unit_y[1:, :-1, 1:])
        + (unit_x[1:, 1:, 1:] - unit_x[1:, 1:, :-1])
    )


def view_correction(view_tile, observed, kernel_y, kernel_x):
    blurred = jnp.zeros(view_tile.shape, jnp.float32)
    for term_index in range(2):
        half_blur = jnp.einsum(
            "yk,zkx->zyx", kernel_y[term_index], view_tile, preferred_element_type=jnp.float32
        ).astype(jnp.bfloat16)
        blurred = blurred + jnp.einsum(
            "zyk,xk->zyx", half_blur, kernel_x[term_index], preferred_element_type=jnp.float32
        )
    quotient = (observed.astype(jnp.float32) / blurred).astype(jnp.bfloat16)
    log_sum = jnp.zeros(view_tile.shape, jnp.float32)
    for term_index in range(2):
        half_back = jnp.einsum(
            "ky,zkx->zyx", kernel_y[term_index], quotient, preferred_element_type=jnp.float32
        ).astype(jnp.bfloat16)
        log_sum = log_sum + jnp.einsum(
            "zyk,kx->zyx", half_back, kernel_x[term_index], preferred_element_type=jnp.float32
        )
    return log_sum.astype(jnp.bfloat16)


def shards(view_data, estimate, psf_taps, offsets):
    owners = lax.axis_size("tiles")
    view_count = lax.axis_size("views")
    observed = view_data[0, 0]
    planes, height, columns = estimate.shape
    view_shift = offsets[0]
    blocks = view_shift.shape[0]
    block_rows = height // blocks
    slot_count = owners * CAP
    kernel_y = jnp.stack(
        [toeplitz_matrix(psf_taps[0, term_index, 0], height) for term_index in range(2)]
    )
    kernel_x = jnp.stack(
        [toeplitz_matrix(psf_taps[0, term_index, 1], columns) for term_index in range(2)]
    )
    position = jnp.arange(blocks, dtype=jnp.int32)
    same_owner = view_shift[:, None] == view_shift[None, :]
    before = position[None, :] < position[:, None]
    slot_rank = jnp.sum((same_owner & before).astype(jnp.int32), axis=1)
    member = lax.axis_index("tiles")
    target = (member + view_shift) % owners
    source_tile = (member - view_shift) % owners
    slot_index = jnp.arange(slot_count, dtype=jnp.int32)
    to_owner = ((target * CAP + slot_rank)[:, None] == slot_index[None, :]).astype(jnp.bfloat16)
    from_tile = ((source_tile * CAP + slot_rank)[:, None] == slot_index[None, :]).astype(
        jnp.bfloat16
    )
    current = estimate
    for _ in range(ITERS):
        padded = with_halo(current, (("tiles", 1), ("gz", 0)), 1)
        padded = jnp.pad(padded, ((0, 0), (0, 0), (1, 1)))
        owned_blocks = current.astype(jnp.bfloat16).reshape(planes, blocks, block_rows, columns)
        outgoing = jnp.einsum(
            "sk,zsrx->kzrx", from_tile, owned_blocks, preferred_element_type=jnp.float32
        ).astype(jnp.bfloat16)
        incoming = lax.all_to_all(
            outgoing.reshape(owners, CAP, planes, block_rows, columns),
            "tiles",
            split_axis=0,
            concat_axis=0,
            tiled=True,
        )
        view_tile = jnp.einsum(
            "sk,kzrx->zsrx",
            to_owner,
            incoming.reshape(slot_count, planes, block_rows, columns),
            preferred_element_type=jnp.float32,
        ).astype(jnp.bfloat16)
        view_tile = view_tile.reshape(planes, height, columns)
        correction = view_correction(view_tile, observed, kernel_y, kernel_x)
        correction = correction.reshape(planes, blocks, block_rows, columns)
        returned = jnp.einsum(
            "sk,zsrx->kzrx", to_owner, correction, preferred_element_type=jnp.float32
        ).astype(jnp.bfloat16)
        gathered = lax.all_to_all(
            returned.reshape(owners, CAP, planes, block_rows, columns),
            "tiles",
            split_axis=0,
            concat_axis=0,
            tiled=True,
        )
        owned_rows = jnp.einsum(
            "sk,kzrx->zsrx",
            from_tile,
            gathered.reshape(slot_count, planes, block_rows, columns),
            preferred_element_type=jnp.float32,
        ).reshape(planes, height, columns)
        log_values = jnp.log(owned_rows)
        share_rows = height // view_count
        log_part = lax.psum_scatter(log_values, "views", scatter_dimension=1, tiled=True)
        first_row = lax.axis_index("views") * share_rows
        window = lax.dynamic_slice_in_dim(padded, first_row, share_rows + 2, 1)
        damping = 1.0 - TV_WEIGHT * curvature(window)
        rows_now = lax.dynamic_slice_in_dim(current, first_row, share_rows, 1)
        updated = rows_now * jnp.exp(log_part / view_count) / damping
        current = lax.all_gather(updated, "views", axis=1, tiled=True)
    return current


INFO_ROWS = 16
PLANE_UNIT = 65534.0
DATA_UNIT = 1024.0
TAP_UNIT = 8192.0
CHUNK = 32
VMEM = pl.BlockSpec(memory_space=pltpu.VMEM)
SMEM = pl.BlockSpec(memory_space=pltpu.SMEM)
LIMIT = pltpu.CompilerParams(vmem_limit_bytes=16 * 2**20)


def matrices_kernel(taps, info_ref, out_ref):
    views, columns = info_ref.shape
    length = out_ref.shape[-2] // 2
    half_width = (taps - 1) // 2
    row = lax.broadcasted_iota(jnp.int32, (length, columns), 0)
    column = lax.broadcasted_iota(jnp.int32, (length, columns), 1)
    band = jnp.abs(row - column) <= half_width
    for v in range(views):
        profile = jnp.broadcast_to(info_ref[v : v + 1, :], (8, columns))
        for kind, (flipped, axis) in enumerate([(0, 0), (1, 1), (1, 0), (0, 1)]):
            for r in range(2):
                lane = (4 * flipped + 2 * r + axis) * taps + half_width
                spread = jnp.broadcast_to(pltpu.roll(profile, columns - lane, 1)[0:1], (length, columns))
                rolled = pltpu.roll(spread, 0, 1, stride=1, stride_axis=0)
                rolled = jnp.where(band, rolled, 0.0).astype(out_ref.dtype)
                out_ref[v, kind, r * length : (r + 1) * length, :] = rolled


def blur_matrices(taps, length, info):
    views, columns = info.shape
    return pl.pallas_call(
        functools.partial(matrices_kernel, taps),
        out_shape=jax.ShapeDtypeStruct((views, 4, 2 * length, columns), jnp.bfloat16),
        in_specs=[VMEM],
        out_specs=VMEM,
        compiler_params=LIMIT,
        name="blur_matrices",
    )(info)


def correction_kernel(tiles, tile_ref, offsets_ref, current_ref, matrices_ref, *refs):
    views, blocks = offsets_ref.shape
    data, log_ref, work = refs[: views * tiles], refs[views * tiles], refs[views * tiles + 1 :]
    height, columns = data[0].shape
    rows = height // blocks
    me = tile_ref[0]
    shift = [[offsets_ref[w, s] for s in range(blocks)] for w in range(views)]
    planes = [work[3 * w] for w in range(views)]
    halves = [work[3 * w + 1] for w in range(views)]
    logs = [work[3 * w + 2] for w in range(views)]

    def first(w, kind):
        half = jnp.dot(matrices_ref[w, kind], planes[w][...], preferred_element_type=jnp.float32)
        half = half.astype(jnp.bfloat16)
        for k in range(tiles):
            for r in range(2):
                halves[w][k * height : (k + 1) * height, r * columns : (r + 1) * columns] = half[
                    r * height : (r + 1) * height, k * columns : (k + 1) * columns
                ]

    for w in range(views):
        for k in range(tiles):
            tile = lax.bitwise_xor(me, k)
            for s in range(blocks):
                owner = lax.rem(tile + shift[w][s], tiles)
                planes[w][s * rows : (s + 1) * rows, k * columns : (k + 1) * columns] = current_ref[
                    owner, s * rows : (s + 1) * rows, :
                ]
    for w in range(views):
        first(w, 0)
    for w in range(views):
        blurred = jnp.dot(halves[w][...], matrices_ref[w, 1], preferred_element_type=jnp.float32)
        for k in range(tiles):
            quotient = data[w * tiles + k][...].astype(jnp.float32) / blurred[k * height : (k + 1) * height]
            planes[w][:, k * columns : (k + 1) * columns] = quotient.astype(jnp.bfloat16)
    for w in range(views):
        first(w, 2)
    for w in range(views):
        back = jnp.dot(halves[w][...], matrices_ref[w, 3], preferred_element_type=jnp.float32)
        logs[w][...] = jnp.log(back.astype(jnp.bfloat16).astype(jnp.float32))
    for o in range(tiles):
        for s in range(blocks):
            total = None
            for w in range(views):
                tile = lax.rem(o - shift[w][s] + tiles, tiles)
                start = pl.multiple_of(lax.bitwise_xor(tile, me) * height + s * rows, rows)
                part = logs[w][pl.ds(start, rows), :]
                total = part if total is None else total + part
            log_ref[o * height + s * rows : o * height + (s + 1) * rows, :] = total


def correction_logs(tile, offsets, current, matrices, data):
    tiles, height, columns = current.shape
    scratch = [
        pltpu.VMEM((height, tiles * columns), jnp.bfloat16),
        pltpu.VMEM((tiles * height, 2 * columns), jnp.bfloat16),
        pltpu.VMEM((tiles * height, columns), jnp.float32),
    ]
    return pl.pallas_call(
        functools.partial(correction_kernel, tiles),
        out_shape=jax.ShapeDtypeStruct((tiles * height, columns), jnp.float32),
        in_specs=[SMEM, SMEM] + [VMEM] * (2 + len(data)),
        out_specs=VMEM,
        scratch_shapes=scratch * offsets.shape[0],
        cost_estimate=pl.CostEstimate(flops=300_000_000, bytes_accessed=1_500_000, transcendentals=0),
        compiler_params=LIMIT,
        name="correction",
    )(tile, offsets, current, matrices, *data)


def update_kernel(views, core_ref, current_ref, twin_ref, other_ref, log_ref, *new_refs):
    total, columns = current_ref.shape
    first = core_ref[0] == 0
    row = lax.broadcasted_iota(jnp.int32, (CHUNK, columns), 0)
    column = lax.broadcasted_iota(jnp.int32, (CHUNK, columns), 1)

    def scale(z, y, x):
        return lax.rsqrt(z * z + y * y + x * x + SMOOTH_SQUARE)

    def pick(low, high, start, size):
        return jnp.where(first, low[start : start + size, :], high[start : start + size, :])

    def next_row(x, following):
        return jnp.where(row == CHUNK - 1, following, pltpu.roll(x, CHUNK - 1, 0))

    def next_column(x):
        return jnp.where(column == columns - 1, 0.0, pltpu.roll(x, columns - 1, 1))

    def edge(x):
        return x * lax.rsqrt(x * x + SMOOTH_SQUARE)

    carry = edge(current_ref[0:1, :])
    for start in range(0, total, CHUNK):
        stop = start + CHUNK
        current = current_ref[start:stop, :]
        above = pick(twin_ref, other_ref, start, CHUNK)
        below = pick(other_ref, twin_ref, start, CHUNK)
        if stop < total:
            current_next, below_next = current_ref[stop : stop + 1, :], pick(other_ref, twin_ref, stop, 1)
        else:
            current_next = below_next = jnp.zeros((1, columns), jnp.float32)
        grad_z = above - current
        grad_y = next_row(current, current_next) - current
        grad_x = next_column(current) - current
        inverse = scale(grad_z, grad_y, grad_x)
        unit_y, unit_x = grad_y * inverse, grad_x * inverse
        before_y = jnp.where(row == 0, carry, pltpu.roll(unit_y, 1, 0))
        before_x = jnp.where(column == 0, edge(current), pltpu.roll(unit_x, 1, 1))
        carry = unit_y[CHUNK - 1 : CHUNK, :]
        lower_z = current - below
        lower = lower_z * scale(lower_z, next_row(below, below_next) - below, next_column(below) - below)
        divergence = grad_z * inverse - lower + (unit_y - before_y) + (unit_x - before_x)
        damping = 1.0 - TV_WEIGHT * divergence
        new = current * jnp.exp(log_ref[start:stop, :] * (1.0 / views)) / damping
        for ref in new_refs:
            ref[start:stop, :] = new.astype(ref.dtype)


def update(views, core, current, twin, other, logs, dtypes):
    return pl.pallas_call(
        functools.partial(update_kernel, views),
        out_shape=[jax.ShapeDtypeStruct(current.shape, dtype) for dtype in dtypes],
        in_specs=[SMEM] + [VMEM] * 4,
        out_specs=[VMEM] * len(dtypes),
        compiler_params=LIMIT,
        name="update",
    )(core, current, twin, other, logs)


def plane_shards(view_data, estimate, psf_taps, offsets):
    tiles, views = lax.axis_size("tiles"), lax.axis_size("views")
    square = ("tiles", "views", "gz")
    planes, height, columns = estimate.shape
    blocks = offsets.shape[1]
    taps = psf_taps.shape[-1]
    tile, view, core = lax.axis_index("tiles"), lax.axis_index("views"), lax.axis_index("gz")
    swap = [(0, 1), (1, 0)]

    def device(t, v, g):
        return (t * views + v) * 2 + g

    def ordered(pieces, shift):
        placed = []
        for i in range(tiles):
            chosen = pieces[i]
            for s in range(1, tiles):
                chosen = jnp.where(shift == s, pieces[i ^ s], chosen)
            placed.append(chosen)
        return placed

    def exchange(pick):
        pieces = []
        for k in range(tiles):
            pairs = [(device(t, v, g), device(t ^ k, g, v)) for t in range(tiles) for v in range(2) for g in range(2)]
            pieces.append(lax.ppermute(pick(k), square, pairs))
        return pieces

    def end_of(chain):
        return jnp.where(chain == 0, 0, tiles - 1)

    me = tile.reshape(1).astype(jnp.int32)
    flag = core.reshape(1).astype(jnp.int32)

    wide = estimate.reshape(tiles, 2, height, columns)
    wide = lax.dynamic_index_in_dim(wide, view, 1, keepdims=True)
    wide = jnp.round((wide - 1.0) * PLANE_UNIT).astype(jnp.int16)
    data = view_data.reshape(tiles, 2, height, columns).astype(jnp.float32)
    data = (data * DATA_UNIT).astype(jnp.int16)
    payload = jnp.concatenate([wide, data], axis=1).reshape(tiles, 3 * height, columns)
    payload, psf_taps, offsets = lax.optimization_barrier((payload, psf_taps, offsets))

    def for_tile(k):
        place = lax.bitwise_xor(lax.bitwise_xor(tile, k), end_of(core))
        return lax.dynamic_index_in_dim(payload, place, 0, keepdims=False)

    pieces = exchange(for_tile)

    profiles = [psf_taps.reshape(-1), psf_taps[..., ::-1].reshape(-1)]
    info = [lax.reduce_precision(p, 8, 7) * TAP_UNIT for p in profiles]
    info = jnp.concatenate([*info, offsets.reshape(-1).astype(jnp.float32)])
    info = jnp.pad(info, (0, columns - info.shape[0])).astype(jnp.int16)
    info = jnp.broadcast_to(info, (INFO_ROWS, columns))
    note = lax.ppermute(info, "views", swap)
    straight = view == core
    notes = jnp.stack([jnp.where(straight, info[0], note[0]), jnp.where(straight, note[0], info[0])])
    notes = notes.astype(jnp.float32)
    shifts = notes[:, 8 * taps : 8 * taps + blocks].astype(jnp.int32)
    matrices = blur_matrices(taps, height, notes * (1.0 / TAP_UNIT))

    planes = [piece[:height] for piece in pieces]
    pairs = [piece[height : 3 * height].reshape(2, height, columns) for piece in pieces]
    keep = [lax.dynamic_index_in_dim(pair, core, 0, keepdims=False) for pair in pairs]
    give = [lax.dynamic_index_in_dim(pair, 1 - core, 0, keepdims=False) for pair in pairs]
    got = lax.ppermute(jnp.concatenate([*planes, *give]), "gz", swap)
    length = tiles * height
    twin = got[:length].reshape(tiles, height, columns)
    take = got[length:].reshape(tiles, height, columns)
    data = [x.astype(jnp.float32) * (1.0 / DATA_UNIT) for x in [*keep, *[take[k] for k in range(tiles)]]]
    data = [x.astype(jnp.bfloat16) for x in data]

    path = [(t, 0) for t in range(tiles)] + [(t, 1) for t in reversed(range(tiles))]
    hops = []
    for here, there in zip(path[:-1], path[1:]):
        one, two = device(*here, 1), device(*there, 0)
        hops += [(one, two), (two, one)]

    def plane_of(coded):
        return coded.astype(jnp.float32) * (1.0 / PLANE_UNIT) + 1.0

    plane = jnp.concatenate(ordered(planes, tile))
    twin = plane_of(jnp.concatenate(ordered([twin[k] for k in range(tiles)], tile)))
    current = plane_of(plane)
    narrow = current.astype(jnp.bfloat16)
    at_end = (tile == 0) & (core == view)
    for iteration in range(ITERS):
        first, last = iteration == 0, iteration == ITERS - 1
        other = lax.ppermute(plane, square, hops)
        if not first:
            twin = lax.ppermute(current, "gz", swap)
        other = jnp.where(at_end, 0.0, plane_of(other) if first else other.astype(jnp.float32) + 1.0)
        logs = correction_logs(me, shifts, narrow.reshape(tiles, height, columns), matrices, data)
        current, *rest = update(
            views, flag, current, twin, other, logs, [jnp.float32] if last else [jnp.float32, jnp.bfloat16]
        )
        if not last:
            narrow = rest[0]
            plane = (current - 1.0).astype(jnp.float16)

    result = current.astype(jnp.float16).reshape(tiles, height, columns)
    pieces = []
    for k in range(tiles):
        piece = lax.dynamic_index_in_dim(result, lax.bitwise_xor(tile, k), 0)
        pieces.append(lax.ppermute(piece, "tiles", [(t, t ^ k) for t in range(tiles)]) if k else piece)
    mine = jnp.concatenate(pieces)
    crossed = [lax.ppermute(pieces[0], "views", swap)]
    crossed.append(lax.ppermute(mine[1:], "views", swap))
    crossed = [crossed[0][0], *[crossed[1][k] for k in range(tiles - 1)]]
    mine = [mine[k] for k in range(tiles)]
    here = lax.bitwise_xor(tile, end_of(core))
    send = [jnp.where(straight, c, m) for c, m in zip(crossed, mine)]
    send = jnp.stack(ordered(send, lax.bitwise_xor(tile, end_of(1 - core))))
    twin = lax.ppermute(send, "gz", swap)
    same = jnp.stack(ordered([jnp.where(straight, m, c) for c, m in zip(crossed, mine)], here))
    parity = lax.broadcasted_iota(jnp.int32, (tiles, 2, height, columns), 1)
    result = jnp.where(parity == core, same[:, None], twin[:, None])
    return result.astype(jnp.float32).reshape(2 * tiles, height, columns)


def one_plane_each(mesh, view_data, estimate, psf_taps, offsets):
    tiles, views, depth = mesh.shape["tiles"], mesh.shape["views"], mesh.shape["gz"]
    planes = estimate.shape[0] // (mesh.shape["groups"] * depth)
    height, columns = estimate.shape[1] // tiles, estimate.shape[2]
    return (
        depth == 2
        and views == 2
        and planes == 2 * tiles
        and tiles & (tiles - 1) == 0
        and height == columns
        and height % (16 * offsets.shape[1]) == 0
        and columns == 128
        and 8 * psf_taps.shape[-1] + offsets.shape[1] <= columns
    )


def solution(mesh):
    in_specs = (
        P(("groups", "views"), "tiles", "gz", None, None),
        P(("groups", "gz"), "tiles", None),
        P("views", None, None, None),
        P("views", None),
    )
    out_specs = P(("groups", "gz"), "tiles", None)

    def step(*arrays):
        if not one_plane_each(mesh, *arrays):
            return jax.shard_map(shards, mesh=mesh, in_specs=in_specs, out_specs=out_specs, check_vma=False)(*arrays)
        body = jax.shard_map(plane_shards, mesh=mesh, in_specs=in_specs, out_specs=out_specs, check_vma=False)
        return body(*arrays)

    return step
```

```python
import functools

import jax
import jax.numpy as jnp
from jax import lax
from jax.experimental import pallas as pl
from jax.experimental.pallas import tpu as pltpu
from jax.sharding import PartitionSpec as P


ITERS = 2
CAP = 4


TV_WEIGHT = 0.1
SMOOTH_SQUARE = 0.0025


def with_halo(cells, sides, width):
    for axis, dim in sides:
        count = lax.axis_size(axis)
        ends = count - 1
        head = lax.slice_in_dim(cells, 0, width, axis=dim)
        tail = lax.slice_in_dim(cells, cells.shape[dim] - width, cells.shape[dim], axis=dim)
        cells = jnp.concatenate(
            [
                lax.ppermute(tail, axis, [(i, (i + 1) % count) for i in range(ends)]),
                cells,
                lax.ppermute(head, axis, [((i + 1) % count, i) for i in range(ends)]),
            ],
            axis=dim,
        )
    return cells


def toeplitz_matrix(profile, length):
    half_width = (profile.shape[0] - 1) // 2
    position = jnp.arange(length, dtype=jnp.int32)
    offset = position[None, :] - position[:, None] + half_width
    tap_index = jnp.arange(profile.shape[0], dtype=jnp.int32)
    picked = (offset[:, :, None] == tap_index[None, None, :]).astype(jnp.float32)
    return jnp.sum(picked * profile[None, None, :], axis=2).astype(jnp.bfloat16)


def curvature(padded):
    anchor = padded[:-1, :-1, :-1]
    grad_z = padded[1:, :-1, :-1] - anchor
    grad_y = padded[:-1, 1:, :-1] - anchor
    grad_x = padded[:-1, :-1, 1:] - anchor
    magnitude = jnp.sqrt(grad_z * grad_z + grad_y * grad_y + grad_x * grad_x + SMOOTH_SQUARE)
    unit_z = grad_z / magnitude
    unit_y = grad_y / magnitude
    unit_x = grad_x / magnitude
    return (
        unit_z[1:, 1:, 1:]
        - unit_z[:-1, 1:, 1:]
        + (unit_y[1:, 1:, 1:] - unit_y[1:, :-1, 1:])
        + (unit_x[1:, 1:, 1:] - unit_x[1:, 1:, :-1])
    )


def view_correction(view_tile, observed, kernel_y, kernel_x):
    blurred = jnp.zeros(view_tile.shape, jnp.float32)
    for term_index in range(2):
        half_blur = jnp.einsum(
            "yk,zkx->zyx", kernel_y[term_index], view_tile, preferred_element_type=jnp.float32
        ).astype(jnp.bfloat16)
        blurred = blurred + jnp.einsum(
            "zyk,xk->zyx", half_blur, kernel_x[term_index], preferred_element_type=jnp.float32
        )
    quotient = (observed.astype(jnp.float32) / blurred).astype(jnp.bfloat16)
    log_sum = jnp.zeros(view_tile.shape, jnp.float32)
    for term_index in range(2):
        half_back = jnp.einsum(
            "ky,zkx->zyx", kernel_y[term_index], quotient, preferred_element_type=jnp.float32
        ).astype(jnp.bfloat16)
        log_sum = log_sum + jnp.einsum(
            "zyk,kx->zyx", half_back, kernel_x[term_index], preferred_element_type=jnp.float32
        )
    return log_sum.astype(jnp.bfloat16)


def shards(view_data, estimate, psf_taps, offsets):
    owners = lax.axis_size("tiles")
    view_count = lax.axis_size("views")
    observed = view_data[0, 0]
    planes, height, columns = estimate.shape
    view_shift = offsets[0]
    blocks = view_shift.shape[0]
    block_rows = height // blocks
    slot_count = owners * CAP
    kernel_y = jnp.stack(
        [toeplitz_matrix(psf_taps[0, term_index, 0], height) for term_index in range(2)]
    )
    kernel_x = jnp.stack(
        [toeplitz_matrix(psf_taps[0, term_index, 1], columns) for term_index in range(2)]
    )
    position = jnp.arange(blocks, dtype=jnp.int32)
    same_owner = view_shift[:, None] == view_shift[None, :]
    before = position[None, :] < position[:, None]
    slot_rank = jnp.sum((same_owner & before).astype(jnp.int32), axis=1)
    member = lax.axis_index("tiles")
    target = (member + view_shift) % owners
    source_tile = (member - view_shift) % owners
    slot_index = jnp.arange(slot_count, dtype=jnp.int32)
    to_owner = ((target * CAP + slot_rank)[:, None] == slot_index[None, :]).astype(jnp.bfloat16)
    from_tile = ((source_tile * CAP + slot_rank)[:, None] == slot_index[None, :]).astype(
        jnp.bfloat16
    )
    current = estimate
    for _ in range(ITERS):
        padded = with_halo(current, (("tiles", 1), ("gz", 0)), 1)
        padded = jnp.pad(padded, ((0, 0), (0, 0), (1, 1)))
        owned_blocks = current.astype(jnp.bfloat16).reshape(planes, blocks, block_rows, columns)
        outgoing = jnp.einsum(
            "sk,zsrx->kzrx", from_tile, owned_blocks, preferred_element_type=jnp.float32
        ).astype(jnp.bfloat16)
        incoming = lax.all_to_all(
            outgoing.reshape(owners, CAP, planes, block_rows, columns),
            "tiles",
            split_axis=0,
            concat_axis=0,
            tiled=True,
        )
        view_tile = jnp.einsum(
            "sk,kzrx->zsrx",
            to_owner,
            incoming.reshape(slot_count, planes, block_rows, columns),
            preferred_element_type=jnp.float32,
        ).astype(jnp.bfloat16)
        view_tile = view_tile.reshape(planes, height, columns)
        correction = view_correction(view_tile, observed, kernel_y, kernel_x)
        correction = correction.reshape(planes, blocks, block_rows, columns)
        returned = jnp.einsum(
            "sk,zsrx->kzrx", to_owner, correction, preferred_element_type=jnp.float32
        ).astype(jnp.bfloat16)
        gathered = lax.all_to_all(
            returned.reshape(owners, CAP, planes, block_rows, columns),
            "tiles",
            split_axis=0,
            concat_axis=0,
            tiled=True,
        )
        owned_rows = jnp.einsum(
            "sk,kzrx->zsrx",
            from_tile,
            gathered.reshape(slot_count, planes, block_rows, columns),
            preferred_element_type=jnp.float32,
        ).reshape(planes, height, columns)
        log_values = jnp.log(owned_rows)
        share_rows = height // view_count
        log_part = lax.psum_scatter(log_values, "views", scatter_dimension=1, tiled=True)
        first_row = lax.axis_index("views") * share_rows
        window = lax.dynamic_slice_in_dim(padded, first_row, share_rows + 2, 1)
        damping = 1.0 - TV_WEIGHT * curvature(window)
        rows_now = lax.dynamic_slice_in_dim(current, first_row, share_rows, 1)
        updated = rows_now * jnp.exp(log_part / view_count) / damping
        current = lax.all_gather(updated, "views", axis=1, tiled=True)
    return current


INFO_ROWS = 16
PLANE_UNIT = 65534.0
DATA_UNIT = 1024.0
TAP_UNIT = 8192.0
CHUNK = 32
VMEM = pl.BlockSpec(memory_space=pltpu.VMEM)
SMEM = pl.BlockSpec(memory_space=pltpu.SMEM)
LIMIT = pltpu.CompilerParams(vmem_limit_bytes=16 * 2**20)


def matrices_kernel(taps, info_ref, out_ref):
    views, columns = info_ref.shape
    length = out_ref.shape[-2] // 2
    half_width = (taps - 1) // 2
    row = lax.broadcasted_iota(jnp.int32, (length, columns), 0)
    column = lax.broadcasted_iota(jnp.int32, (length, columns), 1)
    band = jnp.abs(row - column) <= half_width
    for v in range(views):
        profile = jnp.broadcast_to(info_ref[v : v + 1, :], (8, columns))
        for kind, (flipped, axis) in enumerate([(0, 0), (1, 1), (1, 0), (0, 1)]):
            for r in range(2):
                lane = (4 * flipped + 2 * r + axis) * taps + half_width
                spread = jnp.broadcast_to(pltpu.roll(profile, columns - lane, 1)[0:1], (length, columns))
                rolled = pltpu.roll(spread, 0, 1, stride=1, stride_axis=0)
                rolled = jnp.where(band, rolled, 0.0).astype(out_ref.dtype)
                out_ref[v, kind, r * length : (r + 1) * length, :] = rolled


def blur_matrices(taps, length, info):
    views, columns = info.shape
    return pl.pallas_call(
        functools.partial(matrices_kernel, taps),
        out_shape=jax.ShapeDtypeStruct((views, 4, 2 * length, columns), jnp.bfloat16),
        in_specs=[VMEM],
        out_specs=VMEM,
        compiler_params=LIMIT,
        name="blur_matrices",
    )(info)


def pack_kernel(where_ref, *refs):
    pieces, give_ref = refs[:-1], refs[-1]
    height = give_ref.shape[2]
    other = pl.multiple_of((2 - where_ref[1]) * height, height)
    for k, piece in enumerate(pieces):
        give_ref[k, 0] = piece[0:height, :]
        give_ref[k, 1] = piece[pl.ds(other, height), :]


def pack(where, pieces):
    rows, columns = pieces[0].shape
    return pl.pallas_call(
        pack_kernel,
        out_shape=jax.ShapeDtypeStruct((len(pieces), 2, rows // 3, columns), pieces[0].dtype),
        in_specs=[SMEM] + [VMEM] * len(pieces),
        out_specs=VMEM,
        compiler_params=LIMIT,
        name="pack",
    )(where, *pieces)


def correction_kernel(where_ref, offsets_ref, current_ref, matrices_ref, *refs):
    views, blocks = offsets_ref.shape
    tiles, height, columns = current_ref.shape
    pieces, swapped_ref, log_ref, work = refs[:tiles], refs[tiles], refs[tiles + 1], refs[tiles + 2 :]
    rows = height // blocks
    me = where_ref[0]
    own = pl.multiple_of((1 + where_ref[1]) * height, height)
    shift = [[offsets_ref[w, s] for s in range(blocks)] for w in range(views)]
    planes = [work[3 * w] for w in range(views)]
    halves = [work[3 * w + 1] for w in range(views)]
    logs = [work[3 * w + 2] for w in range(views)]

    def first(w, kind):
        half = jnp.dot(matrices_ref[w, kind], planes[w][...], preferred_element_type=jnp.float32)
        half = half.astype(jnp.bfloat16)
        for k in range(tiles):
            for r in range(2):
                halves[w][k * height : (k + 1) * height, r * columns : (r + 1) * columns] = half[
                    r * height : (r + 1) * height, k * columns : (k + 1) * columns
                ]

    for w in range(views):
        for k in range(tiles):
            tile = lax.bitwise_xor(me, k)
            for s in range(blocks):
                owner = lax.rem(tile + shift[w][s], tiles)
                planes[w][s * rows : (s + 1) * rows, k * columns : (k + 1) * columns] = current_ref[
                    owner, s * rows : (s + 1) * rows, :
                ]
    for w in range(views):
        first(w, 0)
    for w in range(views):
        blurred = jnp.dot(halves[w][...], matrices_ref[w, 1], preferred_element_type=jnp.float32)
        for k in range(tiles):
            observed = pieces[k][pl.ds(own, height), :] if w == 0 else swapped_ref[k, 1]
            observed = observed.astype(jnp.float32) * (1.0 / DATA_UNIT)
            quotient = observed / blurred[k * height : (k + 1) * height]
            planes[w][:, k * columns : (k + 1) * columns] = quotient.astype(jnp.bfloat16)
    for w in range(views):
        first(w, 2)
    for w in range(views):
        back = jnp.dot(halves[w][...], matrices_ref[w, 3], preferred_element_type=jnp.float32)
        logs[w][...] = jnp.log(back.astype(jnp.bfloat16).astype(jnp.float32))
    for o in range(tiles):
        for s in range(blocks):
            total = None
            for w in range(views):
                tile = lax.rem(o - shift[w][s] + tiles, tiles)
                start = pl.multiple_of(lax.bitwise_xor(tile, me) * height + s * rows, rows)
                part = logs[w][pl.ds(start, rows), :]
                total = part if total is None else total + part
            log_ref[o * height + s * rows : o * height + (s + 1) * rows, :] = total


def correction_logs(where, offsets, current, matrices, pieces, swapped):
    tiles, height, columns = current.shape
    scratch = [
        pltpu.VMEM((height, tiles * columns), jnp.bfloat16),
        pltpu.VMEM((tiles * height, 2 * columns), jnp.bfloat16),
        pltpu.VMEM((tiles * height, columns), jnp.float32),
    ]
    return pl.pallas_call(
        correction_kernel,
        out_shape=jax.ShapeDtypeStruct((tiles * height, columns), jnp.float32),
        in_specs=[SMEM, SMEM] + [VMEM] * (3 + tiles),
        out_specs=VMEM,
        scratch_shapes=scratch * offsets.shape[0],
        cost_estimate=pl.CostEstimate(flops=300_000_000, bytes_accessed=1_500_000, transcendentals=0),
        compiler_params=LIMIT,
        name="correction",
    )(where, offsets, current, matrices, *pieces, swapped)


def update_kernel(views, core_ref, current_ref, twin_ref, other_ref, log_ref, *new_refs):
    total, columns = current_ref.shape
    first = core_ref[0] == 0
    row = lax.broadcasted_iota(jnp.int32, (CHUNK, columns), 0)
    column = lax.broadcasted_iota(jnp.int32, (CHUNK, columns), 1)

    def scale(z, y, x):
        return lax.rsqrt(z * z + y * y + x * x + SMOOTH_SQUARE)

    def pick(low, high, start, size):
        return jnp.where(first, low[start : start + size, :], high[start : start + size, :])

    def next_row(x, following):
        return jnp.where(row == CHUNK - 1, following, pltpu.roll(x, CHUNK - 1, 0))

    def next_column(x):
        return jnp.where(column == columns - 1, 0.0, pltpu.roll(x, columns - 1, 1))

    def edge(x):
        return x * lax.rsqrt(x * x + SMOOTH_SQUARE)

    carry = edge(current_ref[0:1, :])
    for start in range(0, total, CHUNK):
        stop = start + CHUNK
        current = current_ref[start:stop, :]
        above = pick(twin_ref, other_ref, start, CHUNK)
        below = pick(other_ref, twin_ref, start, CHUNK)
        if stop < total:
            current_next, below_next = current_ref[stop : stop + 1, :], pick(other_ref, twin_ref, stop, 1)
        else:
            current_next = below_next = jnp.zeros((1, columns), jnp.float32)
        grad_z = above - current
        grad_y = next_row(current, current_next) - current
        grad_x = next_column(current) - current
        inverse = scale(grad_z, grad_y, grad_x)
        unit_y, unit_x = grad_y * inverse, grad_x * inverse
        before_y = jnp.where(row == 0, carry, pltpu.roll(unit_y, 1, 0))
        before_x = jnp.where(column == 0, edge(current), pltpu.roll(unit_x, 1, 1))
        carry = unit_y[CHUNK - 1 : CHUNK, :]
        lower_z = current - below
        lower = lower_z * scale(lower_z, next_row(below, below_next) - below, next_column(below) - below)
        divergence = grad_z * inverse - lower + (unit_y - before_y) + (unit_x - before_x)
        damping = 1.0 - TV_WEIGHT * divergence
        new = current * jnp.exp(log_ref[start:stop, :] * (1.0 / views)) / damping
        for ref in new_refs:
            ref[start:stop, :] = new.astype(ref.dtype)


def update(views, core, current, twin, other, logs, dtypes):
    return pl.pallas_call(
        functools.partial(update_kernel, views),
        out_shape=[jax.ShapeDtypeStruct(current.shape, dtype) for dtype in dtypes],
        in_specs=[SMEM] + [VMEM] * 4,
        out_specs=[VMEM] * len(dtypes),
        compiler_params=LIMIT,
        name="update",
    )(core, current, twin, other, logs)


def plane_shards(view_data, estimate, psf_taps, offsets):
    tiles, views = lax.axis_size("tiles"), lax.axis_size("views")
    square = ("tiles", "views", "gz")
    _, height, columns = estimate.shape
    blocks = offsets.shape[1]
    taps = psf_taps.shape[-1]
    tile, view, core = lax.axis_index("tiles"), lax.axis_index("views"), lax.axis_index("gz")
    swap = [(0, 1), (1, 0)]

    def device(t, v, g):
        return (t * views + v) * 2 + g

    def ordered(pieces, shift):
        placed = []
        for i in range(tiles):
            chosen = pieces[i]
            for s in range(1, tiles):
                chosen = jnp.where(shift == s, pieces[i ^ s], chosen)
            placed.append(chosen)
        return placed

    def exchange(pick):
        pieces = []
        for k in range(tiles):
            pairs = [(device(t, v, g), device(t ^ k, g, v)) for t in range(tiles) for v in range(2) for g in range(2)]
            pieces.append(lax.ppermute(pick(k), square, pairs))
        return pieces

    def end_of(chain):
        return jnp.where(chain == 0, 0, tiles - 1)

    where = jnp.stack([tile, core]).astype(jnp.int32)
    flag = core.reshape(1).astype(jnp.int32)

    wide = estimate.reshape(tiles, 2, height, columns)
    wide = lax.dynamic_index_in_dim(wide, view, 1, keepdims=True)
    wide = jnp.round((wide - 1.0) * PLANE_UNIT).astype(jnp.int16)
    data = view_data.reshape(tiles, 2, height, columns).astype(jnp.float32)
    data = (data * DATA_UNIT).astype(jnp.int16)
    payload = jnp.concatenate([wide, data], axis=1).reshape(tiles, 3 * height, columns)
    payload, psf_taps, offsets = lax.optimization_barrier((payload, psf_taps, offsets))

    def for_tile(k):
        place = lax.bitwise_xor(lax.bitwise_xor(tile, k), end_of(core))
        return lax.dynamic_index_in_dim(payload, place, 0, keepdims=False)

    pieces = exchange(for_tile)

    profiles = [psf_taps.reshape(-1), psf_taps[..., ::-1].reshape(-1)]
    info = [lax.reduce_precision(p, 8, 7) * TAP_UNIT for p in profiles]
    info = jnp.concatenate([*info, offsets.reshape(-1).astype(jnp.float32)])
    info = jnp.pad(info, (0, columns - info.shape[0])).astype(jnp.int16)
    info = jnp.broadcast_to(info, (INFO_ROWS, columns))
    note = lax.ppermute(info, "views", swap)
    straight = view == core
    notes = jnp.stack([jnp.where(straight, info[0], note[0]), jnp.where(straight, note[0], info[0])])
    notes = notes.astype(jnp.float32)
    shifts = notes[:, 8 * taps : 8 * taps + blocks].astype(jnp.int32)
    matrices = blur_matrices(taps, height, notes * (1.0 / TAP_UNIT))

    give = pack(where, pieces)
    swapped = lax.ppermute(give, "gz", swap)

    path = [(t, 0) for t in range(tiles)] + [(t, 1) for t in reversed(range(tiles))]
    hops = []
    for here, there in zip(path[:-1], path[1:]):
        one, two = device(*here, 1), device(*there, 0)
        hops += [(one, two), (two, one)]

    def plane_of(coded):
        return coded.astype(jnp.float32) * (1.0 / PLANE_UNIT) + 1.0

    plane = jnp.concatenate(ordered([piece[:height] for piece in pieces], tile))
    twin = plane_of(jnp.concatenate(ordered([swapped[k, 0] for k in range(tiles)], tile)))
    current = plane_of(plane)
    narrow = current.astype(jnp.bfloat16)
    at_end = (tile == 0) & (core == view)
    for iteration in range(ITERS):
        first, last = iteration == 0, iteration == ITERS - 1
        other = lax.ppermute(plane, square, hops)
        if not first:
            twin = lax.ppermute(current, "gz", swap)
        other = jnp.where(at_end, 0.0, plane_of(other) if first else other.astype(jnp.float32) + 1.0)
        logs = correction_logs(where, shifts, narrow.reshape(tiles, height, columns), matrices, pieces, swapped)
        current, *rest = update(
            views, flag, current, twin, other, logs, [jnp.float32] if last else [jnp.float32, jnp.bfloat16]
        )
        if not last:
            narrow = rest[0]
            plane = (current - 1.0).astype(jnp.float16)

    result = current.astype(jnp.float16).reshape(tiles, height, columns)
    pieces = []
    for k in range(tiles):
        piece = lax.dynamic_index_in_dim(result, lax.bitwise_xor(tile, k), 0)
        pieces.append(lax.ppermute(piece, "tiles", [(t, t ^ k) for t in range(tiles)]) if k else piece)
    mine = jnp.concatenate(pieces)
    crossed = [lax.ppermute(pieces[0], "views", swap)]
    crossed.append(lax.ppermute(mine[1:], "views", swap))
    crossed = [crossed[0][0], *[crossed[1][k] for k in range(tiles - 1)]]
    mine = [mine[k] for k in range(tiles)]
    here = lax.bitwise_xor(tile, end_of(core))
    send = [jnp.where(straight, c, m) for c, m in zip(crossed, mine)]
    send = jnp.stack(ordered(send, lax.bitwise_xor(tile, end_of(1 - core))))
    twin = lax.ppermute(send, "gz", swap)
    same = jnp.stack(ordered([jnp.where(straight, m, c) for c, m in zip(crossed, mine)], here))
    parity = lax.broadcasted_iota(jnp.int32, (tiles, 2, height, columns), 1)
    result = jnp.where(parity == core, same[:, None], twin[:, None])
    return result.astype(jnp.float32).reshape(2 * tiles, height, columns)


def one_plane_each(mesh, view_data, estimate, psf_taps, offsets):
    tiles, views, depth = mesh.shape["tiles"], mesh.shape["views"], mesh.shape["gz"]
    planes = estimate.shape[0] // (mesh.shape["groups"] * depth)
    height, columns = estimate.shape[1] // tiles, estimate.shape[2]
    return (
        depth == 2
        and views == 2
        and planes == 2 * tiles
        and tiles & (tiles - 1) == 0
        and height == columns
        and height % (16 * offsets.shape[1]) == 0
        and columns == 128
        and 8 * psf_taps.shape[-1] + offsets.shape[1] <= columns
    )


def solution(mesh):
    in_specs = (
        P(("groups", "views"), "tiles", "gz", None, None),
        P(("groups", "gz"), "tiles", None),
        P("views", None, None, None),
        P("views", None),
    )
    out_specs = P(("groups", "gz"), "tiles", None)

    def step(*arrays):
        if not one_plane_each(mesh, *arrays):
            return jax.shard_map(shards, mesh=mesh, in_specs=in_specs, out_specs=out_specs, check_vma=False)(*arrays)
        body = jax.shard_map(plane_shards, mesh=mesh, in_specs=in_specs, out_specs=out_specs, check_vma=False)
        return body(*arrays)

    return step
```

```python
import functools

import jax
import jax.numpy as jnp
from jax import lax
from jax.experimental import pallas as pl
from jax.experimental.pallas import tpu as pltpu
from jax.sharding import PartitionSpec as P


ITERS = 2
CAP = 4


TV_WEIGHT = 0.1
SMOOTH_SQUARE = 0.0025


def with_halo(cells, sides, width):
    for axis, dim in sides:
        count = lax.axis_size(axis)
        ends = count - 1
        head = lax.slice_in_dim(cells, 0, width, axis=dim)
        tail = lax.slice_in_dim(cells, cells.shape[dim] - width, cells.shape[dim], axis=dim)
        cells = jnp.concatenate(
            [
                lax.ppermute(tail, axis, [(i, (i + 1) % count) for i in range(ends)]),
                cells,
                lax.ppermute(head, axis, [((i + 1) % count, i) for i in range(ends)]),
            ],
            axis=dim,
        )
    return cells


def toeplitz_matrix(profile, length):
    half_width = (profile.shape[0] - 1) // 2
    position = jnp.arange(length, dtype=jnp.int32)
    offset = position[None, :] - position[:, None] + half_width
    tap_index = jnp.arange(profile.shape[0], dtype=jnp.int32)
    picked = (offset[:, :, None] == tap_index[None, None, :]).astype(jnp.float32)
    return jnp.sum(picked * profile[None, None, :], axis=2).astype(jnp.bfloat16)


def curvature(padded):
    anchor = padded[:-1, :-1, :-1]
    grad_z = padded[1:, :-1, :-1] - anchor
    grad_y = padded[:-1, 1:, :-1] - anchor
    grad_x = padded[:-1, :-1, 1:] - anchor
    magnitude = jnp.sqrt(grad_z * grad_z + grad_y * grad_y + grad_x * grad_x + SMOOTH_SQUARE)
    unit_z = grad_z / magnitude
    unit_y = grad_y / magnitude
    unit_x = grad_x / magnitude
    return (
        unit_z[1:, 1:, 1:]
        - unit_z[:-1, 1:, 1:]
        + (unit_y[1:, 1:, 1:] - unit_y[1:, :-1, 1:])
        + (unit_x[1:, 1:, 1:] - unit_x[1:, 1:, :-1])
    )


def view_correction(view_tile, observed, kernel_y, kernel_x):
    blurred = jnp.zeros(view_tile.shape, jnp.float32)
    for term_index in range(2):
        half_blur = jnp.einsum(
            "yk,zkx->zyx", kernel_y[term_index], view_tile, preferred_element_type=jnp.float32
        ).astype(jnp.bfloat16)
        blurred = blurred + jnp.einsum(
            "zyk,xk->zyx", half_blur, kernel_x[term_index], preferred_element_type=jnp.float32
        )
    quotient = (observed.astype(jnp.float32) / blurred).astype(jnp.bfloat16)
    log_sum = jnp.zeros(view_tile.shape, jnp.float32)
    for term_index in range(2):
        half_back = jnp.einsum(
            "ky,zkx->zyx", kernel_y[term_index], quotient, preferred_element_type=jnp.float32
        ).astype(jnp.bfloat16)
        log_sum = log_sum + jnp.einsum(
            "zyk,kx->zyx", half_back, kernel_x[term_index], preferred_element_type=jnp.float32
        )
    return log_sum.astype(jnp.bfloat16)


def shards(view_data, estimate, psf_taps, offsets):
    owners = lax.axis_size("tiles")
    view_count = lax.axis_size("views")
    observed = view_data[0, 0]
    planes, height, columns = estimate.shape
    view_shift = offsets[0]
    blocks = view_shift.shape[0]
    block_rows = height // blocks
    slot_count = owners * CAP
    kernel_y = jnp.stack(
        [toeplitz_matrix(psf_taps[0, term_index, 0], height) for term_index in range(2)]
    )
    kernel_x = jnp.stack(
        [toeplitz_matrix(psf_taps[0, term_index, 1], columns) for term_index in range(2)]
    )
    position = jnp.arange(blocks, dtype=jnp.int32)
    same_owner = view_shift[:, None] == view_shift[None, :]
    before = position[None, :] < position[:, None]
    slot_rank = jnp.sum((same_owner & before).astype(jnp.int32), axis=1)
    member = lax.axis_index("tiles")
    target = (member + view_shift) % owners
    source_tile = (member - view_shift) % owners
    slot_index = jnp.arange(slot_count, dtype=jnp.int32)
    to_owner = ((target * CAP + slot_rank)[:, None] == slot_index[None, :]).astype(jnp.bfloat16)
    from_tile = ((source_tile * CAP + slot_rank)[:, None] == slot_index[None, :]).astype(
        jnp.bfloat16
    )
    current = estimate
    for _ in range(ITERS):
        padded = with_halo(current, (("tiles", 1), ("gz", 0)), 1)
        padded = jnp.pad(padded, ((0, 0), (0, 0), (1, 1)))
        owned_blocks = current.astype(jnp.bfloat16).reshape(planes, blocks, block_rows, columns)
        outgoing = jnp.einsum(
            "sk,zsrx->kzrx", from_tile, owned_blocks, preferred_element_type=jnp.float32
        ).astype(jnp.bfloat16)
        incoming = lax.all_to_all(
            outgoing.reshape(owners, CAP, planes, block_rows, columns),
            "tiles",
            split_axis=0,
            concat_axis=0,
            tiled=True,
        )
        view_tile = jnp.einsum(
            "sk,kzrx->zsrx",
            to_owner,
            incoming.reshape(slot_count, planes, block_rows, columns),
            preferred_element_type=jnp.float32,
        ).astype(jnp.bfloat16)
        view_tile = view_tile.reshape(planes, height, columns)
        correction = view_correction(view_tile, observed, kernel_y, kernel_x)
        correction = correction.reshape(planes, blocks, block_rows, columns)
        returned = jnp.einsum(
            "sk,zsrx->kzrx", to_owner, correction, preferred_element_type=jnp.float32
        ).astype(jnp.bfloat16)
        gathered = lax.all_to_all(
            returned.reshape(owners, CAP, planes, block_rows, columns),
            "tiles",
            split_axis=0,
            concat_axis=0,
            tiled=True,
        )
        owned_rows = jnp.einsum(
            "sk,kzrx->zsrx",
            from_tile,
            gathered.reshape(slot_count, planes, block_rows, columns),
            preferred_element_type=jnp.float32,
        ).reshape(planes, height, columns)
        log_values = jnp.log(owned_rows)
        share_rows = height // view_count
        log_part = lax.psum_scatter(log_values, "views", scatter_dimension=1, tiled=True)
        first_row = lax.axis_index("views") * share_rows
        window = lax.dynamic_slice_in_dim(padded, first_row, share_rows + 2, 1)
        damping = 1.0 - TV_WEIGHT * curvature(window)
        rows_now = lax.dynamic_slice_in_dim(current, first_row, share_rows, 1)
        updated = rows_now * jnp.exp(log_part / view_count) / damping
        current = lax.all_gather(updated, "views", axis=1, tiled=True)
    return current


INFO_ROWS = 16
PLANE_UNIT = 65534.0
DATA_UNIT = 1024.0
TAP_UNIT = 8192.0
CHUNK = 32
VMEM = pl.BlockSpec(memory_space=pltpu.VMEM)
SMEM = pl.BlockSpec(memory_space=pltpu.SMEM)
LIMIT = pltpu.CompilerParams(vmem_limit_bytes=16 * 2**20)


def matrices_kernel(taps, info_ref, out_ref):
    views, columns = info_ref.shape
    length = out_ref.shape[-2] // 2
    half_width = (taps - 1) // 2
    row = lax.broadcasted_iota(jnp.int32, (length, columns), 0)
    column = lax.broadcasted_iota(jnp.int32, (length, columns), 1)
    band = jnp.abs(row - column) <= half_width
    for v in range(views):
        profile = jnp.broadcast_to(info_ref[v : v + 1, :], (8, columns))
        for kind, (flipped, axis) in enumerate([(0, 0), (1, 1), (1, 0), (0, 1)]):
            for r in range(2):
                lane = (4 * flipped + 2 * r + axis) * taps + half_width
                spread = jnp.broadcast_to(pltpu.roll(profile, columns - lane, 1)[0:1], (length, columns))
                rolled = pltpu.roll(spread, 0, 1, stride=1, stride_axis=0)
                rolled = jnp.where(band, rolled, 0.0).astype(out_ref.dtype)
                out_ref[v, kind, r * length : (r + 1) * length, :] = rolled


def blur_matrices(taps, length, info):
    views, columns = info.shape
    return pl.pallas_call(
        functools.partial(matrices_kernel, taps),
        out_shape=jax.ShapeDtypeStruct((views, 4, 2 * length, columns), jnp.bfloat16),
        in_specs=[VMEM],
        out_specs=VMEM,
        compiler_params=LIMIT,
        name="blur_matrices",
    )(info)


def correction_kernel(tiles, tile_ref, offsets_ref, current_ref, matrices_ref, *refs):
    views, blocks = offsets_ref.shape
    data, log_ref, work = refs[: views * tiles], refs[views * tiles], refs[views * tiles + 1 :]
    height, columns = data[0].shape
    rows = height // blocks
    me = tile_ref[0]
    shift = [[offsets_ref[w, s] for s in range(blocks)] for w in range(views)]
    planes = [work[3 * w] for w in range(views)]
    halves = [work[3 * w + 1] for w in range(views)]
    logs = [work[3 * w + 2] for w in range(views)]

    def first(w, kind):
        half = jnp.dot(matrices_ref[w, kind], planes[w][...], preferred_element_type=jnp.float32)
        half = half.astype(jnp.bfloat16)
        for k in range(tiles):
            for r in range(2):
                halves[w][k * height : (k + 1) * height, r * columns : (r + 1) * columns] = half[
                    r * height : (r + 1) * height, k * columns : (k + 1) * columns
                ]

    for w in range(views):
        for k in range(tiles):
            tile = lax.bitwise_xor(me, k)
            for s in range(blocks):
                owner = lax.rem(tile + shift[w][s], tiles)
                planes[w][s * rows : (s + 1) * rows, k * columns : (k + 1) * columns] = current_ref[
                    owner, s * rows : (s + 1) * rows, :
                ]
    for w in range(views):
        first(w, 0)
    for w in range(views):
        blurred = jnp.dot(halves[w][...], matrices_ref[w, 1], preferred_element_type=jnp.float32)
        for k in range(tiles):
            quotient = data[w * tiles + k][...].astype(jnp.float32) / blurred[k * height : (k + 1) * height]
            planes[w][:, k * columns : (k + 1) * columns] = quotient.astype(jnp.bfloat16)
    for w in range(views):
        first(w, 2)
    for w in range(views):
        back = jnp.dot(halves[w][...], matrices_ref[w, 3], preferred_element_type=jnp.float32)
        logs[w][...] = jnp.log(back.astype(jnp.bfloat16).astype(jnp.float32))
    for o in range(tiles):
        for s in range(blocks):
            total = None
            for w in range(views):
                tile = lax.rem(o - shift[w][s] + tiles, tiles)
                start = pl.multiple_of(lax.bitwise_xor(tile, me) * height + s * rows, rows)
                part = logs[w][pl.ds(start, rows), :]
                total = part if total is None else total + part
            log_ref[o * height + s * rows : o * height + (s + 1) * rows, :] = total


def correction_logs(tile, offsets, current, matrices, data):
    tiles, height, columns = current.shape
    scratch = [
        pltpu.VMEM((height, tiles * columns), jnp.bfloat16),
        pltpu.VMEM((tiles * height, 2 * columns), jnp.bfloat16),
        pltpu.VMEM((tiles * height, columns), jnp.float32),
    ]
    return pl.pallas_call(
        functools.partial(correction_kernel, tiles),
        out_shape=jax.ShapeDtypeStruct((tiles * height, columns), jnp.float32),
        in_specs=[SMEM, SMEM] + [VMEM] * (2 + len(data)),
        out_specs=VMEM,
        scratch_shapes=scratch * offsets.shape[0],
        cost_estimate=pl.CostEstimate(flops=300_000_000, bytes_accessed=1_500_000, transcendentals=0),
        compiler_params=LIMIT,
        name="correction",
    )(tile, offsets, current, matrices, *data)


def update_kernel(views, core_ref, current_ref, twin_ref, other_ref, log_ref, *new_refs):
    total, columns = current_ref.shape
    first = core_ref[0] == 0
    row = lax.broadcasted_iota(jnp.int32, (CHUNK, columns), 0)
    column = lax.broadcasted_iota(jnp.int32, (CHUNK, columns), 1)

    def scale(z, y, x):
        return lax.rsqrt(z * z + y * y + x * x + SMOOTH_SQUARE)

    def pick(low, high, start, size):
        return jnp.where(first, low[start : start + size, :], high[start : start + size, :])

    def next_row(x, following):
        return jnp.where(row == CHUNK - 1, following, pltpu.roll(x, CHUNK - 1, 0))

    def next_column(x):
        return jnp.where(column == columns - 1, 0.0, pltpu.roll(x, columns - 1, 1))

    def edge(x):
        return x * lax.rsqrt(x * x + SMOOTH_SQUARE)

    carry = edge(current_ref[0:1, :])
    for start in range(0, total, CHUNK):
        stop = start + CHUNK
        current = current_ref[start:stop, :]
        above = pick(twin_ref, other_ref, start, CHUNK)
        below = pick(other_ref, twin_ref, start, CHUNK)
        if stop < total:
            current_next, below_next = current_ref[stop : stop + 1, :], pick(other_ref, twin_ref, stop, 1)
        else:
            current_next = below_next = jnp.zeros((1, columns), jnp.float32)
        grad_z = above - current
        grad_y = next_row(current, current_next) - current
        grad_x = next_column(current) - current
        inverse = scale(grad_z, grad_y, grad_x)
        unit_y, unit_x = grad_y * inverse, grad_x * inverse
        before_y = jnp.where(row == 0, carry, pltpu.roll(unit_y, 1, 0))
        before_x = jnp.where(column == 0, edge(current), pltpu.roll(unit_x, 1, 1))
        carry = unit_y[CHUNK - 1 : CHUNK, :]
        lower_z = current - below
        lower = lower_z * scale(lower_z, next_row(below, below_next) - below, next_column(below) - below)
        divergence = grad_z * inverse - lower + (unit_y - before_y) + (unit_x - before_x)
        damping = 1.0 - TV_WEIGHT * divergence
        new = current * jnp.exp(log_ref[start:stop, :] * (1.0 / views)) / damping
        for ref in new_refs:
            ref[start:stop, :] = new.astype(ref.dtype)


def update(views, core, current, twin, other, logs, dtypes):
    return pl.pallas_call(
        functools.partial(update_kernel, views),
        out_shape=[jax.ShapeDtypeStruct(current.shape, dtype) for dtype in dtypes],
        in_specs=[SMEM] + [VMEM] * 4,
        out_specs=[VMEM] * len(dtypes),
        compiler_params=LIMIT,
        name="update",
    )(core, current, twin, other, logs)


def plane_shards(view_data, estimate, psf_taps, offsets):
    tiles, views = lax.axis_size("tiles"), lax.axis_size("views")
    square = ("tiles", "views", "gz")
    planes, height, columns = estimate.shape
    blocks = offsets.shape[1]
    taps = psf_taps.shape[-1]
    tile, view, core = lax.axis_index("tiles"), lax.axis_index("views"), lax.axis_index("gz")
    swap = [(0, 1), (1, 0)]

    def device(t, v, g):
        return (t * views + v) * 2 + g

    def ordered(pieces, shift):
        placed = []
        for i in range(tiles):
            chosen = pieces[i]
            for s in range(1, tiles):
                chosen = jnp.where(shift == s, pieces[i ^ s], chosen)
            placed.append(chosen)
        return placed

    def exchange(pick):
        pieces = []
        for k in range(tiles):
            pairs = [(device(t, v, g), device(t ^ k, g, v)) for t in range(tiles) for v in range(2) for g in range(2)]
            pieces.append(lax.ppermute(pick(k), square, pairs))
        return pieces

    def end_of(chain):
        return jnp.where(chain == 0, 0, tiles - 1)

    me = tile.reshape(1).astype(jnp.int32)
    mine_is = lax.bitwise_xor(core, lax.bitwise_xor(tile, end_of(view)) % 2)
    flag = mine_is.reshape(1).astype(jnp.int32)

    wide = estimate.reshape(tiles, 2, height, columns)
    even, odd = (lax.dynamic_index_in_dim(wide, q, 1, keepdims=True) for q in (view, 1 - view))
    wide = jnp.where(lax.broadcasted_iota(jnp.int32, even.shape, 0) % 2 == 0, even, odd)
    wide = jnp.round((wide - 1.0) * PLANE_UNIT).astype(jnp.int16)
    data = view_data.reshape(tiles, 2, height, columns).astype(jnp.float32)
    data = (data * DATA_UNIT).astype(jnp.int16)
    payload = jnp.concatenate([wide, data], axis=1).reshape(tiles, 3 * height, columns)
    payload, psf_taps, offsets = lax.optimization_barrier((payload, psf_taps, offsets))

    def for_tile(k):
        place = lax.bitwise_xor(lax.bitwise_xor(tile, k), end_of(core))
        return lax.dynamic_index_in_dim(payload, place, 0, keepdims=False)

    pieces = exchange(for_tile)

    profiles = [psf_taps.reshape(-1), psf_taps[..., ::-1].reshape(-1)]
    info = [lax.reduce_precision(p, 8, 7) * TAP_UNIT for p in profiles]
    info = jnp.concatenate([*info, offsets.reshape(-1).astype(jnp.float32)])
    info = jnp.pad(info, (0, columns - info.shape[0])).astype(jnp.int16)
    info = jnp.broadcast_to(info, (INFO_ROWS, columns))
    note = lax.ppermute(info, "views", swap)
    straight = view == core
    notes = jnp.stack([jnp.where(straight, info[0], note[0]), jnp.where(straight, note[0], info[0])])
    notes = notes.astype(jnp.float32)
    shifts = notes[:, 8 * taps : 8 * taps + blocks].astype(jnp.int32)
    matrices = blur_matrices(taps, height, notes * (1.0 / TAP_UNIT))

    planes = [piece[:height] for piece in pieces]
    pairs = [piece[height : 3 * height].reshape(2, height, columns) for piece in pieces]
    keep = [lax.dynamic_index_in_dim(pair, mine_is, 0, keepdims=False) for pair in pairs]
    give = [lax.dynamic_index_in_dim(pair, 1 - mine_is, 0, keepdims=False) for pair in pairs]
    got = lax.ppermute(jnp.concatenate([*planes, *give]), "gz", swap)
    length = tiles * height
    twin = got[:length].reshape(tiles, height, columns)
    take = got[length:].reshape(tiles, height, columns)
    data = [x.astype(jnp.float32) * (1.0 / DATA_UNIT) for x in [*keep, *[take[k] for k in range(tiles)]]]
    data = [x.astype(jnp.bfloat16) for x in data]

    path = [(t, 0) for t in range(tiles)] + [(t, 1) for t in reversed(range(tiles))]
    hops = []
    for p, (here, there) in enumerate(zip(path[:-1], path[1:])):
        one, two = device(*here, (p + 1) % 2), device(*there, (p + 1) % 2)
        hops += [(one, two), (two, one)]

    def plane_of(coded):
        return coded.astype(jnp.float32) * (1.0 / PLANE_UNIT) + 1.0

    plane = jnp.concatenate(ordered(planes, tile))
    twin = plane_of(jnp.concatenate(ordered([twin[k] for k in range(tiles)], tile)))
    current = plane_of(plane)
    narrow = current.astype(jnp.bfloat16)
    at_end = (tile == 0) & (core == 0)
    for iteration in range(ITERS):
        first, last = iteration == 0, iteration == ITERS - 1
        other = lax.ppermute(plane, square, hops)
        if not first:
            twin = lax.ppermute(current, "gz", swap)
        other = jnp.where(at_end, 0.0, plane_of(other) if first else other.astype(jnp.float32) + 1.0)
        logs = correction_logs(me, shifts, narrow.reshape(tiles, height, columns), matrices, data)
        current, *rest = update(
            views, flag, current, twin, other, logs, [jnp.float32] if last else [jnp.float32, jnp.bfloat16]
        )
        if not last:
            narrow = rest[0]
            plane = (current - 1.0).astype(jnp.float16)

    result = current.astype(jnp.float16).reshape(tiles, height, columns)
    pieces = []
    for k in range(tiles):
        piece = lax.dynamic_index_in_dim(result, lax.bitwise_xor(tile, k), 0)
        pieces.append(lax.ppermute(piece, "tiles", [(t, t ^ k) for t in range(tiles)]) if k else piece)
    mine = jnp.concatenate(pieces)
    crossed = [lax.ppermute(pieces[0], "views", swap)]
    crossed.append(lax.ppermute(mine[1:], "views", swap))
    crossed = [crossed[0][0], *[crossed[1][k] for k in range(tiles - 1)]]
    mine = [mine[k] for k in range(tiles)]
    here = lax.bitwise_xor(tile, end_of(core))
    send = [jnp.where(straight, c, m) for c, m in zip(crossed, mine)]
    send = jnp.stack(ordered(send, lax.bitwise_xor(tile, end_of(1 - core))))
    twin = lax.ppermute(send, "gz", swap)
    same = jnp.stack(ordered([jnp.where(straight, m, c) for c, m in zip(crossed, mine)], here))
    parity = lax.broadcasted_iota(jnp.int32, (tiles, 2, height, columns), 1)
    turn = lax.broadcasted_iota(jnp.int32, parity.shape, 0) % 2
    result = jnp.where(parity == lax.bitwise_xor(core, turn), same[:, None], twin[:, None])
    return result.astype(jnp.float32).reshape(2 * tiles, height, columns)


def one_plane_each(mesh, view_data, estimate, psf_taps, offsets):
    tiles, views, depth = mesh.shape["tiles"], mesh.shape["views"], mesh.shape["gz"]
    planes = estimate.shape[0] // (mesh.shape["groups"] * depth)
    height, columns = estimate.shape[1] // tiles, estimate.shape[2]
    return (
        depth == 2
        and views == 2
        and planes == 2 * tiles
        and tiles > 1
        and tiles & (tiles - 1) == 0
        and height == columns
        and height % (16 * offsets.shape[1]) == 0
        and columns == 128
        and 8 * psf_taps.shape[-1] + offsets.shape[1] <= columns
    )


def solution(mesh):
    in_specs = (
        P(("groups", "views"), "tiles", "gz", None, None),
        P(("groups", "gz"), "tiles", None),
        P("views", None, None, None),
        P("views", None),
    )
    out_specs = P(("groups", "gz"), "tiles", None)

    def step(*arrays):
        if not one_plane_each(mesh, *arrays):
            return jax.shard_map(shards, mesh=mesh, in_specs=in_specs, out_specs=out_specs, check_vma=False)(*arrays)
        body = jax.shard_map(plane_shards, mesh=mesh, in_specs=in_specs, out_specs=out_specs, check_vma=False)
        return body(*arrays)

    return step
```

```python
import functools

import jax
import jax.numpy as jnp
from jax import lax
from jax.experimental import pallas as pl
from jax.experimental.pallas import tpu as pltpu
from jax.sharding import PartitionSpec as P


ITERS = 2
CAP = 4


TV_WEIGHT = 0.1
SMOOTH_SQUARE = 0.0025


def with_halo(cells, sides, width):
    for axis, dim in sides:
        count = lax.axis_size(axis)
        ends = count - 1
        head = lax.slice_in_dim(cells, 0, width, axis=dim)
        tail = lax.slice_in_dim(cells, cells.shape[dim] - width, cells.shape[dim], axis=dim)
        cells = jnp.concatenate(
            [
                lax.ppermute(tail, axis, [(i, (i + 1) % count) for i in range(ends)]),
                cells,
                lax.ppermute(head, axis, [((i + 1) % count, i) for i in range(ends)]),
            ],
            axis=dim,
        )
    return cells


def toeplitz_matrix(profile, length):
    half_width = (profile.shape[0] - 1) // 2
    position = jnp.arange(length, dtype=jnp.int32)
    offset = position[None, :] - position[:, None] + half_width
    tap_index = jnp.arange(profile.shape[0], dtype=jnp.int32)
    picked = (offset[:, :, None] == tap_index[None, None, :]).astype(jnp.float32)
    return jnp.sum(picked * profile[None, None, :], axis=2).astype(jnp.bfloat16)


def curvature(padded):
    anchor = padded[:-1, :-1, :-1]
    grad_z = padded[1:, :-1, :-1] - anchor
    grad_y = padded[:-1, 1:, :-1] - anchor
    grad_x = padded[:-1, :-1, 1:] - anchor
    magnitude = jnp.sqrt(grad_z * grad_z + grad_y * grad_y + grad_x * grad_x + SMOOTH_SQUARE)
    unit_z = grad_z / magnitude
    unit_y = grad_y / magnitude
    unit_x = grad_x / magnitude
    return (
        unit_z[1:, 1:, 1:]
        - unit_z[:-1, 1:, 1:]
        + (unit_y[1:, 1:, 1:] - unit_y[1:, :-1, 1:])
        + (unit_x[1:, 1:, 1:] - unit_x[1:, 1:, :-1])
    )


def view_correction(view_tile, observed, kernel_y, kernel_x):
    blurred = jnp.zeros(view_tile.shape, jnp.float32)
    for term_index in range(2):
        half_blur = jnp.einsum(
            "yk,zkx->zyx", kernel_y[term_index], view_tile, preferred_element_type=jnp.float32
        ).astype(jnp.bfloat16)
        blurred = blurred + jnp.einsum(
            "zyk,xk->zyx", half_blur, kernel_x[term_index], preferred_element_type=jnp.float32
        )
    quotient = (observed.astype(jnp.float32) / blurred).astype(jnp.bfloat16)
    log_sum = jnp.zeros(view_tile.shape, jnp.float32)
    for term_index in range(2):
        half_back = jnp.einsum(
            "ky,zkx->zyx", kernel_y[term_index], quotient, preferred_element_type=jnp.float32
        ).astype(jnp.bfloat16)
        log_sum = log_sum + jnp.einsum(
            "zyk,kx->zyx", half_back, kernel_x[term_index], preferred_element_type=jnp.float32
        )
    return log_sum.astype(jnp.bfloat16)


def shards(view_data, estimate, psf_taps, offsets):
    owners = lax.axis_size("tiles")
    view_count = lax.axis_size("views")
    observed = view_data[0, 0]
    planes, height, columns = estimate.shape
    view_shift = offsets[0]
    blocks = view_shift.shape[0]
    block_rows = height // blocks
    slot_count = owners * CAP
    kernel_y = jnp.stack(
        [toeplitz_matrix(psf_taps[0, term_index, 0], height) for term_index in range(2)]
    )
    kernel_x = jnp.stack(
        [toeplitz_matrix(psf_taps[0, term_index, 1], columns) for term_index in range(2)]
    )
    position = jnp.arange(blocks, dtype=jnp.int32)
    same_owner = view_shift[:, None] == view_shift[None, :]
    before = position[None, :] < position[:, None]
    slot_rank = jnp.sum((same_owner & before).astype(jnp.int32), axis=1)
    member = lax.axis_index("tiles")
    target = (member + view_shift) % owners
    source_tile = (member - view_shift) % owners
    slot_index = jnp.arange(slot_count, dtype=jnp.int32)
    to_owner = ((target * CAP + slot_rank)[:, None] == slot_index[None, :]).astype(jnp.bfloat16)
    from_tile = ((source_tile * CAP + slot_rank)[:, None] == slot_index[None, :]).astype(
        jnp.bfloat16
    )
    current = estimate
    for _ in range(ITERS):
        padded = with_halo(current, (("tiles", 1), ("gz", 0)), 1)
        padded = jnp.pad(padded, ((0, 0), (0, 0), (1, 1)))
        owned_blocks = current.astype(jnp.bfloat16).reshape(planes, blocks, block_rows, columns)
        outgoing = jnp.einsum(
            "sk,zsrx->kzrx", from_tile, owned_blocks, preferred_element_type=jnp.float32
        ).astype(jnp.bfloat16)
        incoming = lax.all_to_all(
            outgoing.reshape(owners, CAP, planes, block_rows, columns),
            "tiles",
            split_axis=0,
            concat_axis=0,
            tiled=True,
        )
        view_tile = jnp.einsum(
            "sk,kzrx->zsrx",
            to_owner,
            incoming.reshape(slot_count, planes, block_rows, columns),
            preferred_element_type=jnp.float32,
        ).astype(jnp.bfloat16)
        view_tile = view_tile.reshape(planes, height, columns)
        correction = view_correction(view_tile, observed, kernel_y, kernel_x)
        correction = correction.reshape(planes, blocks, block_rows, columns)
        returned = jnp.einsum(
            "sk,zsrx->kzrx", to_owner, correction, preferred_element_type=jnp.float32
        ).astype(jnp.bfloat16)
        gathered = lax.all_to_all(
            returned.reshape(owners, CAP, planes, block_rows, columns),
            "tiles",
            split_axis=0,
            concat_axis=0,
            tiled=True,
        )
        owned_rows = jnp.einsum(
            "sk,kzrx->zsrx",
            from_tile,
            gathered.reshape(slot_count, planes, block_rows, columns),
            preferred_element_type=jnp.float32,
        ).reshape(planes, height, columns)
        log_values = jnp.log(owned_rows)
        share_rows = height // view_count
        log_part = lax.psum_scatter(log_values, "views", scatter_dimension=1, tiled=True)
        first_row = lax.axis_index("views") * share_rows
        window = lax.dynamic_slice_in_dim(padded, first_row, share_rows + 2, 1)
        damping = 1.0 - TV_WEIGHT * curvature(window)
        rows_now = lax.dynamic_slice_in_dim(current, first_row, share_rows, 1)
        updated = rows_now * jnp.exp(log_part / view_count) / damping
        current = lax.all_gather(updated, "views", axis=1, tiled=True)
    return current


INFO_ROWS = 16
PLANE_UNIT = 65534.0
DATA_UNIT = 1024.0
TAP_UNIT = 8192.0
CHUNK = 32
VMEM = pl.BlockSpec(memory_space=pltpu.VMEM)
SMEM = pl.BlockSpec(memory_space=pltpu.SMEM)
LIMIT = pltpu.CompilerParams(vmem_limit_bytes=16 * 2**20)


def matrices_kernel(taps, info_ref, out_ref):
    views, columns = info_ref.shape
    length = out_ref.shape[-2] // 2
    half_width = (taps - 1) // 2
    row = lax.broadcasted_iota(jnp.int32, (length, columns), 0)
    column = lax.broadcasted_iota(jnp.int32, (length, columns), 1)
    band = jnp.abs(row - column) <= half_width
    for v in range(views):
        profile = jnp.broadcast_to(info_ref[v : v + 1, :], (8, columns))
        for kind, (flipped, axis) in enumerate([(0, 0), (1, 1), (1, 0), (0, 1)]):
            for r in range(2):
                lane = (4 * flipped + 2 * r + axis) * taps + half_width
                spread = jnp.broadcast_to(pltpu.roll(profile, columns - lane, 1)[0:1], (length, columns))
                rolled = pltpu.roll(spread, 0, 1, stride=1, stride_axis=0)
                rolled = jnp.where(band, rolled, 0.0).astype(out_ref.dtype)
                out_ref[v, kind, r * length : (r + 1) * length, :] = rolled


def blur_matrices(taps, length, info):
    views, columns = info.shape
    return pl.pallas_call(
        functools.partial(matrices_kernel, taps),
        out_shape=jax.ShapeDtypeStruct((views, 4, 2 * length, columns), jnp.bfloat16),
        in_specs=[VMEM],
        out_specs=VMEM,
        compiler_params=LIMIT,
        name="blur_matrices",
    )(info)


def correction_kernel(tiles, tile_ref, offsets_ref, current_ref, matrices_ref, *refs):
    views, blocks = offsets_ref.shape
    data, log_ref, work = refs[: views * tiles], refs[views * tiles], refs[views * tiles + 1 :]
    height, columns = data[0].shape
    rows = height // blocks
    me = tile_ref[0]
    shift = [[offsets_ref[w, s] for s in range(blocks)] for w in range(views)]
    planes = [work[3 * w] for w in range(views)]
    halves = [work[3 * w + 1] for w in range(views)]
    logs = [work[3 * w + 2] for w in range(views)]

    def first(w, kind):
        half = jnp.dot(matrices_ref[w, kind], planes[w][...], preferred_element_type=jnp.float32)
        half = half.astype(jnp.bfloat16)
        for k in range(tiles):
            for r in range(2):
                halves[w][k * height : (k + 1) * height, r * columns : (r + 1) * columns] = half[
                    r * height : (r + 1) * height, k * columns : (k + 1) * columns
                ]

    for w in range(views):
        for k in range(tiles):
            tile = lax.bitwise_xor(me, k)
            for s in range(blocks):
                owner = lax.rem(tile + shift[w][s], tiles)
                planes[w][s * rows : (s + 1) * rows, k * columns : (k + 1) * columns] = current_ref[
                    owner, s * rows : (s + 1) * rows, :
                ]
    for w in range(views):
        first(w, 0)
    for w in range(views):
        blurred = jnp.dot(halves[w][...], matrices_ref[w, 1], preferred_element_type=jnp.float32)
        for k in range(tiles):
            quotient = data[w * tiles + k][...].astype(jnp.float32) / blurred[k * height : (k + 1) * height]
            planes[w][:, k * columns : (k + 1) * columns] = quotient.astype(jnp.bfloat16)
    for w in range(views):
        first(w, 2)
    for w in range(views):
        back = jnp.dot(halves[w][...], matrices_ref[w, 3], preferred_element_type=jnp.float32)
        logs[w][...] = jnp.log(back.astype(jnp.bfloat16).astype(jnp.float32))
    for o in range(tiles):
        for s in range(blocks):
            total = None
            for w in range(views):
                tile = lax.rem(o - shift[w][s] + tiles, tiles)
                start = pl.multiple_of(lax.bitwise_xor(tile, me) * height + s * rows, rows)
                part = logs[w][pl.ds(start, rows), :]
                total = part if total is None else total + part
            log_ref[o * height + s * rows : o * height + (s + 1) * rows, :] = total


def correction_logs(tile, offsets, current, matrices, data):
    tiles, height, columns = current.shape
    scratch = [
        pltpu.VMEM((height, tiles * columns), jnp.bfloat16),
        pltpu.VMEM((tiles * height, 2 * columns), jnp.bfloat16),
        pltpu.VMEM((tiles * height, columns), jnp.float32),
    ]
    return pl.pallas_call(
        functools.partial(correction_kernel, tiles),
        out_shape=jax.ShapeDtypeStruct((tiles * height, columns), jnp.float32),
        in_specs=[SMEM, SMEM] + [VMEM] * (2 + len(data)),
        out_specs=VMEM,
        scratch_shapes=scratch * offsets.shape[0],
        cost_estimate=pl.CostEstimate(flops=300_000_000, bytes_accessed=1_500_000, transcendentals=0),
        compiler_params=LIMIT,
        name="correction",
    )(tile, offsets, current, matrices, *data)


def update_kernel(views, core_ref, current_ref, twin_ref, other_ref, log_ref, *new_refs):
    total, columns = current_ref.shape
    first = core_ref[0] == 0
    row = lax.broadcasted_iota(jnp.int32, (CHUNK, columns), 0)
    column = lax.broadcasted_iota(jnp.int32, (CHUNK, columns), 1)

    def scale(z, y, x):
        return lax.rsqrt(z * z + y * y + x * x + SMOOTH_SQUARE)

    def pick(low, high, start, size):
        return jnp.where(first, low[start : start + size, :], high[start : start + size, :])

    def next_row(x, following):
        return jnp.where(row == CHUNK - 1, following, pltpu.roll(x, CHUNK - 1, 0))

    def next_column(x):
        return jnp.where(column == columns - 1, 0.0, pltpu.roll(x, columns - 1, 1))

    def edge(x):
        return x * lax.rsqrt(x * x + SMOOTH_SQUARE)

    carry = edge(current_ref[0:1, :])
    for start in range(0, total, CHUNK):
        stop = start + CHUNK
        current = current_ref[start:stop, :]
        above = pick(twin_ref, other_ref, start, CHUNK)
        below = pick(other_ref, twin_ref, start, CHUNK)
        if stop < total:
            current_next, below_next = current_ref[stop : stop + 1, :], pick(other_ref, twin_ref, stop, 1)
        else:
            current_next = below_next = jnp.zeros((1, columns), jnp.float32)
        grad_z = above - current
        grad_y = next_row(current, current_next) - current
        grad_x = next_column(current) - current
        inverse = scale(grad_z, grad_y, grad_x)
        unit_y, unit_x = grad_y * inverse, grad_x * inverse
        before_y = jnp.where(row == 0, carry, pltpu.roll(unit_y, 1, 0))
        before_x = jnp.where(column == 0, edge(current), pltpu.roll(unit_x, 1, 1))
        carry = unit_y[CHUNK - 1 : CHUNK, :]
        lower_z = current - below
        lower = lower_z * scale(lower_z, next_row(below, below_next) - below, next_column(below) - below)
        divergence = grad_z * inverse - lower + (unit_y - before_y) + (unit_x - before_x)
        damping = 1.0 - TV_WEIGHT * divergence
        new = current * jnp.exp(log_ref[start:stop, :] * (1.0 / views)) / damping
        for ref in new_refs:
            ref[start:stop, :] = new.astype(ref.dtype)


def update(views, core, current, twin, other, logs, dtypes):
    return pl.pallas_call(
        functools.partial(update_kernel, views),
        out_shape=[jax.ShapeDtypeStruct(current.shape, dtype) for dtype in dtypes],
        in_specs=[SMEM] + [VMEM] * 4,
        out_specs=[VMEM] * len(dtypes),
        compiler_params=LIMIT,
        name="update",
    )(core, current, twin, other, logs)


def plane_shards(view_data, estimate, psf_taps, offsets):
    tiles, views = lax.axis_size("tiles"), lax.axis_size("views")
    square = ("tiles", "views", "gz")
    planes, height, columns = estimate.shape
    blocks = offsets.shape[1]
    taps = psf_taps.shape[-1]
    tile, view, core = lax.axis_index("tiles"), lax.axis_index("views"), lax.axis_index("gz")
    swap = [(0, 1), (1, 0)]

    def device(t, v, g):
        return (t * views + v) * 2 + g

    def ordered(pieces, shift):
        placed = []
        for i in range(tiles):
            chosen = pieces[i]
            for s in range(1, tiles):
                chosen = jnp.where(shift == s, pieces[i ^ s], chosen)
            placed.append(chosen)
        return placed

    def exchange(pick):
        pieces = []
        for k in range(tiles):
            pairs = [(device(t, v, g), device(t ^ k, g, v)) for t in range(tiles) for v in range(2) for g in range(2)]
            pieces.append(lax.ppermute(pick(k), square, pairs))
        return pieces

    def end_of(chain):
        return jnp.where(chain == 0, 0, tiles - 1)

    me = tile.reshape(1).astype(jnp.int32)
    flag = core.reshape(1).astype(jnp.int32)

    wide = estimate.reshape(tiles, 2, height, columns)
    wide = lax.dynamic_index_in_dim(wide, view, 1, keepdims=True)
    wide = jnp.round((wide - 1.0) * PLANE_UNIT).astype(jnp.int16)
    data = view_data.reshape(tiles, 2, height, columns).astype(jnp.float32)
    data = (data * DATA_UNIT).astype(jnp.int16)
    payload = jnp.concatenate([wide, data], axis=1).reshape(tiles, 3 * height, columns)
    payload, psf_taps, offsets = lax.optimization_barrier((payload, psf_taps, offsets))

    def for_tile(k):
        place = lax.bitwise_xor(lax.bitwise_xor(tile, k), end_of(core))
        return lax.dynamic_index_in_dim(payload, place, 0, keepdims=False)

    pieces = exchange(for_tile)

    profiles = [psf_taps.reshape(-1), psf_taps[..., ::-1].reshape(-1)]
    info = [lax.reduce_precision(p, 8, 7) * TAP_UNIT for p in profiles]
    info = jnp.concatenate([*info, offsets.reshape(-1).astype(jnp.float32)])
    info = jnp.pad(info, (0, columns - info.shape[0])).astype(jnp.int16)
    info = jnp.broadcast_to(info, (INFO_ROWS, columns))
    note = lax.ppermute(info, "views", swap)
    straight = view == core
    notes = jnp.stack([jnp.where(straight, info[0], note[0]), jnp.where(straight, note[0], info[0])])
    notes = notes.astype(jnp.float32)
    shifts = notes[:, 8 * taps : 8 * taps + blocks].astype(jnp.int32)
    matrices = blur_matrices(taps, height, notes * (1.0 / TAP_UNIT))

    planes = [piece[:height] for piece in pieces]
    pairs = [piece[height : 3 * height].reshape(2, height, columns) for piece in pieces]
    keep = [lax.dynamic_index_in_dim(pair, core, 0, keepdims=False) for pair in pairs]
    give = [lax.dynamic_index_in_dim(pair, 1 - core, 0, keepdims=False) for pair in pairs]
    got = lax.ppermute(jnp.concatenate([*planes, *give]), "gz", swap)
    length = tiles * height
    twin = got[:length].reshape(tiles, height, columns)
    take = got[length:].reshape(tiles, height, columns)
    data = [x.astype(jnp.float32) * (1.0 / DATA_UNIT) for x in [*keep, *[take[k] for k in range(tiles)]]]
    data = [x.astype(jnp.bfloat16) for x in data]

    path = [(t, 0) for t in range(tiles)] + [(t, 1) for t in reversed(range(tiles))]
    hops = []
    for here, there in zip(path[:-1], path[1:]):
        one, two = device(*here, 1), device(*there, 0)
        hops += [(one, two), (two, one)]

    def plane_of(coded):
        return coded.astype(jnp.float32) * (1.0 / PLANE_UNIT) + 1.0

    plane = jnp.concatenate(ordered(planes, tile))
    twin = plane_of(jnp.concatenate(ordered([twin[k] for k in range(tiles)], tile)))
    current = plane_of(plane)
    narrow = current.astype(jnp.bfloat16)
    at_end = (tile == 0) & (core == view)
    for iteration in range(ITERS):
        first, last = iteration == 0, iteration == ITERS - 1
        other = lax.ppermute(plane, square, hops)
        if not first:
            twin = lax.ppermute(current, "gz", swap)
        other = jnp.where(at_end, 0.0, plane_of(other) if first else other.astype(jnp.float32) + 1.0)
        logs = correction_logs(me, shifts, narrow.reshape(tiles, height, columns), matrices, data)
        current, *rest = update(
            views, flag, current, twin, other, logs, [jnp.float32] if last else [jnp.float32, jnp.bfloat16]
        )
        if not last:
            narrow = rest[0]
            plane = (current - 1.0).astype(jnp.float16)

    result = current.astype(jnp.float16).reshape(tiles, height, columns)
    pieces = []
    for k in range(tiles):
        piece = lax.dynamic_index_in_dim(result, lax.bitwise_xor(tile, k), 0)
        pieces.append(lax.ppermute(piece, "tiles", [(t, t ^ k) for t in range(tiles)]) if k else piece)
    far = [k for k in range(tiles) if k != 1]
    came = lax.ppermute(jnp.concatenate([pieces[k] for k in far]), "views", swap)
    near = lax.ppermute(pieces[1], "views", swap)
    crossed = [near[0] if k == 1 else came[far.index(k)] for k in range(tiles)]
    mine = [piece[0] for piece in pieces]
    here = lax.bitwise_xor(tile, end_of(core))
    send = [jnp.where(straight, c, m) for c, m in zip(crossed, mine)]
    send = jnp.stack(ordered(send, lax.bitwise_xor(tile, end_of(1 - core))))
    twin = lax.ppermute(send, "gz", swap)
    same = jnp.stack(ordered([jnp.where(straight, m, c) for c, m in zip(crossed, mine)], here))
    parity = lax.broadcasted_iota(jnp.int32, (tiles, 2, height, columns), 1)
    result = jnp.where(parity == core, same[:, None], twin[:, None])
    return result.astype(jnp.float32).reshape(2 * tiles, height, columns)


def one_plane_each(mesh, view_data, estimate, psf_taps, offsets):
    tiles, views, depth = mesh.shape["tiles"], mesh.shape["views"], mesh.shape["gz"]
    planes = estimate.shape[0] // (mesh.shape["groups"] * depth)
    height, columns = estimate.shape[1] // tiles, estimate.shape[2]
    return (
        depth == 2
        and views == 2
        and planes == 2 * tiles
        and tiles & (tiles - 1) == 0
        and height == columns
        and height % (16 * offsets.shape[1]) == 0
        and columns == 128
        and 8 * psf_taps.shape[-1] + offsets.shape[1] <= columns
    )


def solution(mesh):
    in_specs = (
        P(("groups", "views"), "tiles", "gz", None, None),
        P(("groups", "gz"), "tiles", None),
        P("views", None, None, None),
        P("views", None),
    )
    out_specs = P(("groups", "gz"), "tiles", None)

    def step(*arrays):
        if not one_plane_each(mesh, *arrays):
            return jax.shard_map(shards, mesh=mesh, in_specs=in_specs, out_specs=out_specs, check_vma=False)(*arrays)
        body = jax.shard_map(plane_shards, mesh=mesh, in_specs=in_specs, out_specs=out_specs, check_vma=False)
        return body(*arrays)

    return step
```
